32 devices in a mesh: dp: 8 (over z, x), tensor: 4 (over y, core).
Axes of the slice: x: 2, y: 2, z: 4, core: 2. Of those that a mesh axis runs over, the one named last changes fastest.
Arguments:
- tokens: bfloat16 [8, 1024, 768], P('dp'), may hold values from -6 to 6
- cotangent: bfloat16 [8, 1024, 768], P('dp'), may hold values from -6 to 6
- segments: int32 [8, 1024], P('dp'), may hold values from 0 to 7, never falling along the last dimension, each value on 1 to 512 neighbouring positions
- w_qkv: float32 [768, 3, 768], P('dp', None, 'tensor'), may hold values from -0.3969283 to 0.3969283
- w_proj: float32 [768, 768], P(('tensor', 'dp')), may hold values from -0.875 to 0.875
- w_fc: float32 [768, 3072], P('dp', 'tensor'), may hold values from -0.21875 to 0.21875
- w_fc2: float32 [3072, 768], P(('tensor', 'dp')), may hold values from -0.109375 to 0.109375
- w_vectors: float32 [6, 768], replicated, may hold values from -1.2 to 1.4, as said below
- w_qvbias: float32 [2, 768], P(None, 'tensor'), may hold values from -4 to 4
- w_fcbias: float32 [3072], P('tensor'), may hold values from -4 to 4
- m_qkv: float32 [768, 3, 768], P('dp', None, 'tensor'), may hold values from -112 to 112
- m_proj: float32 [768, 768], P(('tensor', 'dp')), may hold values from -56 to 56
- m_fc: float32 [768, 3072], P('dp', 'tensor'), may hold values from -32 to 32
- m_fc2: float32 [3072, 768], P(('tensor', 'dp')), may hold values from -64 to 64
- m_vectors: float32 [6, 768], replicated, may hold values from -112 to 112
- m_qvbias: float32 [2, 768], P(None, 'tensor'), may hold values from -112 to 112
- m_fcbias: float32 [3072], P('tensor'), may hold values from -32 to 32
- v_qkv: float32 [768, 3, 768], P('dp', None, 'tensor'), may hold values from 40.96 to 819.2
- v_proj: float32 [768, 768], P(('tensor', 'dp')), may hold values from 10.24 to 204.8
- v_fc: float32 [768, 3072], P('dp', 'tensor'), may hold values from 3.6864 to 73.728
- v_fc2: float32 [3072, 768], P(('tensor', 'dp')), may hold values from 14.7456 to 294.912
- v_vectors: float32 [6, 768], replicated, may hold values from 40.96 to 819.2
- v_qvbias: float32 [2, 768], P(None, 'tensor'), may hold values from 40.96 to 819.2
- v_fcbias: float32 [3072], P('tensor'), may hold values from 3.6864 to 73.728
Outputs:
- block_out: bfloat16 [8, 1024, 768], P('dp')
- grad_tokens: bfloat16 [8, 1024, 768], P('dp')
- grad_qkv: float32 [768, 3, 768], P('dp', None, 'tensor')
- grad_proj: float32 [768, 768], P(('tensor', 'dp'))
- grad_fc: float32 [768, 3072], P('dp', 'tensor')
- grad_fc2: float32 [3072, 768], P(('tensor', 'dp'))
- grad_vectors: float32 [6, 768], replicated
- grad_qvbias: float32 [2, 768], P(None, 'tensor')
- grad_fcbias: float32 [3072], P('tensor')
- new_qkv: float32 [768, 3, 768], P('dp', None, 'tensor')
- new_proj: float32 [768, 768], P(('tensor', 'dp'))
- new_fc: float32 [768, 3072], P('dp', 'tensor')
- new_fc2: float32 [3072, 768], P(('tensor', 'dp'))
- new_vectors: float32 [6, 768], replicated
- new_qvbias: float32 [2, 768], P(None, 'tensor')
- new_fcbias: float32 [3072], P('tensor')
- newm_qkv: float32 [768, 3, 768], P('dp', None, 'tensor')
- newm_proj: float32 [768, 768], P(('tensor', 'dp'))
- newm_fc: float32 [768, 3072], P('dp', 'tensor')
- newm_fc2: float32 [3072, 768], P(('tensor', 'dp'))
- newm_vectors: float32 [6, 768], replicated
- newm_qvbias: float32 [2, 768], P(None, 'tensor')
- newm_fcbias: float32 [3072], P('tensor')
- newv_qkv: float32 [768, 3, 768], P('dp', None, 'tensor')
- newv_proj: float32 [768, 768], P(('tensor', 'dp'))
- newv_fc: float32 [768, 3072], P('dp', 'tensor')
- newv_fc2: float32 [3072, 768], P(('tensor', 'dp'))
- newv_vectors: float32 [6, 768], replicated
- newv_qvbias: float32 [2, 768], P(None, 'tensor')
- newv_fcbias: float32 [3072], P('tensor')
The draws below stay inside these ranges and needn't reach their ends.
Inputs may be any that keep to these rules, and one draw needn't show every extreme that they name: `w_vectors`: gains lie near 1 and shifts and biases near 0. `segments`: within each sequence segment numbers never fall; each segment holds at most 512 positions.
All inputs are finite; a program needn't handle non-finite values.
Results may differ from the reference program's by a relative error of at most 0.02.
Values may be sent and summed in bfloat16 or wider, within the bound.
A program may use at most 128 MiB of HBM per device.

```python
import math
from functools import partial
import jax
import jax.numpy as jnp
import numpy as np
from jax import lax

D = 768
HEADS = 12
HD = 64
FF = 3072
SEQ_LEN = 1024
ADAM_STEP = 3
SEQS = 8
N_TENSOR = 4


def draw_w_qkv(key, part):
    base = jnp.clip(jax.random.normal(key, (D, 3, D), jnp.float32), -4.0, 4.0) / math.sqrt(D)
    return base


def draw_w_vectors(key, part):
    noise = jnp.clip(jax.random.normal(key, (6, D), jnp.float32), -4.0, 4.0)
    row_kind = jnp.arange(6)
    is_gain = (row_kind == 0) | (row_kind == 2)
    return jnp.where(is_gain[:, None], 1.0 + 0.1 * noise, 0.3 * noise)


def shard_levels(stream_key, extent, cuts, smallest, high):
    def one(dim, blocks):
        draws = jax.random.uniform(jax.random.fold_in(jax.random.fold_in(stream_key, 6), dim), (blocks,), jnp.float32, smallest / len(cuts), high / len(cuts))
        return jnp.repeat(jnp.exp(draws), extent[dim] // blocks).reshape((-1,) + (1,) * (len(extent) - dim - 1))

    factor_of = one(*cuts[0])
    for cut in cuts[1:]:
        factor_of = factor_of * one(*cut)
    return factor_of


def profile(number_of, total, most, slope):
    portions = [(1 << 20) // math.isqrt(rank ** slope) + 1 for rank in range(2, number_of + 1)]
    rest, given = total - most - (number_of - 1), [1] * (number_of - 1)
    while rest > 0:
        candidates = [i for i in range(number_of - 1) if given[i] < most]
        mass, remaining = sum([portions[i] for i in candidates]), rest
        for i in candidates:
            more = min(most - given[i], max(1, remaining * portions[i] // mass), rest)
            given[i] = given[i] + more
            rest = rest - more
    return np.array([most] + given)


def ragged_sizes(stream_key, number_of, total, limit, lean):
    if number_of == 2:
        one = jax.random.randint(stream_key, (), max(1, total - limit), min(limit, total - 1) + 1)
        return jnp.stack([one, total - one])
    lengths = jnp.asarray(profile(number_of, total, limit, lean), jnp.int32)
    pairs = (number_of - 1) // 2
    donor, taker = lengths[1:1 + 2 * pairs:2], lengths[2:2 + 2 * pairs:2]
    room = jnp.minimum(donor - 1, limit - taker)
    passed = jax.random.randint(jax.random.fold_in(stream_key, 1), (pairs,), 0, 1 << 20) % (room + 1)
    lengths = lengths.at[1:1 + 2 * pairs:2].set(donor - passed).at[2:2 + 2 * pairs:2].set(taker + passed)
    return lengths[jax.random.permutation(jax.random.fold_in(stream_key, 2), number_of)]


def gaussian(rng, dims, scale, most, cuts=(), kind=jnp.bfloat16):
    entries = scale * jax.random.normal(rng, dims, jnp.float32)
    if cuts:
        entries = entries * shard_levels(rng, dims, cuts, -0.22, 0.18)
    return jnp.clip(entries, -most, most).astype(kind)


def setup_inputs(seed: int = 0) -> dict:
    streams_of = jax.random.split(jax.random.key(seed), 25)
    tokens = gaussian(streams_of[0], (SEQS, SEQ_LEN, D), 1.0, 6.0, ((0, 8),))
    cotangent = gaussian(streams_of[1], (SEQS, SEQ_LEN, D), 1.0, 6.0, ((0, 8),))
    segments = jax.vmap(lambda own: jnp.searchsorted(jnp.cumsum(ragged_sizes(own, max(4, SEQ_LEN // 128), SEQ_LEN, SEQ_LEN // 2, 0)), jnp.arange(SEQ_LEN), side="right"))(jax.random.split(streams_of[2], SEQS)).reshape((SEQS, SEQ_LEN)).astype(jnp.int32)
    w_qkv = draw_w_qkv(jax.random.fold_in(streams_of[24], 71), 0)
    w_proj = gaussian(streams_of[4], (D, D), (D // 16) ** -0.5, 0.875, ((0, 32),), jnp.float32)
    w_fc = gaussian(streams_of[5], (D, FF), D ** -0.5, 0.21875, ((0, 8), (1, 4)), jnp.float32)
    w_fc2 = gaussian(streams_of[6], (FF, D), FF ** -0.5, 0.109375, ((0, 32),), jnp.float32)
    w_vectors = draw_w_vectors(jax.random.fold_in(streams_of[24], 71), 0)
    w_qvbias = gaussian(streams_of[8], (2, D), 0.3, 4.0, ((1, 4),), jnp.float32)
    w_fcbias = gaussian(streams_of[9], (FF,), 0.3, 4.0, ((0, 4),), jnp.float32)
    m_qkv = gaussian(streams_of[10], (D, 3, D), (0.2 * (SEQS * SEQ_LEN) ** 0.5), 112.0, ((0, 8), (2, 4)), jnp.float32)
    m_proj = gaussian(streams_of[11], (D, D), (0.1 * (SEQS * SEQ_LEN) ** 0.5), 56.0, ((0, 32),), jnp.float32)
    m_fc = gaussian(streams_of[12], (D, FF), (0.06 * (SEQS * SEQ_LEN) ** 0.5), 32.0, ((0, 8), (1, 4)), jnp.float32)
    m_fc2 = gaussian(streams_of[13], (FF, D), (0.12 * (SEQS * SEQ_LEN) ** 0.5), 64.0, ((0, 32),), jnp.float32)
    m_vectors = gaussian(streams_of[14], (6, D), (0.2 * (SEQS * SEQ_LEN) ** 0.5), 112.0, (), jnp.float32)
    m_qvbias = gaussian(streams_of[15], (2, D), (0.2 * (SEQS * SEQ_LEN) ** 0.5), 112.0, ((1, 4),), jnp.float32)
    m_fcbias = gaussian(streams_of[16], (FF,), (0.06 * (SEQS * SEQ_LEN) ** 0.5), 32.0, ((0, 4),), jnp.float32)
    v_qkv = jnp.clip(jnp.exp(math.log(819.2) - 2.9957323 * jax.random.uniform(streams_of[17], (D, 3, D), jnp.float32) ** shard_levels(streams_of[17], (D, 3, D), ((0, 8), (2, 4)), -0.2, 0.2)), 40.96, 819.2)
    v_proj = jnp.clip(jnp.exp(math.log(204.8) - 2.9957323 * jax.random.uniform(streams_of[18], (D, D), jnp.float32) ** shard_levels(streams_of[18], (D, D), ((0, 32),), -0.2, 0.2)), 10.24, 204.8)
    v_fc = jnp.clip(jnp.exp(math.log(73.728) - 2.9957322 * jax.random.uniform(streams_of[19], (D, FF), jnp.float32) ** shard_levels(streams_of[19], (D, FF), ((0, 8), (1, 4)), -0.2, 0.2)), 3.6864, 73.728)
    v_fc2 = jnp.clip(jnp.exp(math.log(294.912) - 2.9957322 * jax.random.uniform(streams_of[20], (FF, D), jnp.float32) ** shard_levels(streams_of[20], (FF, D), ((0, 32),), -0.2, 0.2)), 14.7456, 294.912)
    v_vectors = jnp.clip(jnp.exp(jax.random.uniform(streams_of[21], (6, D), jnp.float32, math.log(40.96), math.log(819.2))), 40.96, 819.2)
    v_qvbias = jnp.clip(jnp.exp(math.log(819.2) - 2.9957323 * jax.random.uniform(streams_of[22], (2, D), jnp.float32) ** shard_levels(streams_of[22], (2, D), ((1, 4),), -0.2, 0.2)), 40.96, 819.2)
    v_fcbias = jnp.clip(jnp.exp(math.log(73.728) - 2.9957322 * jax.random.uniform(streams_of[23], (FF,), jnp.float32) ** shard_levels(streams_of[23], (FF,), ((0, 4),), -0.2, 0.2)), 3.6864, 73.728)
    return {"tokens": tokens, "cotangent": cotangent, "segments": segments, "w_qkv": w_qkv, "w_proj": w_proj, "w_fc": w_fc, "w_fc2": w_fc2, "w_vectors": w_vectors, "w_qvbias": w_qvbias, "w_fcbias": w_fcbias, "m_qkv": m_qkv, "m_proj": m_proj, "m_fc": m_fc, "m_fc2": m_fc2, "m_vectors": m_vectors, "m_qvbias": m_qvbias, "m_fcbias": m_fcbias, "v_qkv": v_qkv, "v_proj": v_proj, "v_fc": v_fc, "v_fc2": v_fc2, "v_vectors": v_vectors, "v_qvbias": v_qvbias, "v_fcbias": v_fcbias}


NORM_EPS = 1e-05
ADAM_EPS = 1e-08
LEARN_RATE = 0.1
BETA_ONE = 0.9
BETA_TWO = 0.95
DECAY_RATE = 0.1
MASK_FILL = -1e+30
GELU_COEF = 0.7978845608028654
CUBIC_COEF = 0.044715

def layer_norm(values, gain, shift):
    center = values - lax.optimization_barrier(jnp.mean(values, axis=1, keepdims=True))
    inverse = lax.rsqrt(lax.optimization_barrier(jnp.mean(center * center, axis=1, keepdims=True)) + NORM_EPS)
    normed = center * inverse
    return (normed * gain + shift, normed, inverse)

def norm_backward(upstream, normed, inverse, gain):
    scaled = upstream * gain
    inner = scaled - lax.optimization_barrier(jnp.mean(scaled, axis=1, keepdims=True)) - normed * lax.optimization_barrier(jnp.mean(scaled * normed, axis=1, keepdims=True))
    return (inverse * inner, lax.optimization_barrier(jnp.sum(upstream * normed, axis=0)), lax.optimization_barrier(jnp.sum(upstream, axis=0)))

def gelu_value(values):
    inner = GELU_COEF * (values + CUBIC_COEF * values * values * values)
    return 0.5 * values * (1.0 + jnp.tanh(inner))

def gelu_slope(values):
    tangent = jnp.tanh(GELU_COEF * (values + CUBIC_COEF * values * values * values))
    return 0.5 * (1.0 + tangent) + 0.5 * values * (1.0 - tangent * tangent) * GELU_COEF * (1.0 + 3.0 * CUBIC_COEF * values * values)

def head_forward(allowed, parts):
    query_head, key_head, value_head = parts
    scores = jnp.where(allowed, jnp.dot(query_head, key_head.T, preferred_element_type=jnp.float32), MASK_FILL)
    largest = lax.optimization_barrier(jnp.max(scores, axis=1, keepdims=True))
    total = lax.optimization_barrier(jnp.sum(jnp.exp(scores - largest), axis=1, keepdims=True))
    log_total = largest + jnp.log(total)
    probs = jnp.exp(scores - log_total)
    context = jnp.dot(probs.astype(jnp.bfloat16), value_head, preferred_element_type=jnp.float32).astype(jnp.bfloat16)
    return (context, log_total[:, 0])

def head_backward(allowed, scale, parts):
    query_head, key_head, value_head, context_head, log_head, grad_head = parts
    scores = jnp.where(allowed, jnp.dot(query_head, key_head.T, preferred_element_type=jnp.float32), MASK_FILL)
    probs = jnp.exp(scores - log_head[:, None])
    grad_probs = jnp.dot(grad_head, value_head.T, preferred_element_type=jnp.float32)
    delta = lax.optimization_barrier(jnp.sum(grad_head.astype(jnp.float32) * context_head.astype(jnp.float32), axis=1, keepdims=True))
    grad_scores = (probs * (grad_probs - delta)).astype(jnp.bfloat16)
    grad_query = jnp.dot(grad_scores, key_head, preferred_element_type=jnp.float32) * scale
    grad_keys = jnp.dot(grad_scores.T, query_head, preferred_element_type=jnp.float32)
    grad_values = jnp.dot(probs.astype(jnp.bfloat16).T, grad_head, preferred_element_type=jnp.float32)
    return (grad_query, grad_keys, grad_values)

def adam_update(param, grad, first, second, decay):
    first_new = BETA_ONE * first + (1.0 - BETA_ONE) * grad
    second_new = BETA_TWO * second + (1.0 - BETA_TWO) * grad * grad
    first_hat = first_new / (1.0 - BETA_ONE ** ADAM_STEP)
    second_hat = second_new / (1.0 - BETA_TWO ** ADAM_STEP)
    param_new = param - LEARN_RATE * (first_hat / (jnp.sqrt(second_hat) + ADAM_EPS) + decay * param)
    return (param_new, first_new, second_new)

def rounded_sum(terms):
    total = jnp.zeros(terms[0].shape, jnp.float32)
    for term in terms:
        total = total + lax.optimization_barrier(term.astype(jnp.bfloat16)).astype(jnp.float32)
    return total

def reference(tokens, cotangent, segments, w_qkv, w_proj, w_fc, w_fc2, w_vectors, w_qvbias, w_fcbias, m_qkv, m_proj, m_fc, m_fc2, m_vectors, m_qvbias, m_fcbias, v_qkv, v_proj, v_fc, v_fc2, v_vectors, v_qvbias, v_fcbias):
    bfloat = jnp.bfloat16
    group = D // N_TENSOR
    hidden_group = FF // N_TENSOR
    scale = 1.0 / math.sqrt(HD)
    qkv_cube = w_qkv.astype(bfloat)
    qkv_flat = qkv_cube.reshape(D, 3 * D)
    proj_bf = w_proj.astype(bfloat)
    fc_bf = w_fc.astype(bfloat)
    fc2_bf = w_fc2.astype(bfloat)
    position = jnp.arange(SEQ_LEN)

    def split_heads(array):
        return array.reshape(SEQ_LEN, HEADS, HD).transpose(1, 0, 2)

    def join_heads(array):
        return array.transpose(1, 0, 2).reshape(SEQ_LEN, D)

    def one_sequence(totals, inputs):
        token_rows, upstream, seg_row = inputs
        allowed = (seg_row[:, None] == seg_row[None, :]) & (position[None, :] <= position[:, None])
        inputs_f = token_rows.astype(jnp.float32)
        first_in, normed_one, inverse_one = layer_norm(inputs_f, w_vectors[0], w_vectors[1])
        first_bf = first_in.astype(bfloat)
        projected = jnp.dot(first_bf, qkv_flat, preferred_element_type=jnp.float32).reshape(SEQ_LEN, 3, D)
        query = ((projected[:, 0] + w_qvbias[0]) * scale).astype(bfloat)
        keys = projected[:, 1].astype(bfloat)
        values = (projected[:, 2] + w_qvbias[1]).astype(bfloat)
        context, log_total = lax.map(partial(head_forward, allowed), (split_heads(query), split_heads(keys), split_heads(values)))
        context_flat = join_heads(context)
        attn_terms = [jnp.dot(context_flat[:, g * group:(g + 1) * group], proj_bf[g * group:(g + 1) * group], preferred_element_type=jnp.float32) for g in range(N_TENSOR)]
        middle = inputs_f + rounded_sum(attn_terms) + w_vectors[4]
        second_in, normed_two, inverse_two = layer_norm(middle, w_vectors[2], w_vectors[3])
        second_bf = second_in.astype(bfloat)
        hidden_pre = jnp.dot(second_bf, fc_bf, preferred_element_type=jnp.float32) + w_fcbias
        hidden_bf = gelu_value(hidden_pre).astype(bfloat)
        mlp_terms = [jnp.dot(hidden_bf[:, g * hidden_group:(g + 1) * hidden_group], fc2_bf[g * hidden_group:(g + 1) * hidden_group], preferred_element_type=jnp.float32) for g in range(N_TENSOR)]
        output = (middle + rounded_sum(mlp_terms) + w_vectors[5]).astype(bfloat)
        grad_out = upstream.astype(jnp.float32)
        grad_fc2 = jnp.dot(hidden_bf.T, upstream, preferred_element_type=jnp.float32)
        grad_hidden = jnp.dot(upstream, fc2_bf.T, preferred_element_type=jnp.float32) * gelu_slope(hidden_pre)
        grad_hidden_bf = grad_hidden.astype(bfloat)
        grad_fc = jnp.dot(second_bf.T, grad_hidden_bf, preferred_element_type=jnp.float32)
        grad_fcbias = lax.optimization_barrier(jnp.sum(grad_hidden, axis=0))
        norm_two_terms = [jnp.dot(grad_hidden_bf[:, g * hidden_group:(g + 1) * hidden_group], fc_bf[:, g * hidden_group:(g + 1) * hidden_group].T, preferred_element_type=jnp.float32) for g in range(N_TENSOR)]
        back_two, gain_two, shift_two = norm_backward(rounded_sum(norm_two_terms), normed_two, inverse_two, w_vectors[2])
        grad_middle = grad_out + back_two
        grad_middle_bf = grad_middle.astype(bfloat)
        grad_proj = jnp.dot(context_flat.T, grad_middle_bf, preferred_element_type=jnp.float32)
        grad_context = jnp.dot(grad_middle_bf, proj_bf.T, preferred_element_type=jnp.float32).astype(bfloat)
        grad_query, grad_keys, grad_values = lax.map(partial(head_backward, allowed, scale), (split_heads(query), split_heads(keys), split_heads(values), context, log_total, split_heads(grad_context)))
        grad_query = join_heads(grad_query)
        grad_keys = join_heads(grad_keys)
        grad_values = join_heads(grad_values)
        grad_qvbias = jnp.stack([lax.optimization_barrier(jnp.sum(grad_query, axis=0)), lax.optimization_barrier(jnp.sum(grad_values, axis=0))])
        grad_stack = jnp.stack([grad_query, grad_keys, grad_values], axis=1).astype(bfloat)
        grad_qkv = jnp.dot(first_bf.T, grad_stack.reshape(SEQ_LEN, 3 * D), preferred_element_type=jnp.float32).reshape(D, 3, D)
        norm_one_terms = [jnp.dot(grad_stack[:, :, g * group:(g + 1) * group].reshape(SEQ_LEN, 3 * group), qkv_cube[:, :, g * group:(g + 1) * group].reshape(D, 3 * group).T, preferred_element_type=jnp.float32) for g in range(N_TENSOR)]
        back_one, gain_one, shift_one = norm_backward(rounded_sum(norm_one_terms), normed_one, inverse_one, w_vectors[0])
        grad_input = (grad_middle + back_one).astype(bfloat)
        grad_vectors = jnp.stack([gain_one, shift_one, gain_two, shift_two, lax.optimization_barrier(jnp.sum(grad_middle, axis=0)), lax.optimization_barrier(jnp.sum(grad_out, axis=0))])
        terms = (grad_qkv, grad_proj, grad_fc, grad_fc2, grad_vectors, grad_qvbias, grad_fcbias)
        new_totals = tuple((total + term for total, term in zip(totals, terms)))
        return (new_totals, (output, grad_input))
    start = (jnp.zeros((D, 3, D), jnp.float32), jnp.zeros((D, D), jnp.float32), jnp.zeros((D, FF), jnp.float32), jnp.zeros((FF, D), jnp.float32), jnp.zeros((6, D), jnp.float32), jnp.zeros((2, D), jnp.float32), jnp.zeros((FF,), jnp.float32))
    totals, (outputs, grad_inputs) = lax.scan(one_sequence, start, (tokens, cotangent, segments))
    params = (w_qkv, w_proj, w_fc, w_fc2, w_vectors, w_qvbias, w_fcbias)
    firsts = (m_qkv, m_proj, m_fc, m_fc2, m_vectors, m_qvbias, m_fcbias)
    seconds = (v_qkv, v_proj, v_fc, v_fc2, v_vectors, v_qvbias, v_fcbias)
    decays = (DECAY_RATE, DECAY_RATE, DECAY_RATE, DECAY_RATE, 0.0, 0.0, 0.0)
    updates = [adam_update(p, g, m, v, c) for p, g, m, v, c in zip(params, totals, firsts, seconds, decays)]
    return (outputs, grad_inputs, totals[0], totals[1], totals[2], totals[3], totals[4], totals[5], totals[6], updates[0][0], updates[1][0], updates[2][0], updates[3][0], updates[4][0], updates[5][0], updates[6][0], updates[0][1], updates[1][1], updates[2][1], updates[3][1], updates[4][1], updates[5][1], updates[6][1], updates[0][2], updates[1][2], updates[2][2], updates[3][2], updates[4][2], updates[5][2], updates[6][2])
```

```python
import functools
import math

import jax
import jax.numpy as jnp
from jax import lax
from jax.experimental import pallas as pl
from jax.experimental.pallas import tpu as pltpu
from jax.sharding import PartitionSpec as P

HD = 64
ADAM_STEP = 3


NORM_EPS = 1e-05
ADAM_EPS = 1e-08
LEARN_RATE = 0.1
BETA_ONE = 0.9
BETA_TWO = 0.95
DECAY_RATE = 0.1
MASK_FILL = -1e30
GELU_COEF = 0.7978845608028654
CUBIC_COEF = 0.044715


def layer_norm(values, gain, shift):
    center = values - jnp.mean(values, axis=1, keepdims=True)
    inverse = lax.rsqrt(jnp.mean(center * center, axis=1, keepdims=True) + NORM_EPS)
    normed = center * inverse
    return (normed * gain + shift, normed, inverse)


def norm_backward(upstream, normed, inverse, gain):
    scaled = upstream * gain
    inner = (
        scaled
        - jnp.mean(scaled, axis=1, keepdims=True)
        - normed * jnp.mean(scaled * normed, axis=1, keepdims=True)
    )
    return (inverse * inner, jnp.sum(upstream * normed, axis=0), jnp.sum(upstream, axis=0))


def gelu_value(values):
    inner = GELU_COEF * (values + CUBIC_COEF * values * values * values)
    return 0.5 * values * (1.0 + jnp.tanh(inner))


def gelu_slope(values):
    tangent = jnp.tanh(GELU_COEF * (values + CUBIC_COEF * values * values * values))
    return 0.5 * (1.0 + tangent) + 0.5 * values * (1.0 - tangent * tangent) * GELU_COEF * (
        1.0 + 3.0 * CUBIC_COEF * values * values
    )


MESH_ID = pl.DeviceIdType.MESH


def ring_position(index, count):
    odd = lax.rem(index, 2)
    return (1 - odd) * lax.div(index, 2) + odd * (count - 1 - lax.div(index, 2))


def ring_index(position, count):
    place = lax.rem(position + 2 * count, count)
    back = lax.div(place, count // 2)
    return (1 - back) * 2 * place + back * (2 * (count - 1 - place) + 1)


def greet(peers):
    barrier = pltpu.get_barrier_semaphore()
    for peer in peers:
        pl.semaphore_signal(barrier, inc=1, device_id=peer, device_id_type=MESH_ID)
    pl.semaphore_wait(barrier, len(peers))


def ring_peers(count):
    place = ring_position(lax.axis_index("dp"), count)
    return [{"dp": ring_index(place + 1, count)}, {"dp": ring_index(place - 1, count)}]


def flip_bit(index, bit):
    weight = 1 << bit
    return index + weight * (1 - 2 * lax.rem(lax.div(index, weight), 2))


def cube_peers(count):
    index = lax.axis_index("tensor")
    return [{"tensor": flip_bit(index, bit)} for bit in range(count.bit_length() - 1)]


def pieces_of(columns):
    for pieces in (3, 2):
        if columns % (pieces * 128) == 0 and columns // pieces <= 384:
            return pieces
    return 1


class Ring:
    def __init__(self, count, columns):
        self.count = count
        self.index = lax.axis_index("dp")
        self.place = ring_position(self.index, count)
        self.peers = ring_peers(count)
        self.pieces = pieces_of(columns)
        self.width = columns // self.pieces

    def span(self, piece):
        return pl.ds(piece * self.width, self.width)

    def hops(self, way, array):
        return self.count // 2 if way == array else self.count - 1 - self.count // 2

    def at(self, distance, way):
        return ring_index(self.place + (1 - 2 * way) * distance + self.count, self.count)

    def each(self, step):
        return [
            (way, array, piece)
            for piece in range(self.pieces)
            for array in range(2)
            for way in range(2)
            if step < self.hops(way, array)
        ]

    def all(self):
        return [(step, *key) for step in range(self.count // 2) for key in self.each(step)]

    def start(self):
        for key in self.each(0):
            self.copy(0, *key).start()

    def drain(self):
        for key in self.all():
            self.copy(*key).wait_send()


class RingGather(Ring):
    def __init__(self, count, sources, results, sends, receives):
        super().__init__(count, sources[0].shape[-1])
        self.sources, self.results = sources, results
        self.sends, self.receives = sends, receives

    def copy(self, step, way, array, piece):
        target = self.results[array].at[self.at(-step, way), :, self.span(piece)]
        return pltpu.make_async_remote_copy(
            src_ref=self.sources[array].at[:, self.span(piece)] if step == 0 else target,
            dst_ref=target,
            send_sem=self.sends.at[way, array, step, piece],
            recv_sem=self.receives.at[way, array, step, piece],
            device_id=self.peers[way],
            device_id_type=MESH_ID,
        )

    def own(self):
        for array in range(2):
            self.results[array][self.index] = self.sources[array][...]

    def steps(self):
        for step in range(1, self.count // 2):
            for key in self.each(step):
                self.copy(step - 1, *key).wait_recv()
                self.copy(step, *key).start()

    def finish(self):
        for way in range(2):
            for array in range(2):
                for piece in range(self.pieces):
                    self.copy(self.hops(way, array) - 1, way, array, piece).wait_recv()
        self.drain()


class RingReduce(Ring):
    def __init__(self, count, sources, slots, results, sends, receives):
        super().__init__(count, sources[0].shape[-1])
        self.sources, self.slots, self.results = sources, slots, results
        self.sends, self.receives = sends, receives

    def block(self, step, way, array):
        return self.at(self.hops(way, array) - step, way)

    def copy(self, step, way, array, piece):
        span = self.span(piece)
        if step == 0:
            source = self.sources[array].at[self.block(0, way, array), :, span]
        else:
            source = self.slots[array].at[way, step - 1, :, span]
        return pltpu.make_async_remote_copy(
            src_ref=source,
            dst_ref=self.slots[array].at[way, step, :, span],
            send_sem=self.sends.at[way, array, step, piece],
            recv_sem=self.receives.at[way, array, step, piece],
            device_id=self.peers[way],
            device_id_type=MESH_ID,
        )

    def steps(self):
        for step in range(1, self.count // 2):
            for way, array, piece in self.each(step):
                self.copy(step - 1, way, array, piece).wait_recv()
                span = self.span(piece)
                own = self.sources[array][self.block(step, way, array), :, span]
                arrived = self.slots[array][way, step - 1, :, span]
                self.slots[array][way, step - 1, :, span] = (
                    arrived.astype(jnp.float32) + own.astype(jnp.float32)
                ).astype(jnp.bfloat16)
                self.copy(step, way, array, piece).start()

    def finish(self):
        for array in range(2):
            for piece in range(self.pieces):
                span = self.span(piece)
                total = self.sources[array][self.index, :, span].astype(jnp.float32)
                for way in range(2):
                    last = self.hops(way, array) - 1
                    self.copy(last, way, array, piece).wait_recv()
                    total = total + self.slots[array][way, last, :, span].astype(jnp.float32)
                self.results[array][:, span] = total
        self.drain()


class CubeSum:
    def __init__(self, count, source, result, arrivals, sums, sends, receives):
        self.bits = count.bit_length() - 1
        self.source, self.result, self.arrivals, self.sums = source, result, arrivals, sums
        self.sends, self.receives = sends, receives
        self.peers = cube_peers(count)
        self.side = lax.rem(lax.axis_index("tensor"), 2)
        self.chunks, self.rows = arrivals.shape[1], arrivals.shape[2]
        self.half = self.chunks * self.rows

    def mine(self, chunk, side):
        return pl.ds(pl.multiple_of(side * self.half + chunk * self.rows, self.rows), self.rows)

    def copy(self, stage, chunk):
        if stage == 0:
            source = self.source.at[self.mine(chunk, 1 - self.side)]
            target = self.arrivals.at[0, chunk]
        elif stage < self.bits:
            source, target = self.sums.at[stage - 1, chunk], self.arrivals.at[stage, chunk]
        else:
            source = self.result.at[self.mine(chunk, self.side)]
            target = source
        return pltpu.make_async_remote_copy(
            src_ref=source,
            dst_ref=target,
            send_sem=self.sends.at[stage, chunk],
            recv_sem=self.receives.at[stage, chunk],
            device_id=self.peers[stage % self.bits],
            device_id_type=MESH_ID,
        )

    def start(self):
        for chunk in range(self.chunks):
            self.copy(0, chunk).start()

    def add(self, stage):
        for chunk in range(self.chunks):
            self.copy(stage, chunk).wait_recv()
            if stage == 0:
                own = self.source[self.mine(chunk, self.side)]
            else:
                own = self.sums[stage - 1, chunk]
            total = own.astype(jnp.float32) + self.arrivals[stage, chunk].astype(jnp.float32)
            if stage == self.bits - 1:
                self.result[self.mine(chunk, self.side)] = total.astype(jnp.bfloat16)
            else:
                self.sums[stage, chunk] = total.astype(jnp.bfloat16)
            self.copy(stage + 1, chunk).start()

    def last(self):
        for stage in range(1, self.bits):
            self.add(stage)

    def finish(self):
        for chunk in range(self.chunks):
            self.copy(self.bits, chunk).wait_recv()
        for stage in range(self.bits + 1):
            for chunk in range(self.chunks):
                self.copy(stage, chunk).wait_send()


CHUNKS = 4


def cube_scratch(count, rows, columns):
    bits = count.bit_length() - 1
    block = (CHUNKS, rows // 2 // CHUNKS, columns)
    return [
        pltpu.VMEM((bits,) + block, jnp.bfloat16),
        pltpu.VMEM((bits,) + block, jnp.bfloat16),
        pltpu.SemaphoreType.DMA((bits + 1, CHUNKS)),
        pltpu.SemaphoreType.DMA((bits + 1, CHUNKS)),
    ]


def ring_scratch(count, pieces):
    return [
        pltpu.SemaphoreType.DMA((2, 2, count // 2, pieces)),
        pltpu.SemaphoreType.DMA((2, 2, count // 2, pieces)),
    ]


def call_kernel(body, name, number, inputs, outputs, scratch):
    vmem = pl.BlockSpec(memory_space=pltpu.VMEM)
    return pl.pallas_call(
        body,
        name=name,
        out_shape=outputs,
        in_specs=[vmem] * len(inputs),
        out_specs=[vmem] * len(outputs),
        scratch_shapes=scratch,
        compiler_params=pltpu.CompilerParams(collective_id=number, has_side_effects=True),
    )(*inputs)


def gather_pair(number, first, second):
    count = lax.axis_size("dp")

    def body(a_ref, b_ref, c_ref, d_ref, sends, receives):
        greet(ring_peers(count))
        ring = RingGather(count, (a_ref, b_ref), (c_ref, d_ref), sends, receives)
        ring.start()
        ring.own()
        ring.steps()
        ring.finish()

    outputs = [jax.ShapeDtypeStruct((count,) + x.shape, x.dtype) for x in (first, second)]
    scratch = ring_scratch(count, pieces_of(first.shape[-1]))
    return call_kernel(body, "gather_pair", number, (first, second), outputs, scratch)


def sum_and_gather(number, part, first, second):
    count, wide = lax.axis_size("dp"), lax.axis_size("tensor")

    def body(x_ref, a_ref, b_ref, y_ref, c_ref, d_ref, sends, receives, *cube):
        greet(ring_peers(count) + cube_peers(wide))
        ring = RingGather(count, (a_ref, b_ref), (c_ref, d_ref), sends, receives)
        adder = CubeSum(wide, x_ref, y_ref, *cube)
        adder.start()
        ring.start()
        ring.own()
        adder.add(0)
        ring.steps()
        adder.last()
        adder.finish()
        ring.finish()

    outputs = [jax.ShapeDtypeStruct(part.shape, part.dtype)] + [
        jax.ShapeDtypeStruct((count,) + x.shape, x.dtype) for x in (first, second)
    ]
    scratch = ring_scratch(count, pieces_of(first.shape[-1])) + cube_scratch(wide, *part.shape)
    return call_kernel(body, "sum_and_gather", number, (part, first, second), outputs, scratch)


def sum_and_reduce(number, parts, first, second):
    count, wide, several = lax.axis_size("dp"), lax.axis_size("tensor"), len(parts)

    def body(*refs):
        x_refs, (a_ref, b_ref), refs = refs[:several], refs[several : several + 2], refs[several + 2 :]
        y_refs, (c_ref, d_ref), refs = refs[:several], refs[several : several + 2], refs[several + 2 :]
        slot_a, slot_b, sends, receives = refs[:4]
        greet(ring_peers(count) + cube_peers(wide))
        ring = RingReduce(
            count, (a_ref, b_ref), (slot_a, slot_b), (c_ref, d_ref), sends, receives
        )
        adders = [
            CubeSum(wide, x_refs[k], y_refs[k], *refs[4 + 4 * k : 8 + 4 * k])
            for k in range(several)
        ]
        for adder in adders:
            adder.start()
        ring.start()
        for adder in adders:
            adder.add(0)
        ring.steps()
        for adder in adders:
            adder.last()
        ring.finish()
        for adder in adders:
            adder.finish()

    outputs = [jax.ShapeDtypeStruct(x.shape, x.dtype) for x in parts] + [
        jax.ShapeDtypeStruct(x.shape[1:], jnp.float32) for x in (first, second)
    ]
    scratch = [
        pltpu.VMEM((2, count // 2) + x.shape[1:], jnp.bfloat16) for x in (first, second)
    ] + ring_scratch(count, pieces_of(first.shape[-1]))
    for part in parts:
        scratch += cube_scratch(wide, *part.shape)
    return call_kernel(
        body, "sum_and_reduce", number, (*parts, first, second), outputs, scratch
    )


def sum_small(number, values):
    count = lax.axis_size("dp")

    def body(x_ref, y_ref, slots, sends, receives):
        index = lax.axis_index("dp")
        peers = [lax.rem(index + step, count) for step in range(1, count)]
        greet([{"dp": peer} for peer in peers])

        def copy(step):
            return pltpu.make_async_remote_copy(
                src_ref=x_ref,
                dst_ref=slots.at[index],
                send_sem=sends.at[step],
                recv_sem=receives.at[step],
                device_id={"dp": peers[step]},
                device_id_type=MESH_ID,
            )

        for step in range(count - 1):
            copy(step).start()
        slots[index] = x_ref[...]
        for step in range(count - 1):
            copy(step).wait_recv()
        total = slots[0]
        for place in range(1, count):
            total = total + slots[place]
        y_ref[...] = total
        for step in range(count - 1):
            copy(step).wait_send()

    return call_kernel(
        body,
        "sum_small",
        number,
        (values,),
        [jax.ShapeDtypeStruct(values.shape, values.dtype)],
        [
            pltpu.VMEM((count,) + values.shape, values.dtype),
            pltpu.SemaphoreType.DMA((count - 1,)),
            pltpu.SemaphoreType.DMA((count - 1,)),
        ],
    )[0]


SEGMENT_LIMIT = 512
ROWS = 256


def row_blocks(length):
    rows = ROWS if length % ROWS == 0 else length
    for begin in range(0, length, rows):
        yield begin, rows, max(0, begin - SEGMENT_LIMIT // rows * rows), begin + rows


def allowed_block(seg_column, seg_row, begin, rows, low, high):
    query_at = begin + lax.broadcasted_iota(jnp.int32, (rows, high - low), 0)
    key_at = low + lax.broadcasted_iota(jnp.int32, (rows, high - low), 1)
    same = seg_column[begin : begin + rows, :] == seg_row[:, low:high]
    return same & (key_at <= query_at)


def contract(left, right, left_axis, right_axis):
    return lax.dot_general(
        left, right, (((left_axis,), (right_axis,)), ((), ())), preferred_element_type=jnp.float32
    )


def attention_forward(seg_column, seg_row, query, keys, values):
    length, group = query.shape
    heads = group // HD

    def body(sc_ref, sr_ref, q_ref, k_ref, v_ref, c_ref, l_ref):
        for begin, rows, low, high in row_blocks(length):
            allowed = allowed_block(sc_ref, sr_ref, begin, rows, low, high)
            for head in range(heads):
                span = slice(head * HD, (head + 1) * HD)
                own = slice(begin, begin + rows)
                scores = contract(q_ref[own, span], k_ref[low:high, span], 1, 1)
                scores = jnp.where(allowed, scores, MASK_FILL)
                largest = jnp.max(scores, axis=1, keepdims=True)
                raised = jnp.exp(scores - largest)
                total = jnp.sum(raised, axis=1, keepdims=True)
                probs = (raised * (1.0 / total)).astype(jnp.bfloat16)
                c_ref[own, span] = contract(probs, v_ref[low:high, span], 1, 0).astype(jnp.bfloat16)
                l_ref[own, head : head + 1] = largest + jnp.log(total)

    vmem = pl.BlockSpec(memory_space=pltpu.VMEM)
    return pl.pallas_call(
        body,
        name="attention_forward",
        out_shape=[
            jax.ShapeDtypeStruct((length, group), jnp.bfloat16),
            jax.ShapeDtypeStruct((length, heads), jnp.float32),
        ],
        in_specs=[vmem] * 5,
        out_specs=[vmem] * 2,
    )(seg_column, seg_row, query, keys, values)


def attention_backward(seg_column, seg_row, query, keys, values, context, logs, upstream, scale):
    length, group = query.shape
    heads = group // HD

    def body(sc_ref, sr_ref, q_ref, k_ref, v_ref, c_ref, l_ref, u_ref, g_ref, b_ref, dk_ref, dv_ref):
        dk_ref[...] = jnp.zeros_like(dk_ref)
        dv_ref[...] = jnp.zeros_like(dv_ref)
        bias = [jnp.zeros((1, HD), jnp.float32) for _ in range(heads)]
        for begin, rows, low, high in row_blocks(length):
            allowed = allowed_block(sc_ref, sr_ref, begin, rows, low, high)
            own = slice(begin, begin + rows)
            for head in range(heads):
                span = slice(head * HD, (head + 1) * HD)
                query_block, upstream_block = q_ref[own, span], u_ref[own, span]
                keys_block = k_ref[low:high, span]
                scores = jnp.where(allowed, contract(query_block, keys_block, 1, 1), MASK_FILL)
                probs = jnp.exp(scores - l_ref[own, head : head + 1])
                grad_probs = contract(upstream_block, v_ref[low:high, span], 1, 1)
                delta = jnp.sum(
                    upstream_block.astype(jnp.float32) * c_ref[own, span].astype(jnp.float32),
                    axis=1,
                    keepdims=True,
                )
                grad_scores = (probs * (grad_probs - delta)).astype(jnp.bfloat16)
                grad_query = contract(grad_scores, keys_block, 1, 0) * scale
                g_ref[own, span] = grad_query.astype(jnp.bfloat16)
                bias[head] = bias[head] + jnp.sum(grad_query, axis=0, keepdims=True)
                dk_ref[head, low:high] += contract(grad_scores, query_block, 0, 0)
                dv_ref[head, low:high] += contract(
                    probs.astype(jnp.bfloat16), upstream_block, 0, 0
                )
        for head in range(heads):
            span = slice(head * HD, (head + 1) * HD)
            b_ref[0:1, span] = bias[head]
            b_ref[1:2, span] = jnp.sum(dv_ref[head], axis=0, keepdims=True)
            g_ref[:, group + head * HD : group + (head + 1) * HD] = dk_ref[head].astype(
                jnp.bfloat16
            )
            g_ref[:, 2 * group + head * HD : 2 * group + (head + 1) * HD] = dv_ref[head].astype(
                jnp.bfloat16
            )

    vmem = pl.BlockSpec(memory_space=pltpu.VMEM)
    return pl.pallas_call(
        body,
        name="attention_backward",
        out_shape=[
            jax.ShapeDtypeStruct((length, 3 * group), jnp.bfloat16),
            jax.ShapeDtypeStruct((2, group), jnp.float32),
        ],
        in_specs=[vmem] * 8,
        out_specs=[vmem] * 2,
        scratch_shapes=[pltpu.VMEM((heads, length, HD), jnp.float32)] * 2,
    )(seg_column, seg_row, query, keys, values, context, logs, upstream)


def adam_update(param, grad, first, second, decay):
    first_new = BETA_ONE * first + (1.0 - BETA_ONE) * grad
    second_new = BETA_TWO * second + (1.0 - BETA_TWO) * grad * grad
    first_hat = first_new / (1.0 - BETA_ONE**ADAM_STEP)
    second_hat = second_new / (1.0 - BETA_TWO**ADAM_STEP)
    param_new = param - LEARN_RATE * (first_hat / (jnp.sqrt(second_hat) + ADAM_EPS) + decay * param)
    return (param_new, first_new, second_new)


def on_device(
    tokens,
    cotangent,
    segments,
    w_qkv,
    w_proj,
    w_fc,
    w_fc2,
    w_vectors,
    w_qvbias,
    w_fcbias,
    m_qkv,
    m_proj,
    m_fc,
    m_fc2,
    m_vectors,
    m_qvbias,
    m_fcbias,
    v_qkv,
    v_proj,
    v_fc,
    v_fc2,
    v_vectors,
    v_qvbias,
    v_fcbias,
):
    bfloat = jnp.bfloat16
    count = lax.axis_size("dp")
    depth, _, group = w_qkv.shape
    width = depth * count
    scale = 1.0 / math.sqrt(HD)
    proj_rows = w_proj.shape[0]
    qkv_bf = w_qkv.astype(bfloat)
    first_pair = jnp.concatenate([qkv_bf[:, 0], qkv_bf[:, 1]], axis=1)
    second_pair = jnp.concatenate(
        [qkv_bf[:, 2], w_proj.astype(bfloat).reshape(depth, proj_rows * width // depth)], axis=1
    )
    pair_full = gather_pair(0, first_pair, second_pair)
    first_full, second_full = (x.reshape(width, x.shape[2]) for x in pair_full)
    qkv_flat = jnp.concatenate([first_full, second_full[:, :group]], axis=1)
    proj_full = second_full[:, group:].reshape(proj_rows * count, width)

    inputs_f = tokens[0].astype(jnp.float32)
    seg_row = segments[0]
    first_in, normed_one, inverse_one = layer_norm(inputs_f, w_vectors[0], w_vectors[1])
    first_bf = first_in.astype(bfloat)
    projected = jnp.dot(first_bf, qkv_flat, preferred_element_type=jnp.float32)
    query = ((projected[:, :group] + w_qvbias[0]) * scale).astype(bfloat)
    keys = projected[:, group : 2 * group].astype(bfloat)
    values = (projected[:, 2 * group :] + w_qvbias[1]).astype(bfloat)
    sides = (seg_row[:, None], seg_row[None, :])
    context_flat, log_total = attention_forward(*sides, query, keys, values)
    attn_part = jnp.dot(context_flat, proj_full, preferred_element_type=jnp.float32)
    attn_sum, fc_full, fc2_full = sum_and_gather(
        1, attn_part.astype(bfloat), w_fc.astype(bfloat), w_fc2.astype(bfloat)
    )
    fc_full = fc_full.reshape(width, w_fc.shape[1])
    fc2_full = fc2_full.reshape(w_fc2.shape[0] * count, width)
    middle = (
        inputs_f
        + attn_sum.astype(jnp.float32)
        + w_vectors[4]
    )
    second_in, normed_two, inverse_two = layer_norm(middle, w_vectors[2], w_vectors[3])
    second_bf = second_in.astype(bfloat)
    hidden_pre = jnp.dot(second_bf, fc_full, preferred_element_type=jnp.float32) + w_fcbias
    hidden_bf = gelu_value(hidden_pre).astype(bfloat)
    mlp_part = jnp.dot(hidden_bf, fc2_full, preferred_element_type=jnp.float32)
    upstream = cotangent[0]
    grad_out = upstream.astype(jnp.float32)
    grad_fc2 = jnp.dot(hidden_bf.T, upstream, preferred_element_type=jnp.float32)
    grad_hidden = jnp.dot(upstream, fc2_full.T, preferred_element_type=jnp.float32) * gelu_slope(
        hidden_pre
    )
    grad_hidden_bf = grad_hidden.astype(bfloat)
    grad_fc = jnp.dot(second_bf.T, grad_hidden_bf, preferred_element_type=jnp.float32)
    grad_fcbias = jnp.sum(grad_hidden, axis=0)
    norm_two_part = jnp.dot(grad_hidden_bf, fc_full.T, preferred_element_type=jnp.float32)
    mlp_sum, norm_two_sum, fc2_summed, fc_summed = sum_and_reduce(
        2,
        (mlp_part.astype(bfloat), norm_two_part.astype(bfloat)),
        grad_fc2.astype(bfloat).reshape(count, w_fc2.shape[0], width),
        grad_fc.astype(bfloat).reshape(count, depth, w_fc.shape[1]),
    )
    output = (middle + mlp_sum.astype(jnp.float32) + w_vectors[5]).astype(bfloat)
    back_two, gain_two, shift_two = norm_backward(
        norm_two_sum.astype(jnp.float32),
        normed_two,
        inverse_two,
        w_vectors[2],
    )
    grad_middle = grad_out + back_two
    grad_middle_bf = grad_middle.astype(bfloat)
    grad_proj = jnp.dot(context_flat.T, grad_middle_bf, preferred_element_type=jnp.float32)
    grad_context = jnp.dot(grad_middle_bf, proj_full.T, preferred_element_type=jnp.float32).astype(
        bfloat
    )
    grad_stack, grad_qvbias = attention_backward(
        *sides, query, keys, values, context_flat, log_total, grad_context, scale
    )
    grad_qkv = jnp.dot(first_bf.T, grad_stack, preferred_element_type=jnp.float32).astype(bfloat)
    norm_one_part = jnp.dot(grad_stack, qkv_flat.T, preferred_element_type=jnp.float32)
    grad_first = grad_qkv[:, : 2 * group].reshape(count, depth, 2 * group)
    grad_second = jnp.concatenate(
        [grad_qkv[:, 2 * group :], grad_proj.astype(bfloat).reshape(width, group)], axis=1
    ).reshape(count, depth, 2 * group)
    norm_one_sum, first_summed, second_summed = sum_and_reduce(
        3, (norm_one_part.astype(bfloat),), grad_first, grad_second
    )
    qkv_summed = jnp.concatenate([first_summed, second_summed[:, :group]], axis=1).reshape(
        depth, 3, group
    )
    proj_summed = second_summed[:, group:].reshape(proj_rows, width)
    back_one, gain_one, shift_one = norm_backward(
        norm_one_sum.astype(jnp.float32),
        normed_one,
        inverse_one,
        w_vectors[0],
    )
    grad_input = (grad_middle + back_one).astype(bfloat)
    grad_vectors = jnp.stack(
        [
            gain_one,
            shift_one,
            gain_two,
            shift_two,
            jnp.sum(grad_middle, axis=0),
            jnp.sum(grad_out, axis=0),
        ]
    )
    small = jnp.concatenate(
        [grad_vectors.reshape(-1), grad_qvbias.reshape(-1), grad_fcbias.reshape(-1)]
    )
    small_size = small.shape[0]
    small_rows = -(-small_size // width)
    small_sum = sum_small(
        4, jnp.pad(small, (0, small_rows * width - small_size)).reshape(small_rows, width)
    ).reshape(-1)
    cut_one = grad_vectors.size
    cut_two = cut_one + grad_qvbias.size
    vectors_summed = small_sum[:cut_one].reshape(grad_vectors.shape)
    qvbias_summed = small_sum[cut_one:cut_two].reshape(grad_qvbias.shape)
    fcbias_summed = small_sum[cut_two:small_size]
    params = (w_qkv, w_proj, w_fc, w_fc2, w_vectors, w_qvbias, w_fcbias)
    gradients = (
        qkv_summed,
        proj_summed,
        fc_summed,
        fc2_summed,
        vectors_summed,
        qvbias_summed,
        fcbias_summed,
    )
    firsts = (m_qkv, m_proj, m_fc, m_fc2, m_vectors, m_qvbias, m_fcbias)
    seconds = (v_qkv, v_proj, v_fc, v_fc2, v_vectors, v_qvbias, v_fcbias)
    decays = (DECAY_RATE, DECAY_RATE, DECAY_RATE, DECAY_RATE, 0.0, 0.0, 0.0)
    updates = [
        adam_update(p, g, m, v, c)
        for p, g, m, v, c in zip(params, gradients, firsts, seconds, decays)
    ]
    return (
        output[None],
        grad_input[None],
        gradients[0],
        gradients[1],
        gradients[2],
        gradients[3],
        gradients[4],
        gradients[5],
        gradients[6],
        updates[0][0],
        updates[1][0],
        updates[2][0],
        updates[3][0],
        updates[4][0],
        updates[5][0],
        updates[6][0],
        updates[0][1],
        updates[1][1],
        updates[2][1],
        updates[3][1],
        updates[4][1],
        updates[5][1],
        updates[6][1],
        updates[0][2],
        updates[1][2],
        updates[2][2],
        updates[3][2],
        updates[4][2],
        updates[5][2],
        updates[6][2],
    )


BLOCK = 256


class Wires:
    def __init__(self, sends, receives):
        self.sends, self.receives, self.made = sends, receives, []

    def copy(self, source, target, peer):
        place = len(self.made)
        made = pltpu.make_async_remote_copy(
            src_ref=source,
            dst_ref=target,
            send_sem=self.sends.at[place],
            recv_sem=self.receives.at[place],
            device_id=peer,
            device_id_type=MESH_ID,
        )
        self.made.append(made)
        return made

    def drain(self):
        for made in self.made:
            made.wait_send()


class Grid:
    def __init__(self):
        self.count = lax.axis_size("dp")
        self.lines = self.count // 2
        self.index = lax.axis_index("dp")
        self.line, self.pair = lax.div(self.index, 2), lax.rem(self.index, 2)
        self.across = {"dp": self.line * 2 + 1 - self.pair}
        tensor = lax.axis_index("tensor")
        self.side = lax.rem(tensor, 2)
        self.core, self.far = {"tensor": flip_bit(tensor, 0)}, {"tensor": flip_bit(tensor, 1)}

    def owner(self, step, pair):
        return lax.rem(self.line + step + 2 * self.lines, self.lines) * 2 + pair

    def along(self, step):
        return {"dp": self.owner(step, self.pair)}

    def peers(self):
        return [self.across, self.core, self.far] + [self.along(s) for s in range(1, self.lines)]


class Gather:
    def __init__(self, grid, wires, full):
        self.grid, self.full, self.depth = grid, full, full.shape[0] // grid.count
        own = self.rows(grid.index)
        self.long = [
            wires.copy(own, own, grid.along(step)) for step in range(1, grid.lines)
        ]
        self.short = [wires.copy(own, own, grid.across)]
        for step in range(1, grid.lines):
            block = self.rows(grid.owner(-step, grid.pair))
            self.short.append(wires.copy(block, block, grid.across))

    def span(self, owner):
        return pl.ds(pl.multiple_of(owner * self.depth, 16), self.depth)

    def rows(self, owner):
        return self.full.at[self.span(owner)]

    def start(self):
        for made in self.long + self.short[:1]:
            made.start()

    def forward(self):
        for step in range(1, self.grid.lines):
            self.long[step - 1].wait_recv()
            self.short[step].start()

    def finish(self):
        for made in self.short:
            made.wait_recv()


class Reduce:
    def __init__(self, grid, wires, source, near, far):
        self.grid, self.source, self.near, self.far = grid, source, near, far
        self.depth = source.shape[0] // grid.count
        self.short = [
            wires.copy(
                self.rows(grid.owner(step, 1 - grid.pair)), near.at[step - 1], grid.across
            )
            for step in range(1, grid.lines + 1)
        ]
        self.long = [
            wires.copy(self.rows(grid.owner(step, grid.pair)), far.at[step - 1], grid.along(step))
            for step in range(1, grid.lines)
        ]

    def span(self, owner):
        return pl.ds(pl.multiple_of(owner * self.depth, 16), self.depth)

    def rows(self, owner):
        return self.source.at[self.span(owner)]

    def start(self):
        for made in self.short:
            made.start()

    def forward(self):
        for step in range(1, self.grid.lines):
            self.short[step - 1].wait_recv()
            span = self.span(self.grid.owner(step, self.grid.pair))
            own, arrived = self.source[span, :], self.near[step - 1]
            self.source[span, :] = (
                own.astype(jnp.float32) + arrived.astype(jnp.float32)
            ).astype(jnp.bfloat16)
            self.long[step - 1].start()

    def finish(self):
        total = self.source[self.span(self.grid.index), :].astype(jnp.float32)
        self.short[-1].wait_recv()
        total = total + self.near[self.grid.lines - 1].astype(jnp.float32)
        for step in range(1, self.grid.lines):
            self.long[step - 1].wait_recv()
            total = total + self.far[step - 1].astype(jnp.float32)
        return total


class Share:
    def __init__(self, grid, wires, part, arrivals, out):
        self.part, self.arrivals, self.out = part, arrivals, out
        self.half, self.side = arrivals.shape[2], grid.side
        blocks = range(arrivals.shape[1])
        self.first = [
            wires.copy(part.at[self.span(b, 1 - grid.side)], arrivals.at[0, b], grid.core)
            for b in blocks
        ]
        self.second = [
            wires.copy(part.at[self.mine(b)], arrivals.at[1, b], grid.far) for b in blocks
        ]
        self.third = [
            wires.copy(out.at[self.mine(b)], out.at[self.mine(b)], grid.core) for b in blocks
        ]

    def span(self, block, side):
        begin = block * 2 * self.half + side * self.half
        return pl.ds(pl.multiple_of(begin, self.half), self.half)

    def mine(self, block):
        return self.span(block, self.side)

    def give(self, block, value):
        rows = 2 * self.half
        self.part[block * rows : (block + 1) * rows, :] = value.astype(jnp.bfloat16)
        self.first[block].start()

    def cross(self, block):
        self.first[block].wait_recv()
        span = self.mine(block)
        own, arrived = self.part[span, :], self.arrivals[0, block]
        self.part[span, :] = (own.astype(jnp.float32) + arrived.astype(jnp.float32)).astype(
            jnp.bfloat16
        )
        self.second[block].start()

    def take(self, block):
        self.second[block].wait_recv()
        own, arrived = self.part[self.mine(block), :], self.arrivals[1, block]
        return own.astype(jnp.float32) + arrived.astype(jnp.float32)

    def put(self, block, value):
        self.out[self.mine(block), :] = value.astype(jnp.bfloat16)
        self.third[block].start()

    def close(self, block):
        self.third[block].wait_recv()


def column_sum(values):
    return jnp.sum(values, axis=0, keepdims=True)


def padded_rows(rows):
    return -(-rows // 16) * 16


def fused_body(scale, shapes, *refs):
    length, width, group, hidden, depth, proj_rows = shapes
    (
        x_ref, g_ref, sc_ref, sr_ref, wq_ref, wo_ref, w1_ref, w2_ref, vec_ref, qv_ref, fb_ref,
        out_ref, gt_ref, gq_ref, go_ref, g1_ref, g2_ref, gv_ref, gqv_ref, gfb_ref,
        fq, fo, f1, f2, wo_f, wo, a1, q_s, k_s, v_s, c_s, pr_s, h_s, dh_s, a2, dhb, gw, u_s, dz_s,
        dk_s, dv_s, dp_s, part_a, part_n, part_m, part_i, arr_a, arr_n, arr_m, arr_i,
        sq, so, s1, s2, nq, no, n1, n2, rq, ro, r1, r2, sm_own, sm_core, sm_two, sm_pair, sm_four,
        sm_line, sends, receives,
    ) = refs
    f32, b16 = jnp.float32, jnp.bfloat16
    grid, wires = Grid(), Wires(sends, receives)
    heads, rows = group // HD, BLOCK
    pad = padded_rows(proj_rows)
    blocks = length // rows
    order = list(range(blocks))[::-1]

    gathers = {n: Gather(grid, wires, f) for n, f in (("q", fq), ("o", fo), ("2", f2), ("1", f1))}
    share_a = Share(grid, wires, part_a, arr_a, a2)
    share_n = Share(grid, wires, part_n, arr_n, dhb)
    share_m = Share(grid, wires, part_m, arr_m, out_ref)
    share_i = Share(grid, wires, part_i, arr_i, gt_ref)
    reduce_2, reduce_1 = Reduce(grid, wires, s2, n2, r2), Reduce(grid, wires, s1, n1, r1)
    reduce_q, reduce_o = Reduce(grid, wires, sq, nq, rq), Reduce(grid, wires, so, no, ro)
    small_core = wires.copy(sm_own, sm_core, grid.core)
    small_pair = wires.copy(sm_two, sm_pair, grid.across)
    small_line = [
        wires.copy(sm_four, sm_line.at[s - 1], grid.along(s)) for s in range(1, grid.lines)
    ]

    def block_rows(b):
        return slice(b * rows, (b + 1) * rows)

    barrier = pltpu.get_barrier_semaphore()
    peers = grid.peers()
    for peer in peers:
        pl.semaphore_signal(barrier, inc=1, device_id=peer, device_id_type=MESH_ID)
    own_rows = gathers["q"].span(grid.index)
    for j in range(3):
        fq[own_rows, j * group : (j + 1) * group] = wq_ref[j].astype(b16)
    own_proj = wo_ref[...]
    if pad > proj_rows:
        own_proj = jnp.concatenate([own_proj, jnp.zeros((pad - proj_rows, width), f32)], axis=0)
    fo[gathers["o"].span(grid.index), :] = own_proj.astype(b16)
    f2[gathers["2"].span(grid.index), :] = w2_ref[...].astype(b16)
    f1[gathers["1"].span(grid.index), :] = w1_ref[...].astype(b16)
    pl.semaphore_wait(barrier, len(peers))
    gathers["q"].start()
    gathers["o"].start()

    for b in order:
        first_in, _, _ = layer_norm(x_ref[block_rows(b), :].astype(f32), vec_ref[0:1], vec_ref[1:2])
        a1[block_rows(b), :] = first_in.astype(b16)
    dk_s[...] = jnp.zeros_like(dk_s)
    dv_s[...] = jnp.zeros_like(dv_s)
    sum_g = jnp.zeros((1, width), f32)
    for b in order:
        sum_g = sum_g + column_sum(g_ref[share_a.mine(b), :].astype(f32))
    sm_own[5:6, :] = sum_g

    gathers["q"].forward()
    gathers["o"].forward()
    gathers["2"].start()
    gathers["1"].start()
    gathers["q"].finish()
    for b in order:
        projected = jnp.dot(a1[block_rows(b), :], fq[...], preferred_element_type=f32)
        q_s[block_rows(b), :] = ((projected[:, :group] + qv_ref[0:1]) * scale).astype(b16)
        k_s[block_rows(b), :] = projected[:, group : 2 * group].astype(b16)
        v_s[block_rows(b), :] = (projected[:, 2 * group :] + qv_ref[1:2]).astype(b16)
    gathers["o"].finish()
    for i in range(grid.count):
        block = fo[i * pad : (i + 1) * pad, :].astype(f32)
        wo_f[i * proj_rows : (i + 1) * proj_rows, :] = block[:proj_rows]
    wo[...] = wo_f[...].astype(b16)

    def window(b):
        return max(0, b * rows - -(-SEGMENT_LIMIT // rows) * rows), (b + 1) * rows

    def attend(b):
        low, high = window(b)
        allowed = allowed_block(sc_ref, sr_ref, b * rows, rows, low, high)
        bias = jnp.where(allowed, 0.0, MASK_FILL)
        for head in range(heads):
            span = slice(head * HD, (head + 1) * HD)
            scores = contract(q_s[block_rows(b), span], k_s[low:high, span], 1, 1) + bias
            largest = jnp.max(scores, axis=1, keepdims=True)
            raised = jnp.exp(scores - largest)
            total = jnp.sum(raised, axis=1, keepdims=True)
            probs = (raised * (1.0 / total)).astype(b16)
            pr_s[b, head, :, : high - low] = probs
            c_s[block_rows(b), span] = contract(probs, v_s[low:high, span], 1, 0).astype(b16)

    for i, b in enumerate(order):
        attend(b)
        share_a.give(b, jnp.dot(c_s[block_rows(b), :], wo[...], preferred_element_type=f32))
        if i >= 1:
            share_a.cross(order[i - 1])
        if i == blocks - 2:
            gathers["2"].forward()
    share_a.cross(order[-1])
    gathers["1"].forward()

    gathers["2"].finish()
    for b in order:
        total = share_a.take(b)
        middle = x_ref[share_a.mine(b), :].astype(f32) + total + vec_ref[4:5]
        h_s[b] = middle
        second_in, _, _ = layer_norm(middle, vec_ref[2:3], vec_ref[3:4])
        share_a.put(b, second_in)
        gw[block_rows(b), :] = contract(g_ref[block_rows(b), :], f2[...], 1, 1)
    gathers["1"].finish()

    tile = 256 if hidden % 256 == 0 else hidden
    sum_fb = [jnp.zeros((1, tile), f32) for _ in range(hidden // tile)]
    sums = {"gain2": jnp.zeros((1, width), f32), "shift2": jnp.zeros((1, width), f32)}
    sums["mid"] = jnp.zeros((1, width), f32)

    def take_n(b):
        upstream = share_n.take(b)
        _, normed, inverse = layer_norm(h_s[b], vec_ref[2:3], vec_ref[3:4])
        back, _, _ = norm_backward(upstream, normed, inverse, vec_ref[2:3])
        sums["gain2"] = sums["gain2"] + column_sum(upstream * normed)
        sums["shift2"] = sums["shift2"] + column_sum(upstream)
        grad_middle = g_ref[share_n.mine(b), :].astype(f32) + back
        sums["mid"] = sums["mid"] + column_sum(grad_middle)
        dh_s[b] = grad_middle
        share_n.put(b, grad_middle)

    for i, b in enumerate(order):
        share_a.close(b)
        for c in range(hidden // tile):
            span = slice(c * tile, (c + 1) * tile)
            z = jnp.dot(a2[block_rows(b), :], f1[:, span], preferred_element_type=f32)
            z = z + fb_ref[:, span]
            square = z * z
            tangent = jnp.tanh(GELU_COEF * z * (1.0 + CUBIC_COEF * square))
            half = 0.5 * (1.0 + tangent)
            u_s[block_rows(b), span] = (z * half).astype(b16)
            slope = half + 0.5 * z * (1.0 - tangent * tangent) * GELU_COEF * (
                1.0 + 3.0 * CUBIC_COEF * square
            )
            dz = gw[block_rows(b), span] * slope
            sum_fb[c] = sum_fb[c] + column_sum(dz)
            dz_s[block_rows(b), span] = dz.astype(b16)
        share_n.give(b, contract(dz_s[block_rows(b), :], f1[...], 1, 1))
        share_m.give(b, jnp.dot(u_s[block_rows(b), :], f2[...], preferred_element_type=f32))
        share_n.cross(b)
        if i >= 1:
            take_n(order[i - 1])
    for c in range(hidden // tile):
        sm_own[6:7, c * tile : (c + 1) * tile] = sum_fb[c]

    def outer(target, left, right):
        for begin in range(0, target.shape[0], BLOCK):
            target[begin : begin + BLOCK, :] = contract(
                left[:, begin : begin + BLOCK], right[...], 0, 0
            ).astype(b16)

    outer(s2, u_s, g_ref)
    reduce_2.start()
    take_n(order[-1])
    outer(s1, a2, dz_s)
    reduce_1.start()
    for name, row in (("gain2", 2), ("shift2", 3), ("mid", 4)):
        sm_own[row : row + 1, :] = sums[name]
    for b in order:
        share_m.cross(b)

    bias_q = [jnp.zeros((1, HD), f32) for _ in range(heads)]
    bias_v = [jnp.zeros((1, HD), f32) for _ in range(heads)]

    def attend_back(b):
        low, high = window(b)
        grad_context = contract(dhb[block_rows(b), :], wo[...], 1, 1).astype(b16)
        for head in range(heads):
            span = slice(head * HD, (head + 1) * HD)
            upstream = grad_context[:, span]
            probs = pr_s[b, head, :, : high - low]
            keys_block = k_s[low:high, span]
            grad_probs = contract(upstream, v_s[low:high, span], 1, 1)
            delta = jnp.sum(
                upstream.astype(f32) * c_s[block_rows(b), span].astype(f32), axis=1, keepdims=True
            )
            grad_scores = (probs.astype(f32) * (grad_probs - delta)).astype(b16)
            grad_query = contract(grad_scores, keys_block, 1, 0) * scale
            dp_s[block_rows(b), span] = grad_query.astype(b16)
            bias_q[head] = bias_q[head] + column_sum(grad_query)
            dk_s[head, low:high] += contract(grad_scores, q_s[block_rows(b), span], 0, 0)
            dv_s[head, low:high] += contract(probs, upstream, 0, 0)
        for head in range(heads):
            begin = group + head * HD
            dp_s[block_rows(b), begin : begin + HD] = dk_s[head, block_rows(b)].astype(b16)
            grad_value = dv_s[head, block_rows(b)]
            bias_v[head] = bias_v[head] + column_sum(grad_value)
            dp_s[block_rows(b), begin + group : begin + group + HD] = grad_value.astype(b16)

    for i, b in enumerate(order):
        share_n.close(b)
        attend_back(b)
        share_i.give(b, contract(dp_s[block_rows(b), :], fq[...], 1, 1))
        if i >= 1:
            share_i.cross(order[i - 1])
        if i == 0:
            reduce_2.forward()
        if i == min(2, blocks - 1):
            reduce_1.forward()
    share_i.cross(order[-1])
    sm_own[7:8, :] = jnp.zeros((1, width), f32)
    for head in range(heads):
        sm_own[7:8, head * HD : (head + 1) * HD] = bias_q[head]
        sm_own[7:8, group + head * HD : group + (head + 1) * HD] = bias_v[head]

    outer(sq, a1, dp_s)
    reduce_q.start()
    grad_proj = contract(c_s[...], dhb[...], 0, 0)
    for i in range(grid.count):
        block = grad_proj[i * proj_rows : (i + 1) * proj_rows]
        if pad > proj_rows:
            block = jnp.concatenate([block, jnp.zeros((pad - proj_rows, width), f32)], axis=0)
        so[i * pad : (i + 1) * pad, :] = block.astype(b16)
    reduce_o.start()

    for b in order:
        share_m_total = share_m.take(b)
        share_m.put(b, h_s[b] + share_m_total + vec_ref[5:6])
    gain, shift = jnp.zeros((1, width), f32), jnp.zeros((1, width), f32)
    for i, b in enumerate(order):
        upstream = share_i.take(b)
        _, normed, inverse = layer_norm(
            x_ref[share_i.mine(b), :].astype(f32), vec_ref[0:1], vec_ref[1:2]
        )
        back, _, _ = norm_backward(upstream, normed, inverse, vec_ref[0:1])
        gain = gain + column_sum(upstream * normed)
        shift = shift + column_sum(upstream)
        share_i.put(b, dh_s[b] + back)
        if i == 0:
            reduce_q.forward()
            reduce_o.forward()
    sm_own[0:1, :] = gain
    sm_own[1:2, :] = shift
    small_core.start()
    g2_ref[...] = reduce_2.finish()
    small_core.wait_recv()
    sm_two[0:6, :] = sm_own[0:6, :] + sm_core[0:6, :]
    sm_two[6:8, :] = sm_own[6:8, :]
    small_pair.start()
    g1_ref[...] = reduce_1.finish()
    small_pair.wait_recv()
    sm_four[...] = sm_two[...] + sm_pair[...]
    for made in small_line:
        made.start()
    total_q = reduce_q.finish()
    for j in range(3):
        gq_ref[j] = total_q[:, j * group : (j + 1) * group]
    go_ref[...] = reduce_o.finish()[:proj_rows]
    total = sm_four[...]
    for step, made in enumerate(small_line):
        made.wait_recv()
        total = total + sm_line[step]
    gv_ref[...] = total[0:6]
    gfb_ref[...] = total[6:7]
    gqv_ref[0:1, :] = total[7:8, :group]
    gqv_ref[1:2, :] = total[7:8, group : 2 * group]
    for b in order:
        share_m.close(b)
        share_i.close(b)
    wires.drain()


def fused_call(x, g, seg, wq, wo, w1, w2, vec, qv, fb):
    f32, b16 = jnp.float32, jnp.bfloat16
    length, width = x.shape
    _, depth, group = wq.shape
    hidden, proj_rows = w1.shape[1], wo.shape[0]
    count, lines, blocks = lax.axis_size("dp"), lax.axis_size("dp") // 2, length // BLOCK
    heads, pad, half = group // HD, padded_rows(proj_rows), BLOCK // 2
    reach = min(length, -(-SEGMENT_LIMIT // BLOCK) * BLOCK + BLOCK)

    def full(*shape):
        return pltpu.VMEM(shape, b16)

    def wide(*shape):
        return pltpu.VMEM(shape, f32)

    scratch = [
        full(width, 3 * group), full(count * pad, width), full(width, hidden), full(hidden, width),
        wide(group, width), full(group, width), full(length, width),
        full(length, group), full(length, group), full(length, group), full(length, group),
        full(blocks, heads, BLOCK, reach),
        wide(blocks, half, width), wide(blocks, half, width),
        full(length, width), full(length, width), wide(length, hidden),
        full(length, hidden), full(length, hidden),
        wide(heads, length, HD), wide(heads, length, HD), full(length, 3 * group),
    ]
    scratch += [full(length, width)] * 4 + [full(2, blocks, half, width)] * 4
    shards = [(depth, 3 * group), (pad, width), (depth, hidden), (w2.shape[0], width)]
    scratch += [full(count * a, b) for a, b in shards]
    scratch += [full(lines, a, b) for a, b in shards]
    scratch += [full(lines - 1, a, b) for a, b in shards]
    scratch += [wide(8, width)] * 5 + [wide(lines - 1, 8, width)]
    copies = 8 * (2 * lines - 1) + 12 * blocks + 2 + lines - 1
    scratch += [pltpu.SemaphoreType.DMA((copies,))] * 2
    outputs = [
        jax.ShapeDtypeStruct(s, t)
        for s, t in (
            (x.shape, b16), (x.shape, b16), (wq.shape, f32), (wo.shape, f32), (w1.shape, f32),
            (w2.shape, f32), (vec.shape, f32), (qv.shape, f32), (fb.shape, f32),
        )
    ]
    vmem = pl.BlockSpec(memory_space=pltpu.VMEM)
    inputs = (x, g, seg.reshape(length, 1), seg.reshape(1, length), wq, wo, w1, w2, vec, qv, fb)
    shapes = (length, width, group, hidden, depth, proj_rows)
    return pl.pallas_call(
        functools.partial(fused_body, 1.0 / math.sqrt(HD), shapes),
        name="fused_block",
        out_shape=outputs,
        in_specs=[vmem] * len(inputs),
        out_specs=[vmem] * len(outputs),
        scratch_shapes=scratch,
        compiler_params=pltpu.CompilerParams(
            collective_id=5, has_side_effects=True, vmem_limit_bytes=VMEM_BYTES
        ),
    )(*inputs)


VMEM_BYTES = 63 * 1024 * 1024


def adam_body(number, *refs):
    keep = number // 4
    sources, results = refs[:number], refs[number:]
    pieces = [sources[k * keep : (k + 1) * keep] for k in range(4)]
    for k in range(keep):
        param, grad, first, second = (piece[k][...] for piece in pieces)
        decay = DECAY_RATE if k < 4 else 0.0
        new, first_new, second_new = adam_update(param, grad, first, second, decay)
        results[k][...] = grad
        results[keep + k][...] = new
        results[2 * keep + k][...] = first_new
        results[3 * keep + k][...] = second_new


def adam_call(params, gradients, firsts, seconds):
    inputs = (*params, *gradients, *firsts, *seconds)
    vmem = pl.BlockSpec(memory_space=pltpu.VMEM)
    outputs = [jax.ShapeDtypeStruct(p.shape, p.dtype) for p in params] * 4
    return pl.pallas_call(
        functools.partial(adam_body, len(inputs)),
        name="adam_step",
        out_shape=outputs,
        in_specs=[vmem] * len(inputs),
        out_specs=[vmem] * len(outputs),
    )(*inputs)


def turn(array):
    return jnp.transpose(array, (1, 0, 2))


def on_device_fused(tokens, cotangent, segments, *state):
    params, firsts, seconds = state[:7], state[7:14], state[14:]

    def shaped(group):
        return (turn(group[0]), *group[1:6], group[6].reshape(1, -1))

    params, firsts, seconds = shaped(params), shaped(firsts), shaped(seconds)
    results = fused_call(tokens[0], cotangent[0], segments[0], *params)
    updated = adam_call(params, results[2:], firsts, seconds)
    restored = [
        (turn(updated[k]), *updated[k + 1 : k + 6], updated[k + 6].reshape(-1))
        for k in range(0, 28, 7)
    ]
    return (results[0][None], results[1][None]) + sum(restored, ())


def fused_fits(mesh, args):
    tokens, w_qkv, w_proj, w_fc, w_fc2 = args[0], args[3], args[4], args[5], args[6]
    count, wide = mesh.shape["dp"], mesh.shape["tensor"]
    width, length = tokens.shape[2], tokens.shape[1]
    depth, group, hidden = width // count, w_qkv.shape[2] // wide, w_fc.shape[1] // wide
    proj_rows = w_proj.shape[0] // (wide * count)
    return (
        wide == 4
        and count % 2 == 0
        and count >= 4
        and depth % 16 == 0
        and (w_fc2.shape[0] // (wide * count)) % 16 == 0
        and proj_rows % 8 == 0
        and length % BLOCK == 0
        and width % BLOCK == 0
        and hidden % BLOCK == 0
        and hidden == width
        and 2 * group <= width
    )


def mapped(mesh, body):
    return jax.shard_map(
        body,
        mesh=mesh,
        in_specs=(
            P("dp", None, None),
            P("dp", None, None),
            P("dp", None),
            P("dp", None, "tensor"),
            P(("tensor", "dp"), None),
            P("dp", "tensor"),
            P(("tensor", "dp"), None),
            P(),
            P(None, "tensor"),
            P("tensor"),
            P("dp", None, "tensor"),
            P(("tensor", "dp"), None),
            P("dp", "tensor"),
            P(("tensor", "dp"), None),
            P(),
            P(None, "tensor"),
            P("tensor"),
            P("dp", None, "tensor"),
            P(("tensor", "dp"), None),
            P("dp", "tensor"),
            P(("tensor", "dp"), None),
            P(),
            P(None, "tensor"),
            P("tensor"),
        ),
        out_specs=(
            P("dp", None, None),
            P("dp", None, None),
            P("dp", None, "tensor"),
            P(("tensor", "dp"), None),
            P("dp", "tensor"),
            P(("tensor", "dp"), None),
            P(),
            P(None, "tensor"),
            P("tensor"),
            P("dp", None, "tensor"),
            P(("tensor", "dp"), None),
            P("dp", "tensor"),
            P(("tensor", "dp"), None),
            P(),
            P(None, "tensor"),
            P("tensor"),
            P("dp", None, "tensor"),
            P(("tensor", "dp"), None),
            P("dp", "tensor"),
            P(("tensor", "dp"), None),
            P(),
            P(None, "tensor"),
            P("tensor"),
            P("dp", None, "tensor"),
            P(("tensor", "dp"), None),
            P("dp", "tensor"),
            P(("tensor", "dp"), None),
            P(),
            P(None, "tensor"),
            P("tensor"),
        ),
        check_vma=False,
    )


def solution(mesh):
    def run(*args):
        body = on_device_fused if fused_fits(mesh, args) else on_device
        return mapped(mesh, body)(*args)

    return run
```

```python
import functools
import math

import jax
import jax.numpy as jnp
from jax import lax
from jax.experimental import pallas as pl
from jax.experimental.pallas import tpu as pltpu
from jax.sharding import PartitionSpec as P

HD = 64
ADAM_STEP = 3


NORM_EPS = 1e-05
ADAM_EPS = 1e-08
LEARN_RATE = 0.1
BETA_ONE = 0.9
BETA_TWO = 0.95
DECAY_RATE = 0.1
MASK_FILL = -1e30
GELU_COEF = 0.7978845608028654
CUBIC_COEF = 0.044715


def layer_norm(values, gain, shift):
    center = values - jnp.mean(values, axis=1, keepdims=True)
    inverse = lax.rsqrt(jnp.mean(center * center, axis=1, keepdims=True) + NORM_EPS)
    normed = center * inverse
    return (normed * gain + shift, normed, inverse)


def norm_backward(upstream, normed, inverse, gain):
    scaled = upstream * gain
    inner = (
        scaled
        - jnp.mean(scaled, axis=1, keepdims=True)
        - normed * jnp.mean(scaled * normed, axis=1, keepdims=True)
    )
    return (inverse * inner, jnp.sum(upstream * normed, axis=0), jnp.sum(upstream, axis=0))


def gelu_value(values):
    inner = GELU_COEF * (values + CUBIC_COEF * values * values * values)
    return 0.5 * values * (1.0 + jnp.tanh(inner))


def gelu_slope(values):
    tangent = jnp.tanh(GELU_COEF * (values + CUBIC_COEF * values * values * values))
    return 0.5 * (1.0 + tangent) + 0.5 * values * (1.0 - tangent * tangent) * GELU_COEF * (
        1.0 + 3.0 * CUBIC_COEF * values * values
    )


MESH_ID = pl.DeviceIdType.MESH


def ring_position(index, count):
    odd = lax.rem(index, 2)
    return (1 - odd) * lax.div(index, 2) + odd * (count - 1 - lax.div(index, 2))


def ring_index(position, count):
    place = lax.rem(position + 2 * count, count)
    back = lax.div(place, count // 2)
    return (1 - back) * 2 * place + back * (2 * (count - 1 - place) + 1)


def greet(peers):
    barrier = pltpu.get_barrier_semaphore()
    for peer in peers:
        pl.semaphore_signal(barrier, inc=1, device_id=peer, device_id_type=MESH_ID)
    pl.semaphore_wait(barrier, len(peers))


def ring_peers(count):
    place = ring_position(lax.axis_index("dp"), count)
    return [{"dp": ring_index(place + 1, count)}, {"dp": ring_index(place - 1, count)}]


def flip_bit(index, bit):
    weight = 1 << bit
    return index + weight * (1 - 2 * lax.rem(lax.div(index, weight), 2))


def cube_peers(count):
    index = lax.axis_index("tensor")
    return [{"tensor": flip_bit(index, bit)} for bit in range(count.bit_length() - 1)]


def pieces_of(columns):
    for pieces in (3, 2):
        if columns % (pieces * 128) == 0 and columns // pieces <= 384:
            return pieces
    return 1


class Ring:
    def __init__(self, count, columns):
        self.count = count
        self.index = lax.axis_index("dp")
        self.place = ring_position(self.index, count)
        self.peers = ring_peers(count)
        self.pieces = pieces_of(columns)
        self.width = columns // self.pieces

    def span(self, piece):
        return pl.ds(piece * self.width, self.width)

    def hops(self, way, array):
        return self.count // 2 if way == array else self.count - 1 - self.count // 2

    def at(self, distance, way):
        return ring_index(self.place + (1 - 2 * way) * distance + self.count, self.count)

    def each(self, step):
        return [
            (way, array, piece)
            for piece in range(self.pieces)
            for array in range(2)
            for way in range(2)
            if step < self.hops(way, array)
        ]

    def all(self):
        return [(step, *key) for step in range(self.count // 2) for key in self.each(step)]

    def start(self):
        for key in self.each(0):
            self.copy(0, *key).start()

    def drain(self):
        for key in self.all():
            self.copy(*key).wait_send()


class RingGather(Ring):
    def __init__(self, count, sources, results, sends, receives):
        super().__init__(count, sources[0].shape[-1])
        self.sources, self.results = sources, results
        self.sends, self.receives = sends, receives

    def copy(self, step, way, array, piece):
        target = self.results[array].at[self.at(-step, way), :, self.span(piece)]
        return pltpu.make_async_remote_copy(
            src_ref=self.sources[array].at[:, self.span(piece)] if step == 0 else target,
            dst_ref=target,
            send_sem=self.sends.at[way, array, step, piece],
            recv_sem=self.receives.at[way, array, step, piece],
            device_id=self.peers[way],
            device_id_type=MESH_ID,
        )

    def own(self):
        for array in range(2):
            self.results[array][self.index] = self.sources[array][...]

    def steps(self):
        for step in range(1, self.count // 2):
            for key in self.each(step):
                self.copy(step - 1, *key).wait_recv()
                self.copy(step, *key).start()

    def finish(self):
        for way in range(2):
            for array in range(2):
                for piece in range(self.pieces):
                    self.copy(self.hops(way, array) - 1, way, array, piece).wait_recv()
        self.drain()


class RingReduce(Ring):
    def __init__(self, count, sources, slots, results, sends, receives):
        super().__init__(count, sources[0].shape[-1])
        self.sources, self.slots, self.results = sources, slots, results
        self.sends, self.receives = sends, receives

    def block(self, step, way, array):
        return self.at(self.hops(way, array) - step, way)

    def copy(self, step, way, array, piece):
        span = self.span(piece)
        if step == 0:
            source = self.sources[array].at[self.block(0, way, array), :, span]
        else:
            source = self.slots[array].at[way, step - 1, :, span]
        return pltpu.make_async_remote_copy(
            src_ref=source,
            dst_ref=self.slots[array].at[way, step, :, span],
            send_sem=self.sends.at[way, array, step, piece],
            recv_sem=self.receives.at[way, array, step, piece],
            device_id=self.peers[way],
            device_id_type=MESH_ID,
        )

    def steps(self):
        for step in range(1, self.count // 2):
            for way, array, piece in self.each(step):
                self.copy(step - 1, way, array, piece).wait_recv()
                span = self.span(piece)
                own = self.sources[array][self.block(step, way, array), :, span]
                arrived = self.slots[array][way, step - 1, :, span]
                self.slots[array][way, step - 1, :, span] = (
                    arrived.astype(jnp.float32) + own.astype(jnp.float32)
                ).astype(jnp.bfloat16)
                self.copy(step, way, array, piece).start()

    def finish(self):
        for array in range(2):
            for piece in range(self.pieces):
                span = self.span(piece)
                total = self.sources[array][self.index, :, span].astype(jnp.float32)
                for way in range(2):
                    last = self.hops(way, array) - 1
                    self.copy(last, way, array, piece).wait_recv()
                    total = total + self.slots[array][way, last, :, span].astype(jnp.float32)
                self.results[array][:, span] = total
        self.drain()


class CubeSum:
    def __init__(self, count, source, result, arrivals, sums, sends, receives):
        self.bits = count.bit_length() - 1
        self.source, self.result, self.arrivals, self.sums = source, result, arrivals, sums
        self.sends, self.receives = sends, receives
        self.peers = cube_peers(count)
        self.side = lax.rem(lax.axis_index("tensor"), 2)
        self.chunks, self.rows = arrivals.shape[1], arrivals.shape[2]
        self.half = self.chunks * self.rows

    def mine(self, chunk, side):
        return pl.ds(pl.multiple_of(side * self.half + chunk * self.rows, self.rows), self.rows)

    def copy(self, stage, chunk):
        if stage == 0:
            source = self.source.at[self.mine(chunk, 1 - self.side)]
            target = self.arrivals.at[0, chunk]
        elif stage < self.bits:
            source, target = self.sums.at[stage - 1, chunk], self.arrivals.at[stage, chunk]
        else:
            source = self.result.at[self.mine(chunk, self.side)]
            target = source
        return pltpu.make_async_remote_copy(
            src_ref=source,
            dst_ref=target,
            send_sem=self.sends.at[stage, chunk],
            recv_sem=self.receives.at[stage, chunk],
            device_id=self.peers[stage % self.bits],
            device_id_type=MESH_ID,
        )

    def start(self):
        for chunk in range(self.chunks):
            self.copy(0, chunk).start()

    def add(self, stage):
        for chunk in range(self.chunks):
            self.copy(stage, chunk).wait_recv()
            if stage == 0:
                own = self.source[self.mine(chunk, self.side)]
            else:
                own = self.sums[stage - 1, chunk]
            total = own.astype(jnp.float32) + self.arrivals[stage, chunk].astype(jnp.float32)
            if stage == self.bits - 1:
                self.result[self.mine(chunk, self.side)] = total.astype(jnp.bfloat16)
            else:
                self.sums[stage, chunk] = total.astype(jnp.bfloat16)
            self.copy(stage + 1, chunk).start()

    def last(self):
        for stage in range(1, self.bits):
            self.add(stage)

    def finish(self):
        for chunk in range(self.chunks):
            self.copy(self.bits, chunk).wait_recv()
        for stage in range(self.bits + 1):
            for chunk in range(self.chunks):
                self.copy(stage, chunk).wait_send()


CHUNKS = 4


def cube_scratch(count, rows, columns):
    bits = count.bit_length() - 1
    block = (CHUNKS, rows // 2 // CHUNKS, columns)
    return [
        pltpu.VMEM((bits,) + block, jnp.bfloat16),
        pltpu.VMEM((bits,) + block, jnp.bfloat16),
        pltpu.SemaphoreType.DMA((bits + 1, CHUNKS)),
        pltpu.SemaphoreType.DMA((bits + 1, CHUNKS)),
    ]


def ring_scratch(count, pieces):
    return [
        pltpu.SemaphoreType.DMA((2, 2, count // 2, pieces)),
        pltpu.SemaphoreType.DMA((2, 2, count // 2, pieces)),
    ]


def call_kernel(body, name, number, inputs, outputs, scratch):
    vmem = pl.BlockSpec(memory_space=pltpu.VMEM)
    return pl.pallas_call(
        body,
        name=name,
        out_shape=outputs,
        in_specs=[vmem] * len(inputs),
        out_specs=[vmem] * len(outputs),
        scratch_shapes=scratch,
        compiler_params=pltpu.CompilerParams(collective_id=number, has_side_effects=True),
    )(*inputs)


def gather_pair(number, first, second):
    count = lax.axis_size("dp")

    def body(a_ref, b_ref, c_ref, d_ref, sends, receives):
        greet(ring_peers(count))
        ring = RingGather(count, (a_ref, b_ref), (c_ref, d_ref), sends, receives)
        ring.start()
        ring.own()
        ring.steps()
        ring.finish()

    outputs = [jax.ShapeDtypeStruct((count,) + x.shape, x.dtype) for x in (first, second)]
    scratch = ring_scratch(count, pieces_of(first.shape[-1]))
    return call_kernel(body, "gather_pair", number, (first, second), outputs, scratch)


def sum_and_gather(number, part, first, second):
    count, wide = lax.axis_size("dp"), lax.axis_size("tensor")

    def body(x_ref, a_ref, b_ref, y_ref, c_ref, d_ref, sends, receives, *cube):
        greet(ring_peers(count) + cube_peers(wide))
        ring = RingGather(count, (a_ref, b_ref), (c_ref, d_ref), sends, receives)
        adder = CubeSum(wide, x_ref, y_ref, *cube)
        adder.start()
        ring.start()
        ring.own()
        adder.add(0)
        ring.steps()
        adder.last()
        adder.finish()
        ring.finish()

    outputs = [jax.ShapeDtypeStruct(part.shape, part.dtype)] + [
        jax.ShapeDtypeStruct((count,) + x.shape, x.dtype) for x in (first, second)
    ]
    scratch = ring_scratch(count, pieces_of(first.shape[-1])) + cube_scratch(wide, *part.shape)
    return call_kernel(body, "sum_and_gather", number, (part, first, second), outputs, scratch)


def sum_and_reduce(number, parts, first, second):
    count, wide, several = lax.axis_size("dp"), lax.axis_size("tensor"), len(parts)

    def body(*refs):
        x_refs, (a_ref, b_ref), refs = refs[:several], refs[several : several + 2], refs[several + 2 :]
        y_refs, (c_ref, d_ref), refs = refs[:several], refs[several : several + 2], refs[several + 2 :]
        slot_a, slot_b, sends, receives = refs[:4]
        greet(ring_peers(count) + cube_peers(wide))
        ring = RingReduce(
            count, (a_ref, b_ref), (slot_a, slot_b), (c_ref, d_ref), sends, receives
        )
        adders = [
            CubeSum(wide, x_refs[k], y_refs[k], *refs[4 + 4 * k : 8 + 4 * k])
            for k in range(several)
        ]
        for adder in adders:
            adder.start()
        ring.start()
        for adder in adders:
            adder.add(0)
        ring.steps()
        for adder in adders:
            adder.last()
        ring.finish()
        for adder in adders:
            adder.finish()

    outputs = [jax.ShapeDtypeStruct(x.shape, x.dtype) for x in parts] + [
        jax.ShapeDtypeStruct(x.shape[1:], jnp.float32) for x in (first, second)
    ]
    scratch = [
        pltpu.VMEM((2, count // 2) + x.shape[1:], jnp.bfloat16) for x in (first, second)
    ] + ring_scratch(count, pieces_of(first.shape[-1]))
    for part in parts:
        scratch += cube_scratch(wide, *part.shape)
    return call_kernel(
        body, "sum_and_reduce", number, (*parts, first, second), outputs, scratch
    )


def sum_small(number, values):
    count = lax.axis_size("dp")

    def body(x_ref, y_ref, slots, sends, receives):
        index = lax.axis_index("dp")
        peers = [lax.rem(index + step, count) for step in range(1, count)]
        greet([{"dp": peer} for peer in peers])

        def copy(step):
            return pltpu.make_async_remote_copy(
                src_ref=x_ref,
                dst_ref=slots.at[index],
                send_sem=sends.at[step],
                recv_sem=receives.at[step],
                device_id={"dp": peers[step]},
                device_id_type=MESH_ID,
            )

        for step in range(count - 1):
            copy(step).start()
        slots[index] = x_ref[...]
        for step in range(count - 1):
            copy(step).wait_recv()
        total = slots[0]
        for place in range(1, count):
            total = total + slots[place]
        y_ref[...] = total
        for step in range(count - 1):
            copy(step).wait_send()

    return call_kernel(
        body,
        "sum_small",
        number,
        (values,),
        [jax.ShapeDtypeStruct(values.shape, values.dtype)],
        [
            pltpu.VMEM((count,) + values.shape, values.dtype),
            pltpu.SemaphoreType.DMA((count - 1,)),
            pltpu.SemaphoreType.DMA((count - 1,)),
        ],
    )[0]


SEGMENT_LIMIT = 512
ROWS = 256


def row_blocks(length):
    rows = ROWS if length % ROWS == 0 else length
    for begin in range(0, length, rows):
        yield begin, rows, max(0, begin - SEGMENT_LIMIT // rows * rows), begin + rows


def allowed_block(seg_column, seg_row, begin, rows, low, high):
    query_at = begin + lax.broadcasted_iota(jnp.int32, (rows, high - low), 0)
    key_at = low + lax.broadcasted_iota(jnp.int32, (rows, high - low), 1)
    same = seg_column[begin : begin + rows, :] == seg_row[:, low:high]
    return same & (key_at <= query_at)


def contract(left, right, left_axis, right_axis):
    return lax.dot_general(
        left, right, (((left_axis,), (right_axis,)), ((), ())), preferred_element_type=jnp.float32
    )


def attention_forward(seg_column, seg_row, query, keys, values):
    length, group = query.shape
    heads = group // HD

    def body(sc_ref, sr_ref, q_ref, k_ref, v_ref, c_ref, l_ref):
        for begin, rows, low, high in row_blocks(length):
            allowed = allowed_block(sc_ref, sr_ref, begin, rows, low, high)
            for head in range(heads):
                span = slice(head * HD, (head + 1) * HD)
                own = slice(begin, begin + rows)
                scores = contract(q_ref[own, span], k_ref[low:high, span], 1, 1)
                scores = jnp.where(allowed, scores, MASK_FILL)
                largest = jnp.max(scores, axis=1, keepdims=True)
                raised = jnp.exp(scores - largest)
                total = jnp.sum(raised, axis=1, keepdims=True)
                probs = (raised * (1.0 / total)).astype(jnp.bfloat16)
                c_ref[own, span] = contract(probs, v_ref[low:high, span], 1, 0).astype(jnp.bfloat16)
                l_ref[own, head : head + 1] = largest + jnp.log(total)

    vmem = pl.BlockSpec(memory_space=pltpu.VMEM)
    return pl.pallas_call(
        body,
        name="attention_forward",
        out_shape=[
            jax.ShapeDtypeStruct((length, group), jnp.bfloat16),
            jax.ShapeDtypeStruct((length, heads), jnp.float32),
        ],
        in_specs=[vmem] * 5,
        out_specs=[vmem] * 2,
    )(seg_column, seg_row, query, keys, values)


def attention_backward(seg_column, seg_row, query, keys, values, context, logs, upstream, scale):
    length, group = query.shape
    heads = group // HD

    def body(sc_ref, sr_ref, q_ref, k_ref, v_ref, c_ref, l_ref, u_ref, g_ref, b_ref, dk_ref, dv_ref):
        dk_ref[...] = jnp.zeros_like(dk_ref)
        dv_ref[...] = jnp.zeros_like(dv_ref)
        bias = [jnp.zeros((1, HD), jnp.float32) for _ in range(heads)]
        for begin, rows, low, high in row_blocks(length):
            allowed = allowed_block(sc_ref, sr_ref, begin, rows, low, high)
            own = slice(begin, begin + rows)
            for head in range(heads):
                span = slice(head * HD, (head + 1) * HD)
                query_block, upstream_block = q_ref[own, span], u_ref[own, span]
                keys_block = k_ref[low:high, span]
                scores = jnp.where(allowed, contract(query_block, keys_block, 1, 1), MASK_FILL)
                probs = jnp.exp(scores - l_ref[own, head : head + 1])
                grad_probs = contract(upstream_block, v_ref[low:high, span], 1, 1)
                delta = jnp.sum(
                    upstream_block.astype(jnp.float32) * c_ref[own, span].astype(jnp.float32),
                    axis=1,
                    keepdims=True,
                )
                grad_scores = (probs * (grad_probs - delta)).astype(jnp.bfloat16)
                grad_query = contract(grad_scores, keys_block, 1, 0) * scale
                g_ref[own, span] = grad_query.astype(jnp.bfloat16)
                bias[head] = bias[head] + jnp.sum(grad_query, axis=0, keepdims=True)
                dk_ref[head, low:high] += contract(grad_scores, query_block, 0, 0)
                dv_ref[head, low:high] += contract(
                    probs.astype(jnp.bfloat16), upstream_block, 0, 0
                )
        for head in range(heads):
            span = slice(head * HD, (head + 1) * HD)
            b_ref[0:1, span] = bias[head]
            b_ref[1:2, span] = jnp.sum(dv_ref[head], axis=0, keepdims=True)
            g_ref[:, group + head * HD : group + (head + 1) * HD] = dk_ref[head].astype(
                jnp.bfloat16
            )
            g_ref[:, 2 * group + head * HD : 2 * group + (head + 1) * HD] = dv_ref[head].astype(
                jnp.bfloat16
            )

    vmem = pl.BlockSpec(memory_space=pltpu.VMEM)
    return pl.pallas_call(
        body,
        name="attention_backward",
        out_shape=[
            jax.ShapeDtypeStruct((length, 3 * group), jnp.bfloat16),
            jax.ShapeDtypeStruct((2, group), jnp.float32),
        ],
        in_specs=[vmem] * 8,
        out_specs=[vmem] * 2,
        scratch_shapes=[pltpu.VMEM((heads, length, HD), jnp.float32)] * 2,
    )(seg_column, seg_row, query, keys, values, context, logs, upstream)


def adam_update(param, grad, first, second, decay):
    first_new = BETA_ONE * first + (1.0 - BETA_ONE) * grad
    second_new = BETA_TWO * second + (1.0 - BETA_TWO) * grad * grad
    first_hat = first_new / (1.0 - BETA_ONE**ADAM_STEP)
    second_hat = second_new / (1.0 - BETA_TWO**ADAM_STEP)
    param_new = param - LEARN_RATE * (first_hat / (jnp.sqrt(second_hat) + ADAM_EPS) + decay * param)
    return (param_new, first_new, second_new)


def on_device(
    tokens,
    cotangent,
    segments,
    w_qkv,
    w_proj,
    w_fc,
    w_fc2,
    w_vectors,
    w_qvbias,
    w_fcbias,
    m_qkv,
    m_proj,
    m_fc,
    m_fc2,
    m_vectors,
    m_qvbias,
    m_fcbias,
    v_qkv,
    v_proj,
    v_fc,
    v_fc2,
    v_vectors,
    v_qvbias,
    v_fcbias,
):
    bfloat = jnp.bfloat16
    count = lax.axis_size("dp")
    depth, _, group = w_qkv.shape
    width = depth * count
    scale = 1.0 / math.sqrt(HD)
    proj_rows = w_proj.shape[0]
    qkv_bf = w_qkv.astype(bfloat)
    first_pair = jnp.concatenate([qkv_bf[:, 0], qkv_bf[:, 1]], axis=1)
    second_pair = jnp.concatenate(
        [qkv_bf[:, 2], w_proj.astype(bfloat).reshape(depth, proj_rows * width // depth)], axis=1
    )
    pair_full = gather_pair(0, first_pair, second_pair)
    first_full, second_full = (x.reshape(width, x.shape[2]) for x in pair_full)
    qkv_flat = jnp.concatenate([first_full, second_full[:, :group]], axis=1)
    proj_full = second_full[:, group:].reshape(proj_rows * count, width)

    inputs_f = tokens[0].astype(jnp.float32)
    seg_row = segments[0]
    first_in, normed_one, inverse_one = layer_norm(inputs_f, w_vectors[0], w_vectors[1])
    first_bf = first_in.astype(bfloat)
    projected = jnp.dot(first_bf, qkv_flat, preferred_element_type=jnp.float32)
    query = ((projected[:, :group] + w_qvbias[0]) * scale).astype(bfloat)
    keys = projected[:, group : 2 * group].astype(bfloat)
    values = (projected[:, 2 * group :] + w_qvbias[1]).astype(bfloat)
    sides = (seg_row[:, None], seg_row[None, :])
    context_flat, log_total = attention_forward(*sides, query, keys, values)
    attn_part = jnp.dot(context_flat, proj_full, preferred_element_type=jnp.float32)
    attn_sum, fc_full, fc2_full = sum_and_gather(
        1, attn_part.astype(bfloat), w_fc.astype(bfloat), w_fc2.astype(bfloat)
    )
    fc_full = fc_full.reshape(width, w_fc.shape[1])
    fc2_full = fc2_full.reshape(w_fc2.shape[0] * count, width)
    middle = (
        inputs_f
        + attn_sum.astype(jnp.float32)
        + w_vectors[4]
    )
    second_in, normed_two, inverse_two = layer_norm(middle, w_vectors[2], w_vectors[3])
    second_bf = second_in.astype(bfloat)
    hidden_pre = jnp.dot(second_bf, fc_full, preferred_element_type=jnp.float32) + w_fcbias
    hidden_bf = gelu_value(hidden_pre).astype(bfloat)
    mlp_part = jnp.dot(hidden_bf, fc2_full, preferred_element_type=jnp.float32)
    upstream = cotangent[0]
    grad_out = upstream.astype(jnp.float32)
    grad_fc2 = jnp.dot(hidden_bf.T, upstream, preferred_element_type=jnp.float32)
    grad_hidden = jnp.dot(upstream, fc2_full.T, preferred_element_type=jnp.float32) * gelu_slope(
        hidden_pre
    )
    grad_hidden_bf = grad_hidden.astype(bfloat)
    grad_fc = jnp.dot(second_bf.T, grad_hidden_bf, preferred_element_type=jnp.float32)
    grad_fcbias = jnp.sum(grad_hidden, axis=0)
    norm_two_part = jnp.dot(grad_hidden_bf, fc_full.T, preferred_element_type=jnp.float32)
    mlp_sum, norm_two_sum, fc2_summed, fc_summed = sum_and_reduce(
        2,
        (mlp_part.astype(bfloat), norm_two_part.astype(bfloat)),
        grad_fc2.astype(bfloat).reshape(count, w_fc2.shape[0], width),
        grad_fc.astype(bfloat).reshape(count, depth, w_fc.shape[1]),
    )
    output = (middle + mlp_sum.astype(jnp.float32) + w_vectors[5]).astype(bfloat)
    back_two, gain_two, shift_two = norm_backward(
        norm_two_sum.astype(jnp.float32),
        normed_two,
        inverse_two,
        w_vectors[2],
    )
    grad_middle = grad_out + back_two
    grad_middle_bf = grad_middle.astype(bfloat)
    grad_proj = jnp.dot(context_flat.T, grad_middle_bf, preferred_element_type=jnp.float32)
    grad_context = jnp.dot(grad_middle_bf, proj_full.T, preferred_element_type=jnp.float32).astype(
        bfloat
    )
    grad_stack, grad_qvbias = attention_backward(
        *sides, query, keys, values, context_flat, log_total, grad_context, scale
    )
    grad_qkv = jnp.dot(first_bf.T, grad_stack, preferred_element_type=jnp.float32).astype(bfloat)
    norm_one_part = jnp.dot(grad_stack, qkv_flat.T, preferred_element_type=jnp.float32)
    grad_first = grad_qkv[:, : 2 * group].reshape(count, depth, 2 * group)
    grad_second = jnp.concatenate(
        [grad_qkv[:, 2 * group :], grad_proj.astype(bfloat).reshape(width, group)], axis=1
    ).reshape(count, depth, 2 * group)
    norm_one_sum, first_summed, second_summed = sum_and_reduce(
        3, (norm_one_part.astype(bfloat),), grad_first, grad_second
    )
    qkv_summed = jnp.concatenate([first_summed, second_summed[:, :group]], axis=1).reshape(
        depth, 3, group
    )
    proj_summed = second_summed[:, group:].reshape(proj_rows, width)
    back_one, gain_one, shift_one = norm_backward(
        norm_one_sum.astype(jnp.float32),
        normed_one,
        inverse_one,
        w_vectors[0],
    )
    grad_input = (grad_middle + back_one).astype(bfloat)
    grad_vectors = jnp.stack(
        [
            gain_one,
            shift_one,
            gain_two,
            shift_two,
            jnp.sum(grad_middle, axis=0),
            jnp.sum(grad_out, axis=0),
        ]
    )
    small = jnp.concatenate(
        [grad_vectors.reshape(-1), grad_qvbias.reshape(-1), grad_fcbias.reshape(-1)]
    )
    small_size = small.shape[0]
    small_rows = -(-small_size // width)
    small_sum = sum_small(
        4, jnp.pad(small, (0, small_rows * width - small_size)).reshape(small_rows, width)
    ).reshape(-1)
    cut_one = grad_vectors.size
    cut_two = cut_one + grad_qvbias.size
    vectors_summed = small_sum[:cut_one].reshape(grad_vectors.shape)
    qvbias_summed = small_sum[cut_one:cut_two].reshape(grad_qvbias.shape)
    fcbias_summed = small_sum[cut_two:small_size]
    params = (w_qkv, w_proj, w_fc, w_fc2, w_vectors, w_qvbias, w_fcbias)
    gradients = (
        qkv_summed,
        proj_summed,
        fc_summed,
        fc2_summed,
        vectors_summed,
        qvbias_summed,
        fcbias_summed,
    )
    firsts = (m_qkv, m_proj, m_fc, m_fc2, m_vectors, m_qvbias, m_fcbias)
    seconds = (v_qkv, v_proj, v_fc, v_fc2, v_vectors, v_qvbias, v_fcbias)
    decays = (DECAY_RATE, DECAY_RATE, DECAY_RATE, DECAY_RATE, 0.0, 0.0, 0.0)
    updates = [
        adam_update(p, g, m, v, c)
        for p, g, m, v, c in zip(params, gradients, firsts, seconds, decays)
    ]
    return (
        output[None],
        grad_input[None],
        gradients[0],
        gradients[1],
        gradients[2],
        gradients[3],
        gradients[4],
        gradients[5],
        gradients[6],
        updates[0][0],
        updates[1][0],
        updates[2][0],
        updates[3][0],
        updates[4][0],
        updates[5][0],
        updates[6][0],
        updates[0][1],
        updates[1][1],
        updates[2][1],
        updates[3][1],
        updates[4][1],
        updates[5][1],
        updates[6][1],
        updates[0][2],
        updates[1][2],
        updates[2][2],
        updates[3][2],
        updates[4][2],
        updates[5][2],
        updates[6][2],
    )


BLOCK = 256


class Wires:
    def __init__(self, sends, receives):
        self.sends, self.receives, self.made = sends, receives, []

    def copy(self, source, target, peer):
        place = len(self.made)
        made = pltpu.make_async_remote_copy(
            src_ref=source,
            dst_ref=target,
            send_sem=self.sends.at[place],
            recv_sem=self.receives.at[place],
            device_id=peer,
            device_id_type=MESH_ID,
        )
        self.made.append(made)
        return made

    def drain(self):
        for made in self.made:
            made.wait_send()


class Grid:
    def __init__(self):
        self.count = lax.axis_size("dp")
        self.lines = self.count // 2
        self.index = lax.axis_index("dp")
        self.line, self.pair = lax.div(self.index, 2), lax.rem(self.index, 2)
        self.across = {"dp": self.line * 2 + 1 - self.pair}
        tensor = lax.axis_index("tensor")
        self.side = lax.rem(tensor, 2)
        self.core, self.far = {"tensor": flip_bit(tensor, 0)}, {"tensor": flip_bit(tensor, 1)}

    def owner(self, step, pair):
        return lax.rem(self.line + step + 2 * self.lines, self.lines) * 2 + pair

    def along(self, step):
        return {"dp": self.owner(step, self.pair)}

    def peers(self):
        return [self.across, self.core, self.far] + [self.along(s) for s in range(1, self.lines)]


class Gather:
    def __init__(self, grid, wires, full):
        self.grid, self.full, self.depth = grid, full, full.shape[0] // grid.count
        own = self.rows(grid.index)
        self.long = [
            wires.copy(own, own, grid.along(step)) for step in range(1, grid.lines)
        ]
        self.short = [wires.copy(own, own, grid.across)]
        for step in range(1, grid.lines):
            block = self.rows(grid.owner(-step, grid.pair))
            self.short.append(wires.copy(block, block, grid.across))

    def span(self, owner):
        return pl.ds(pl.multiple_of(owner * self.depth, 16), self.depth)

    def rows(self, owner):
        return self.full.at[self.span(owner)]

    def start(self):
        for made in self.long + self.short[:1]:
            made.start()

    def forward(self):
        for step in range(1, self.grid.lines):
            self.long[step - 1].wait_recv()
            self.short[step].start()

    def finish(self):
        for made in self.short:
            made.wait_recv()


class Reduce:
    def __init__(self, grid, wires, source, near, far):
        self.grid, self.source, self.near, self.far = grid, source, near, far
        self.depth = source.shape[0] // grid.count
        self.short = [
            wires.copy(
                self.rows(grid.owner(step, 1 - grid.pair)), near.at[step - 1], grid.across
            )
            for step in range(1, grid.lines + 1)
        ]
        self.long = [
            wires.copy(self.rows(grid.owner(step, grid.pair)), far.at[step - 1], grid.along(step))
            for step in range(1, grid.lines)
        ]

    def span(self, owner):
        return pl.ds(pl.multiple_of(owner * self.depth, 16), self.depth)

    def rows(self, owner):
        return self.source.at[self.span(owner)]

    def start(self):
        for made in self.short:
            made.start()

    def forward(self):
        for step in range(1, self.grid.lines):
            self.short[step - 1].wait_recv()
            span = self.span(self.grid.owner(step, self.grid.pair))
            own, arrived = self.source[span, :], self.near[step - 1]
            self.source[span, :] = (
                own.astype(jnp.float32) + arrived.astype(jnp.float32)
            ).astype(jnp.bfloat16)
            self.long[step - 1].start()

    def finish(self):
        total = self.source[self.span(self.grid.index), :].astype(jnp.float32)
        self.short[-1].wait_recv()
        total = total + self.near[self.grid.lines - 1].astype(jnp.float32)
        for step in range(1, self.grid.lines):
            self.long[step - 1].wait_recv()
            total = total + self.far[step - 1].astype(jnp.float32)
        return total


class Share:
    def __init__(self, grid, wires, part, arrivals, out):
        self.part, self.arrivals, self.out = part, arrivals, out
        self.half, self.side = arrivals.shape[2], grid.side
        blocks = range(arrivals.shape[1])
        self.first = [
            wires.copy(part.at[self.span(b, 1 - grid.side)], arrivals.at[0, b], grid.core)
            for b in blocks
        ]
        self.second = [
            wires.copy(part.at[self.mine(b)], arrivals.at[1, b], grid.far) for b in blocks
        ]
        self.third = [
            wires.copy(out.at[self.mine(b)], out.at[self.mine(b)], grid.core) for b in blocks
        ]

    def span(self, block, side):
        begin = block * 2 * self.half + side * self.half
        return pl.ds(pl.multiple_of(begin, self.half), self.half)

    def mine(self, block):
        return self.span(block, self.side)

    def give(self, block, value):
        rows = 2 * self.half
        self.part[block * rows : (block + 1) * rows, :] = value.astype(jnp.bfloat16)
        self.first[block].start()

    def cross(self, block):
        self.first[block].wait_recv()
        span = self.mine(block)
        own, arrived = self.part[span, :], self.arrivals[0, block]
        self.part[span, :] = (own.astype(jnp.float32) + arrived.astype(jnp.float32)).astype(
            jnp.bfloat16
        )
        self.second[block].start()

    def take(self, block):
        self.second[block].wait_recv()
        own, arrived = self.part[self.mine(block), :], self.arrivals[1, block]
        return own.astype(jnp.float32) + arrived.astype(jnp.float32)

    def put(self, block, value):
        self.out[self.mine(block), :] = value.astype(jnp.bfloat16)
        self.third[block].start()

    def close(self, block):
        self.third[block].wait_recv()


def column_sum(values):
    return jnp.sum(values, axis=0, keepdims=True)


def padded_rows(rows):
    return -(-rows // 16) * 16


def fused_body(scale, shapes, *refs):
    length, width, group, hidden, depth, proj_rows = shapes
    (
        x_ref, g_ref, sr_ref, wq_ref, wo_ref, w1_ref, w2_ref, vec_ref, qv_ref, fb_ref,
        out_ref, gt_ref, gq_ref, go_ref, g1_ref, g2_ref, gv_ref, gqv_ref, gfb_ref,
        fq, fo, f1, f2, wo_f, wo, a1, q_s, k_s, v_s, c_s, pr_s, h_s, dh_s, a2, dhb, gw, u_s, dz_s,
        dk_s, dv_s, dp_s, part_a, part_n, part_m, part_i, arr_a, arr_n, arr_m, arr_i,
        sq, so, s1, s2, nq, no, n1, n2, rq, ro, r1, r2, sm_own, sm_core, sm_two, sm_pair, sm_four,
        sm_line, sc_ref, sends, receives,
    ) = refs
    f32, b16 = jnp.float32, jnp.bfloat16
    grid, wires = Grid(), Wires(sends, receives)
    heads, rows = group // HD, BLOCK
    pad = padded_rows(proj_rows)
    blocks = length // rows
    order = list(range(blocks))[::-1]

    gathers = {n: Gather(grid, wires, f) for n, f in (("q", fq), ("o", fo), ("2", f2), ("1", f1))}
    share_a = Share(grid, wires, part_a, arr_a, a2)
    share_n = Share(grid, wires, part_n, arr_n, dhb)
    share_m = Share(grid, wires, part_m, arr_m, out_ref)
    share_i = Share(grid, wires, part_i, arr_i, gt_ref)
    reduce_2, reduce_1 = Reduce(grid, wires, s2, n2, r2), Reduce(grid, wires, s1, n1, r1)
    reduce_q, reduce_o = Reduce(grid, wires, sq, nq, rq), Reduce(grid, wires, so, no, ro)
    small_core = wires.copy(sm_own, sm_core, grid.core)
    small_pair = wires.copy(sm_two, sm_pair, grid.across)
    small_line = [
        wires.copy(sm_four, sm_line.at[s - 1], grid.along(s)) for s in range(1, grid.lines)
    ]

    def block_rows(b):
        return slice(b * rows, (b + 1) * rows)

    barrier = pltpu.get_barrier_semaphore()
    peers = grid.peers()
    for peer in peers:
        pl.semaphore_signal(barrier, inc=1, device_id=peer, device_id_type=MESH_ID)
    own_rows = gathers["q"].span(grid.index)
    for j in range(3):
        fq[own_rows, j * group : (j + 1) * group] = wq_ref[j].astype(b16)
    own_proj = wo_ref[...]
    if pad > proj_rows:
        own_proj = jnp.concatenate([own_proj, jnp.zeros((pad - proj_rows, width), f32)], axis=0)
    fo[gathers["o"].span(grid.index), :] = own_proj.astype(b16)
    f2[gathers["2"].span(grid.index), :] = w2_ref[...].astype(b16)
    f1[gathers["1"].span(grid.index), :] = w1_ref[...].astype(b16)
    pl.semaphore_wait(barrier, len(peers))
    gathers["q"].start()
    gathers["o"].start()

    for b in order:
        first_in, _, _ = layer_norm(x_ref[block_rows(b), :].astype(f32), vec_ref[0:1], vec_ref[1:2])
        a1[block_rows(b), :] = first_in.astype(b16)
    dk_s[...] = jnp.zeros_like(dk_s)
    dv_s[...] = jnp.zeros_like(dv_s)
    for b in order:
        wide_row = jnp.broadcast_to(sr_ref[:, block_rows(b)], (8, rows)).astype(f32)
        sc_ref[block_rows(b), :] = jnp.transpose(wide_row)[:, :1].astype(jnp.int32)
    sum_g = jnp.zeros((1, width), f32)
    for b in order:
        sum_g = sum_g + column_sum(g_ref[share_a.mine(b), :].astype(f32))
    sm_own[5:6, :] = sum_g

    gathers["q"].forward()
    gathers["o"].forward()
    gathers["2"].start()
    gathers["1"].start()
    gathers["q"].finish()
    for b in order:
        projected = jnp.dot(a1[block_rows(b), :], fq[...], preferred_element_type=f32)
        q_s[block_rows(b), :] = ((projected[:, :group] + qv_ref[0:1]) * scale).astype(b16)
        k_s[block_rows(b), :] = projected[:, group : 2 * group].astype(b16)
        v_s[block_rows(b), :] = (projected[:, 2 * group :] + qv_ref[1:2]).astype(b16)
    gathers["o"].finish()
    for i in range(grid.count):
        block = fo[i * pad : (i + 1) * pad, :].astype(f32)
        wo_f[i * proj_rows : (i + 1) * proj_rows, :] = block[:proj_rows]
    wo[...] = wo_f[...].astype(b16)

    def window(b):
        return max(0, b * rows - -(-SEGMENT_LIMIT // rows) * rows), (b + 1) * rows

    def attend(b):
        low, high = window(b)
        allowed = allowed_block(sc_ref, sr_ref, b * rows, rows, low, high)
        bias = jnp.where(allowed, 0.0, MASK_FILL)
        for head in range(heads):
            span = slice(head * HD, (head + 1) * HD)
            scores = contract(q_s[block_rows(b), span], k_s[low:high, span], 1, 1) + bias
            largest = jnp.max(scores, axis=1, keepdims=True)
            raised = jnp.exp(scores - largest)
            total = jnp.sum(raised, axis=1, keepdims=True)
            probs = (raised * (1.0 / total)).astype(b16)
            pr_s[b, head, :, : high - low] = probs
            c_s[block_rows(b), span] = contract(probs, v_s[low:high, span], 1, 0).astype(b16)

    for i, b in enumerate(order):
        attend(b)
        share_a.give(b, jnp.dot(c_s[block_rows(b), :], wo[...], preferred_element_type=f32))
        if i >= 1:
            share_a.cross(order[i - 1])
        if i == blocks - 2:
            gathers["2"].forward()
    share_a.cross(order[-1])
    gathers["1"].forward()

    gathers["2"].finish()
    for b in order:
        total = share_a.take(b)
        middle = x_ref[share_a.mine(b), :].astype(f32) + total + vec_ref[4:5]
        h_s[b] = middle
        second_in, _, _ = layer_norm(middle, vec_ref[2:3], vec_ref[3:4])
        share_a.put(b, second_in)
        gw[block_rows(b), :] = contract(g_ref[block_rows(b), :], f2[...], 1, 1)
    gathers["1"].finish()

    tile = 256 if hidden % 256 == 0 else hidden
    sum_fb = [jnp.zeros((1, tile), f32) for _ in range(hidden // tile)]
    sums = {"gain2": jnp.zeros((1, width), f32), "shift2": jnp.zeros((1, width), f32)}
    sums["mid"] = jnp.zeros((1, width), f32)

    def take_n(b):
        upstream = share_n.take(b)
        _, normed, inverse = layer_norm(h_s[b], vec_ref[2:3], vec_ref[3:4])
        back, _, _ = norm_backward(upstream, normed, inverse, vec_ref[2:3])
        sums["gain2"] = sums["gain2"] + column_sum(upstream * normed)
        sums["shift2"] = sums["shift2"] + column_sum(upstream)
        grad_middle = g_ref[share_n.mine(b), :].astype(f32) + back
        sums["mid"] = sums["mid"] + column_sum(grad_middle)
        dh_s[b] = grad_middle
        share_n.put(b, grad_middle)

    for i, b in enumerate(order):
        share_a.close(b)
        for c in range(hidden // tile):
            span = slice(c * tile, (c + 1) * tile)
            z = jnp.dot(a2[block_rows(b), :], f1[:, span], preferred_element_type=f32)
            z = z + fb_ref[span].reshape(1, tile)
            square = z * z
            tangent = jnp.tanh(GELU_COEF * z * (1.0 + CUBIC_COEF * square))
            half = 0.5 * (1.0 + tangent)
            u_s[block_rows(b), span] = (z * half).astype(b16)
            slope = half + 0.5 * z * (1.0 - tangent * tangent) * GELU_COEF * (
                1.0 + 3.0 * CUBIC_COEF * square
            )
            dz = gw[block_rows(b), span] * slope
            sum_fb[c] = sum_fb[c] + column_sum(dz)
            dz_s[block_rows(b), span] = dz.astype(b16)
        share_n.give(b, contract(dz_s[block_rows(b), :], f1[...], 1, 1))
        share_m.give(b, jnp.dot(u_s[block_rows(b), :], f2[...], preferred_element_type=f32))
        share_n.cross(b)
        if i >= 1:
            take_n(order[i - 1])
    for c in range(hidden // tile):
        sm_own[6:7, c * tile : (c + 1) * tile] = sum_fb[c]

    def outer(target, left, right):
        for begin in range(0, target.shape[0], BLOCK):
            target[begin : begin + BLOCK, :] = contract(
                left[:, begin : begin + BLOCK], right[...], 0, 0
            ).astype(b16)

    outer(s2, u_s, g_ref)
    reduce_2.start()
    take_n(order[-1])
    outer(s1, a2, dz_s)
    reduce_1.start()
    for name, row in (("gain2", 2), ("shift2", 3), ("mid", 4)):
        sm_own[row : row + 1, :] = sums[name]
    for b in order[: blocks // 2]:
        share_m.cross(b)

    bias_q = [jnp.zeros((1, HD), f32) for _ in range(heads)]
    bias_v = [jnp.zeros((1, HD), f32) for _ in range(heads)]

    def attend_back(b):
        low, high = window(b)
        grad_context = contract(dhb[block_rows(b), :], wo[...], 1, 1).astype(b16)
        for head in range(heads):
            span = slice(head * HD, (head + 1) * HD)
            upstream = grad_context[:, span]
            probs = pr_s[b, head, :, : high - low]
            keys_block = k_s[low:high, span]
            grad_probs = contract(upstream, v_s[low:high, span], 1, 1)
            delta = jnp.sum(
                upstream.astype(f32) * c_s[block_rows(b), span].astype(f32), axis=1, keepdims=True
            )
            grad_scores = (probs.astype(f32) * (grad_probs - delta)).astype(b16)
            grad_query = contract(grad_scores, keys_block, 1, 0) * scale
            dp_s[block_rows(b), span] = grad_query.astype(b16)
            bias_q[head] = bias_q[head] + column_sum(grad_query)
            dk_s[head, low:high] += contract(grad_scores, q_s[block_rows(b), span], 0, 0)
            dv_s[head, low:high] += contract(probs, upstream, 0, 0)
        for head in range(heads):
            begin = group + head * HD
            dp_s[block_rows(b), begin : begin + HD] = dk_s[head, block_rows(b)].astype(b16)
            grad_value = dv_s[head, block_rows(b)]
            bias_v[head] = bias_v[head] + column_sum(grad_value)
            dp_s[block_rows(b), begin + group : begin + group + HD] = grad_value.astype(b16)

    for i, b in enumerate(order):
        share_n.close(b)
        attend_back(b)
        share_i.give(b, contract(dp_s[block_rows(b), :], fq[...], 1, 1))
        if i >= 1:
            share_i.cross(order[i - 1])
        if i == 0:
            reduce_2.forward()
        if i == min(2, blocks - 1):
            reduce_1.forward()
    share_i.cross(order[-1])
    for b in order[blocks // 2 :]:
        share_m.cross(b)
    sm_own[7:8, :] = jnp.zeros((1, width), f32)
    for head in range(heads):
        sm_own[7:8, head * HD : (head + 1) * HD] = bias_q[head]
        sm_own[7:8, group + head * HD : group + (head + 1) * HD] = bias_v[head]

    outer(sq, a1, dp_s)
    reduce_q.start()
    grad_proj = contract(c_s[...], dhb[...], 0, 0)
    for i in range(grid.count):
        block = grad_proj[i * proj_rows : (i + 1) * proj_rows]
        if pad > proj_rows:
            block = jnp.concatenate([block, jnp.zeros((pad - proj_rows, width), f32)], axis=0)
        so[i * pad : (i + 1) * pad, :] = block.astype(b16)
    reduce_o.start()

    gain, shift = jnp.zeros((1, width), f32), jnp.zeros((1, width), f32)
    for i, b in enumerate(order):
        upstream = share_i.take(b)
        _, normed, inverse = layer_norm(
            x_ref[share_i.mine(b), :].astype(f32), vec_ref[0:1], vec_ref[1:2]
        )
        back, _, _ = norm_backward(upstream, normed, inverse, vec_ref[0:1])
        gain = gain + column_sum(upstream * normed)
        shift = shift + column_sum(upstream)
        share_i.put(b, dh_s[b] + back)
        if i == 0:
            reduce_q.forward()
            reduce_o.forward()
    sm_own[0:1, :] = gain
    sm_own[1:2, :] = shift
    small_core.start()

    def take_m(b):
        share_m.put(b, h_s[b] + share_m.take(b) + vec_ref[5:6])

    for b in order[: blocks // 2]:
        take_m(b)
    g2_ref[...] = reduce_2.finish()
    small_core.wait_recv()
    sm_two[0:6, :] = sm_own[0:6, :] + sm_core[0:6, :]
    sm_two[6:8, :] = sm_own[6:8, :]
    small_pair.start()
    g1_ref[...] = reduce_1.finish()
    small_pair.wait_recv()
    sm_four[...] = sm_two[...] + sm_pair[...]
    for made in small_line:
        made.start()
    total_q = reduce_q.finish()
    for j in range(3):
        gq_ref[j] = total_q[:, j * group : (j + 1) * group]
    go_ref[...] = reduce_o.finish()[:proj_rows]
    total = sm_four[...]
    for step, made in enumerate(small_line):
        made.wait_recv()
        total = total + sm_line[step]
    gv_ref[...] = total[0:6]
    gfb_ref[...] = total[6:7].reshape(width)
    gqv_ref[0:1, :] = total[7:8, :group]
    gqv_ref[1:2, :] = total[7:8, group : 2 * group]
    for b in order[blocks // 2 :]:
        take_m(b)
    for b in order:
        share_m.close(b)
        share_i.close(b)
    wires.drain()


def fused_call(x, g, seg, wq, wo, w1, w2, vec, qv, fb):
    f32, b16 = jnp.float32, jnp.bfloat16
    length, width = x.shape
    _, depth, group = wq.shape
    hidden, proj_rows = w1.shape[1], wo.shape[0]
    count, lines, blocks = lax.axis_size("dp"), lax.axis_size("dp") // 2, length // BLOCK
    heads, pad, half = group // HD, padded_rows(proj_rows), BLOCK // 2
    reach = min(length, -(-SEGMENT_LIMIT // BLOCK) * BLOCK + BLOCK)

    def full(*shape):
        return pltpu.VMEM(shape, b16)

    def wide(*shape):
        return pltpu.VMEM(shape, f32)

    scratch = [
        full(width, 3 * group), full(count * pad, width), full(width, hidden), full(hidden, width),
        wide(group, width), full(group, width), full(length, width),
        full(length, group), full(length, group), full(length, group), full(length, group),
        full(blocks, heads, BLOCK, reach),
        wide(blocks, half, width), wide(blocks, half, width),
        full(length, width), full(length, width), wide(length, hidden),
        full(length, hidden), full(length, hidden),
        wide(heads, length, HD), wide(heads, length, HD), full(length, 3 * group),
    ]
    scratch += [full(length, width)] * 4 + [full(2, blocks, half, width)] * 4
    shards = [(depth, 3 * group), (pad, width), (depth, hidden), (w2.shape[0], width)]
    scratch += [full(count * a, b) for a, b in shards]
    scratch += [full(lines, a, b) for a, b in shards]
    scratch += [full(lines - 1, a, b) for a, b in shards]
    scratch += [wide(8, width)] * 5 + [wide(lines - 1, 8, width)]
    copies = 8 * (2 * lines - 1) + 12 * blocks + 2 + lines - 1
    scratch += [pltpu.VMEM((length, 1), jnp.int32)]
    scratch += [pltpu.SemaphoreType.DMA((copies,))] * 2
    outputs = [
        jax.ShapeDtypeStruct(s, t)
        for s, t in (
            (x.shape, b16), (x.shape, b16), (wq.shape, f32), (wo.shape, f32), (w1.shape, f32),
            (w2.shape, f32), (vec.shape, f32), (qv.shape, f32), (fb.shape, f32),
        )
    ]
    vmem = pl.BlockSpec(memory_space=pltpu.VMEM)
    inputs = (x, g, seg, wq, wo, w1, w2, vec, qv, fb)
    shapes = (length, width, group, hidden, depth, proj_rows)
    return pl.pallas_call(
        functools.partial(fused_body, 1.0 / math.sqrt(HD), shapes),
        name="fused_block",
        out_shape=outputs,
        in_specs=[vmem] * len(inputs),
        out_specs=[vmem] * len(outputs),
        scratch_shapes=scratch,
        compiler_params=pltpu.CompilerParams(
            collective_id=5, has_side_effects=True, vmem_limit_bytes=VMEM_BYTES
        ),
    )(*inputs)


VMEM_BYTES = 63 * 1024 * 1024


def adam_body(number, *refs):
    keep = number // 4
    (x_ref, g_ref), sources, refs = refs[:2], refs[2 : 2 + number], refs[2 + number :]
    (y_ref, h_ref), results, sems = refs[:2], refs[2 : 2 + number], refs[2 + number]
    moves = [
        pltpu.make_async_copy(x_ref, y_ref, sems.at[0]),
        pltpu.make_async_copy(g_ref, h_ref, sems.at[1]),
    ]
    for move in moves:
        move.start()
    pieces = [sources[k * keep : (k + 1) * keep] for k in range(4)]
    for k in range(keep):
        param, grad, first, second = (piece[k][...] for piece in pieces)
        decay = DECAY_RATE if k < 4 else 0.0
        new, first_new, second_new = adam_update(param, grad, first, second, decay)
        results[k][...] = grad
        results[keep + k][...] = new
        results[2 * keep + k][...] = first_new
        results[3 * keep + k][...] = second_new
    for move in moves:
        move.wait()


def adam_call(carried, params, gradients, firsts, seconds):
    inputs = (*params, *gradients, *firsts, *seconds)
    vmem, free = pl.BlockSpec(memory_space=pltpu.VMEM), pl.BlockSpec(memory_space=pl.ANY)
    outputs = [jax.ShapeDtypeStruct(p.shape, p.dtype) for p in (*carried, *params * 4)]
    return pl.pallas_call(
        functools.partial(adam_body, len(inputs)),
        name="adam_step",
        out_shape=outputs,
        in_specs=[free] * 2 + [vmem] * len(inputs),
        out_specs=[free] * 2 + [vmem] * (len(outputs) - 2),
        scratch_shapes=[pltpu.SemaphoreType.DMA((2,))],
    )(*carried, *inputs)


def turn(array):
    return jnp.transpose(array, (1, 0, 2))


def on_device_fused(tokens, cotangent, segments, *state):
    params, firsts, seconds = state[:7], state[7:14], state[14:]

    def shaped(group):
        return (turn(group[0]), *group[1:])

    params, firsts, seconds = shaped(params), shaped(firsts), shaped(seconds)
    results = fused_call(tokens[0], cotangent[0], segments, *params)
    updated = adam_call(results[:2], params, results[2:], firsts, seconds)
    restored = [
        (turn(updated[k]), *updated[k + 1 : k + 7])
        for k in range(2, 30, 7)
    ]
    return (updated[0][None], updated[1][None]) + sum(restored, ())


def fused_fits(mesh, args):
    tokens, w_qkv, w_proj, w_fc, w_fc2 = args[0], args[3], args[4], args[5], args[6]
    count, wide = mesh.shape["dp"], mesh.shape["tensor"]
    width, length = tokens.shape[2], tokens.shape[1]
    depth, group, hidden = width // count, w_qkv.shape[2] // wide, w_fc.shape[1] // wide
    proj_rows = w_proj.shape[0] // (wide * count)
    return (
        wide == 4
        and count % 2 == 0
        and count >= 4
        and depth % 16 == 0
        and (w_fc2.shape[0] // (wide * count)) % 16 == 0
        and proj_rows % 8 == 0
        and length % BLOCK == 0
        and width % BLOCK == 0
        and hidden % BLOCK == 0
        and hidden == width
        and 2 * group <= width
    )


def mapped(mesh, body):
    return jax.shard_map(
        body,
        mesh=mesh,
        in_specs=(
            P("dp", None, None),
            P("dp", None, None),
            P("dp", None),
            P("dp", None, "tensor"),
            P(("tensor", "dp"), None),
            P("dp", "tensor"),
            P(("tensor", "dp"), None),
            P(),
            P(None, "tensor"),
            P("tensor"),
            P("dp", None, "tensor"),
            P(("tensor", "dp"), None),
            P("dp", "tensor"),
            P(("tensor", "dp"), None),
            P(),
            P(None, "tensor"),
            P("tensor"),
            P("dp", None, "tensor"),
            P(("tensor", "dp"), None),
            P("dp", "tensor"),
            P(("tensor", "dp"), None),
            P(),
            P(None, "tensor"),
            P("tensor"),
        ),
        out_specs=(
            P("dp", None, None),
            P("dp", None, None),
            P("dp", None, "tensor"),
            P(("tensor", "dp"), None),
            P("dp", "tensor"),
            P(("tensor", "dp"), None),
            P(),
            P(None, "tensor"),
            P("tensor"),
            P("dp", None, "tensor"),
            P(("tensor", "dp"), None),
            P("dp", "tensor"),
            P(("tensor", "dp"), None),
            P(),
            P(None, "tensor"),
            P("tensor"),
            P("dp", None, "tensor"),
            P(("tensor", "dp"), None),
            P("dp", "tensor"),
            P(("tensor", "dp"), None),
            P(),
            P(None, "tensor"),
            P("tensor"),
            P("dp", None, "tensor"),
            P(("tensor", "dp"), None),
            P("dp", "tensor"),
            P(("tensor", "dp"), None),
            P(),
            P(None, "tensor"),
            P("tensor"),
        ),
        check_vma=False,
    )


def solution(mesh):
    def run(*args):
        body = on_device_fused if fused_fits(mesh, args) else on_device
        return mapped(mesh, body)(*args)

    return run
```

```python
import functools
import math

import jax
import jax.numpy as jnp
from jax import lax
from jax.experimental import pallas as pl
from jax.experimental.pallas import tpu as pltpu
from jax.sharding import PartitionSpec as P

HD = 64
ADAM_STEP = 3


NORM_EPS = 1e-05
ADAM_EPS = 1e-08
LEARN_RATE = 0.1
BETA_ONE = 0.9
BETA_TWO = 0.95
DECAY_RATE = 0.1
MASK_FILL = -1e30
GELU_COEF = 0.7978845608028654
CUBIC_COEF = 0.044715


def layer_norm(values, gain, shift):
    center = values - jnp.mean(values, axis=1, keepdims=True)
    inverse = lax.rsqrt(jnp.mean(center * center, axis=1, keepdims=True) + NORM_EPS)
    normed = center * inverse
    return (normed * gain + shift, normed, inverse)


def norm_backward(upstream, normed, inverse, gain):
    scaled = upstream * gain
    inner = (
        scaled
        - jnp.mean(scaled, axis=1, keepdims=True)
        - normed * jnp.mean(scaled * normed, axis=1, keepdims=True)
    )
    return (inverse * inner, jnp.sum(upstream * normed, axis=0), jnp.sum(upstream, axis=0))


def gelu_value(values):
    inner = GELU_COEF * (values + CUBIC_COEF * values * values * values)
    return 0.5 * values * (1.0 + jnp.tanh(inner))


def gelu_slope(values):
    tangent = jnp.tanh(GELU_COEF * (values + CUBIC_COEF * values * values * values))
    return 0.5 * (1.0 + tangent) + 0.5 * values * (1.0 - tangent * tangent) * GELU_COEF * (
        1.0 + 3.0 * CUBIC_COEF * values * values
    )


MESH_ID = pl.DeviceIdType.MESH


def ring_position(index, count):
    odd = lax.rem(index, 2)
    return (1 - odd) * lax.div(index, 2) + odd * (count - 1 - lax.div(index, 2))


def ring_index(position, count):
    place = lax.rem(position + 2 * count, count)
    back = lax.div(place, count // 2)
    return (1 - back) * 2 * place + back * (2 * (count - 1 - place) + 1)


def greet(peers):
    barrier = pltpu.get_barrier_semaphore()
    for peer in peers:
        pl.semaphore_signal(barrier, inc=1, device_id=peer, device_id_type=MESH_ID)
    pl.semaphore_wait(barrier, len(peers))


def ring_peers(count):
    place = ring_position(lax.axis_index("dp"), count)
    return [{"dp": ring_index(place + 1, count)}, {"dp": ring_index(place - 1, count)}]


def flip_bit(index, bit):
    weight = 1 << bit
    return index + weight * (1 - 2 * lax.rem(lax.div(index, weight), 2))


def cube_peers(count):
    index = lax.axis_index("tensor")
    return [{"tensor": flip_bit(index, bit)} for bit in range(count.bit_length() - 1)]


def pieces_of(columns):
    for pieces in (3, 2):
        if columns % (pieces * 128) == 0 and columns // pieces <= 384:
            return pieces
    return 1


class Ring:
    def __init__(self, count, columns):
        self.count = count
        self.index = lax.axis_index("dp")
        self.place = ring_position(self.index, count)
        self.peers = ring_peers(count)
        self.pieces = pieces_of(columns)
        self.width = columns // self.pieces

    def span(self, piece):
        return pl.ds(piece * self.width, self.width)

    def hops(self, way, array):
        return self.count // 2 if way == array else self.count - 1 - self.count // 2

    def at(self, distance, way):
        return ring_index(self.place + (1 - 2 * way) * distance + self.count, self.count)

    def each(self, step):
        return [
            (way, array, piece)
            for piece in range(self.pieces)
            for array in range(2)
            for way in range(2)
            if step < self.hops(way, array)
        ]

    def all(self):
        return [(step, *key) for step in range(self.count // 2) for key in self.each(step)]

    def start(self):
        for key in self.each(0):
            self.copy(0, *key).start()

    def drain(self):
        for key in self.all():
            self.copy(*key).wait_send()


class RingGather(Ring):
    def __init__(self, count, sources, results, sends, receives):
        super().__init__(count, sources[0].shape[-1])
        self.sources, self.results = sources, results
        self.sends, self.receives = sends, receives

    def copy(self, step, way, array, piece):
        target = self.results[array].at[self.at(-step, way), :, self.span(piece)]
        return pltpu.make_async_remote_copy(
            src_ref=self.sources[array].at[:, self.span(piece)] if step == 0 else target,
            dst_ref=target,
            send_sem=self.sends.at[way, array, step, piece],
            recv_sem=self.receives.at[way, array, step, piece],
            device_id=self.peers[way],
            device_id_type=MESH_ID,
        )

    def own(self):
        for array in range(2):
            self.results[array][self.index] = self.sources[array][...]

    def steps(self):
        for step in range(1, self.count // 2):
            for key in self.each(step):
                self.copy(step - 1, *key).wait_recv()
                self.copy(step, *key).start()

    def finish(self):
        for way in range(2):
            for array in range(2):
                for piece in range(self.pieces):
                    self.copy(self.hops(way, array) - 1, way, array, piece).wait_recv()
        self.drain()


class RingReduce(Ring):
    def __init__(self, count, sources, slots, results, sends, receives):
        super().__init__(count, sources[0].shape[-1])
        self.sources, self.slots, self.results = sources, slots, results
        self.sends, self.receives = sends, receives

    def block(self, step, way, array):
        return self.at(self.hops(way, array) - step, way)

    def copy(self, step, way, array, piece):
        span = self.span(piece)
        if step == 0:
            source = self.sources[array].at[self.block(0, way, array), :, span]
        else:
            source = self.slots[array].at[way, step - 1, :, span]
        return pltpu.make_async_remote_copy(
            src_ref=source,
            dst_ref=self.slots[array].at[way, step, :, span],
            send_sem=self.sends.at[way, array, step, piece],
            recv_sem=self.receives.at[way, array, step, piece],
            device_id=self.peers[way],
            device_id_type=MESH_ID,
        )

    def steps(self):
        for step in range(1, self.count // 2):
            for way, array, piece in self.each(step):
                self.copy(step - 1, way, array, piece).wait_recv()
                span = self.span(piece)
                own = self.sources[array][self.block(step, way, array), :, span]
                arrived = self.slots[array][way, step - 1, :, span]
                self.slots[array][way, step - 1, :, span] = (
                    arrived.astype(jnp.float32) + own.astype(jnp.float32)
                ).astype(jnp.bfloat16)
                self.copy(step, way, array, piece).start()

    def finish(self):
        for array in range(2):
            for piece in range(self.pieces):
                span = self.span(piece)
                total = self.sources[array][self.index, :, span].astype(jnp.float32)
                for way in range(2):
                    last = self.hops(way, array) - 1
                    self.copy(last, way, array, piece).wait_recv()
                    total = total + self.slots[array][way, last, :, span].astype(jnp.float32)
                self.results[array][:, span] = total
        self.drain()


class CubeSum:
    def __init__(self, count, source, result, arrivals, sums, sends, receives):
        self.bits = count.bit_length() - 1
        self.source, self.result, self.arrivals, self.sums = source, result, arrivals, sums
        self.sends, self.receives = sends, receives
        self.peers = cube_peers(count)
        self.side = lax.rem(lax.axis_index("tensor"), 2)
        self.chunks, self.rows = arrivals.shape[1], arrivals.shape[2]
        self.half = self.chunks * self.rows

    def mine(self, chunk, side):
        return pl.ds(pl.multiple_of(side * self.half + chunk * self.rows, self.rows), self.rows)

    def copy(self, stage, chunk):
        if stage == 0:
            source = self.source.at[self.mine(chunk, 1 - self.side)]
            target = self.arrivals.at[0, chunk]
        elif stage < self.bits:
            source, target = self.sums.at[stage - 1, chunk], self.arrivals.at[stage, chunk]
        else:
            source = self.result.at[self.mine(chunk, self.side)]
            target = source
        return pltpu.make_async_remote_copy(
            src_ref=source,
            dst_ref=target,
            send_sem=self.sends.at[stage, chunk],
            recv_sem=self.receives.at[stage, chunk],
            device_id=self.peers[stage % self.bits],
            device_id_type=MESH_ID,
        )

    def start(self):
        for chunk in range(self.chunks):
            self.copy(0, chunk).start()

    def add(self, stage):
        for chunk in range(self.chunks):
            self.copy(stage, chunk).wait_recv()
            if stage == 0:
                own = self.source[self.mine(chunk, self.side)]
            else:
                own = self.sums[stage - 1, chunk]
            total = own.astype(jnp.float32) + self.arrivals[stage, chunk].astype(jnp.float32)
            if stage == self.bits - 1:
                self.result[self.mine(chunk, self.side)] = total.astype(jnp.bfloat16)
            else:
                self.sums[stage, chunk] = total.astype(jnp.bfloat16)
            self.copy(stage + 1, chunk).start()

    def last(self):
        for stage in range(1, self.bits):
            self.add(stage)

    def finish(self):
        for chunk in range(self.chunks):
            self.copy(self.bits, chunk).wait_recv()
        for stage in range(self.bits + 1):
            for chunk in range(self.chunks):
                self.copy(stage, chunk).wait_send()


CHUNKS = 4


def cube_scratch(count, rows, columns):
    bits = count.bit_length() - 1
    block = (CHUNKS, rows // 2 // CHUNKS, columns)
    return [
        pltpu.VMEM((bits,) + block, jnp.bfloat16),
        pltpu.VMEM((bits,) + block, jnp.bfloat16),
        pltpu.SemaphoreType.DMA((bits + 1, CHUNKS)),
        pltpu.SemaphoreType.DMA((bits + 1, CHUNKS)),
    ]


def ring_scratch(count, pieces):
    return [
        pltpu.SemaphoreType.DMA((2, 2, count // 2, pieces)),
        pltpu.SemaphoreType.DMA((2, 2, count // 2, pieces)),
    ]


def call_kernel(body, name, number, inputs, outputs, scratch):
    vmem = pl.BlockSpec(memory_space=pltpu.VMEM)
    return pl.pallas_call(
        body,
        name=name,
        out_shape=outputs,
        in_specs=[vmem] * len(inputs),
        out_specs=[vmem] * len(outputs),
        scratch_shapes=scratch,
        compiler_params=pltpu.CompilerParams(collective_id=number, has_side_effects=True),
    )(*inputs)


def gather_pair(number, first, second):
    count = lax.axis_size("dp")

    def body(a_ref, b_ref, c_ref, d_ref, sends, receives):
        greet(ring_peers(count))
        ring = RingGather(count, (a_ref, b_ref), (c_ref, d_ref), sends, receives)
        ring.start()
        ring.own()
        ring.steps()
        ring.finish()

    outputs = [jax.ShapeDtypeStruct((count,) + x.shape, x.dtype) for x in (first, second)]
    scratch = ring_scratch(count, pieces_of(first.shape[-1]))
    return call_kernel(body, "gather_pair", number, (first, second), outputs, scratch)


def sum_and_gather(number, part, first, second):
    count, wide = lax.axis_size("dp"), lax.axis_size("tensor")

    def body(x_ref, a_ref, b_ref, y_ref, c_ref, d_ref, sends, receives, *cube):
        greet(ring_peers(count) + cube_peers(wide))
        ring = RingGather(count, (a_ref, b_ref), (c_ref, d_ref), sends, receives)
        adder = CubeSum(wide, x_ref, y_ref, *cube)
        adder.start()
        ring.start()
        ring.own()
        adder.add(0)
        ring.steps()
        adder.last()
        adder.finish()
        ring.finish()

    outputs = [jax.ShapeDtypeStruct(part.shape, part.dtype)] + [
        jax.ShapeDtypeStruct((count,) + x.shape, x.dtype) for x in (first, second)
    ]
    scratch = ring_scratch(count, pieces_of(first.shape[-1])) + cube_scratch(wide, *part.shape)
    return call_kernel(body, "sum_and_gather", number, (part, first, second), outputs, scratch)


def sum_and_reduce(number, parts, first, second):
    count, wide, several = lax.axis_size("dp"), lax.axis_size("tensor"), len(parts)

    def body(*refs):
        x_refs, (a_ref, b_ref), refs = refs[:several], refs[several : several + 2], refs[several + 2 :]
        y_refs, (c_ref, d_ref), refs = refs[:several], refs[several : several + 2], refs[several + 2 :]
        slot_a, slot_b, sends, receives = refs[:4]
        greet(ring_peers(count) + cube_peers(wide))
        ring = RingReduce(
            count, (a_ref, b_ref), (slot_a, slot_b), (c_ref, d_ref), sends, receives
        )
        adders = [
            CubeSum(wide, x_refs[k], y_refs[k], *refs[4 + 4 * k : 8 + 4 * k])
            for k in range(several)
        ]
        for adder in adders:
            adder.start()
        ring.start()
        for adder in adders:
            adder.add(0)
        ring.steps()
        for adder in adders:
            adder.last()
        ring.finish()
        for adder in adders:
            adder.finish()

    outputs = [jax.ShapeDtypeStruct(x.shape, x.dtype) for x in parts] + [
        jax.ShapeDtypeStruct(x.shape[1:], jnp.float32) for x in (first, second)
    ]
    scratch = [
        pltpu.VMEM((2, count // 2) + x.shape[1:], jnp.bfloat16) for x in (first, second)
    ] + ring_scratch(count, pieces_of(first.shape[-1]))
    for part in parts:
        scratch += cube_scratch(wide, *part.shape)
    return call_kernel(
        body, "sum_and_reduce", number, (*parts, first, second), outputs, scratch
    )


def sum_small(number, values):
    count = lax.axis_size("dp")

    def body(x_ref, y_ref, slots, sends, receives):
        index = lax.axis_index("dp")
        peers = [lax.rem(index + step, count) for step in range(1, count)]
        greet([{"dp": peer} for peer in peers])

        def copy(step):
            return pltpu.make_async_remote_copy(
                src_ref=x_ref,
                dst_ref=slots.at[index],
                send_sem=sends.at[step],
                recv_sem=receives.at[step],
                device_id={"dp": peers[step]},
                device_id_type=MESH_ID,
            )

        for step in range(count - 1):
            copy(step).start()
        slots[index] = x_ref[...]
        for step in range(count - 1):
            copy(step).wait_recv()
        total = slots[0]
        for place in range(1, count):
            total = total + slots[place]
        y_ref[...] = total
        for step in range(count - 1):
            copy(step).wait_send()

    return call_kernel(
        body,
        "sum_small",
        number,
        (values,),
        [jax.ShapeDtypeStruct(values.shape, values.dtype)],
        [
            pltpu.VMEM((count,) + values.shape, values.dtype),
            pltpu.SemaphoreType.DMA((count - 1,)),
            pltpu.SemaphoreType.DMA((count - 1,)),
        ],
    )[0]


SEGMENT_LIMIT = 512
ROWS = 256


def row_blocks(length):
    rows = ROWS if length % ROWS == 0 else length
    for begin in range(0, length, rows):
        yield begin, rows, max(0, begin - SEGMENT_LIMIT // rows * rows), begin + rows


def allowed_block(seg_column, seg_row, begin, rows, low, high):
    query_at = begin + lax.broadcasted_iota(jnp.int32, (rows, high - low), 0)
    key_at = low + lax.broadcasted_iota(jnp.int32, (rows, high - low), 1)
    same = seg_column[begin : begin + rows, :] == seg_row[:, low:high]
    return same & (key_at <= query_at)


def contract(left, right, left_axis, right_axis):
    return lax.dot_general(
        left, right, (((left_axis,), (right_axis,)), ((), ())), preferred_element_type=jnp.float32
    )


def attention_forward(seg_column, seg_row, query, keys, values):
    length, group = query.shape
    heads = group // HD

    def body(sc_ref, sr_ref, q_ref, k_ref, v_ref, c_ref, l_ref):
        for begin, rows, low, high in row_blocks(length):
            allowed = allowed_block(sc_ref, sr_ref, begin, rows, low, high)
            for head in range(heads):
                span = slice(head * HD, (head + 1) * HD)
                own = slice(begin, begin + rows)
                scores = contract(q_ref[own, span], k_ref[low:high, span], 1, 1)
                scores = jnp.where(allowed, scores, MASK_FILL)
                largest = jnp.max(scores, axis=1, keepdims=True)
                raised = jnp.exp(scores - largest)
                total = jnp.sum(raised, axis=1, keepdims=True)
                probs = (raised * (1.0 / total)).astype(jnp.bfloat16)
                c_ref[own, span] = contract(probs, v_ref[low:high, span], 1, 0).astype(jnp.bfloat16)
                l_ref[own, head : head + 1] = largest + jnp.log(total)

    vmem = pl.BlockSpec(memory_space=pltpu.VMEM)
    return pl.pallas_call(
        body,
        name="attention_forward",
        out_shape=[
            jax.ShapeDtypeStruct((length, group), jnp.bfloat16),
            jax.ShapeDtypeStruct((length, heads), jnp.float32),
        ],
        in_specs=[vmem] * 5,
        out_specs=[vmem] * 2,
    )(seg_column, seg_row, query, keys, values)


def attention_backward(seg_column, seg_row, query, keys, values, context, logs, upstream, scale):
    length, group = query.shape
    heads = group // HD

    def body(sc_ref, sr_ref, q_ref, k_ref, v_ref, c_ref, l_ref, u_ref, g_ref, b_ref, dk_ref, dv_ref):
        dk_ref[...] = jnp.zeros_like(dk_ref)
        dv_ref[...] = jnp.zeros_like(dv_ref)
        bias = [jnp.zeros((1, HD), jnp.float32) for _ in range(heads)]
        for begin, rows, low, high in row_blocks(length):
            allowed = allowed_block(sc_ref, sr_ref, begin, rows, low, high)
            own = slice(begin, begin + rows)
            for head in range(heads):
                span = slice(head * HD, (head + 1) * HD)
                query_block, upstream_block = q_ref[own, span], u_ref[own, span]
                keys_block = k_ref[low:high, span]
                scores = jnp.where(allowed, contract(query_block, keys_block, 1, 1), MASK_FILL)
                probs = jnp.exp(scores - l_ref[own, head : head + 1])
                grad_probs = contract(upstream_block, v_ref[low:high, span], 1, 1)
                delta = jnp.sum(
                    upstream_block.astype(jnp.float32) * c_ref[own, span].astype(jnp.float32),
                    axis=1,
                    keepdims=True,
                )
                grad_scores = (probs * (grad_probs - delta)).astype(jnp.bfloat16)
                grad_query = contract(grad_scores, keys_block, 1, 0) * scale
                g_ref[own, span] = grad_query.astype(jnp.bfloat16)
                bias[head] = bias[head] + jnp.sum(grad_query, axis=0, keepdims=True)
                dk_ref[head, low:high] += contract(grad_scores, query_block, 0, 0)
                dv_ref[head, low:high] += contract(
                    probs.astype(jnp.bfloat16), upstream_block, 0, 0
                )
        for head in range(heads):
            span = slice(head * HD, (head + 1) * HD)
            b_ref[0:1, span] = bias[head]
            b_ref[1:2, span] = jnp.sum(dv_ref[head], axis=0, keepdims=True)
            g_ref[:, group + head * HD : group + (head + 1) * HD] = dk_ref[head].astype(
                jnp.bfloat16
            )
            g_ref[:, 2 * group + head * HD : 2 * group + (head + 1) * HD] = dv_ref[head].astype(
                jnp.bfloat16
            )

    vmem = pl.BlockSpec(memory_space=pltpu.VMEM)
    return pl.pallas_call(
        body,
        name="attention_backward",
        out_shape=[
            jax.ShapeDtypeStruct((length, 3 * group), jnp.bfloat16),
            jax.ShapeDtypeStruct((2, group), jnp.float32),
        ],
        in_specs=[vmem] * 8,
        out_specs=[vmem] * 2,
        scratch_shapes=[pltpu.VMEM((heads, length, HD), jnp.float32)] * 2,
    )(seg_column, seg_row, query, keys, values, context, logs, upstream)


def adam_update(param, grad, first, second, decay):
    first_new = BETA_ONE * first + (1.0 - BETA_ONE) * grad
    second_new = BETA_TWO * second + (1.0 - BETA_TWO) * grad * grad
    first_hat = first_new / (1.0 - BETA_ONE**ADAM_STEP)
    second_hat = second_new / (1.0 - BETA_TWO**ADAM_STEP)
    param_new = param - LEARN_RATE * (first_hat / (jnp.sqrt(second_hat) + ADAM_EPS) + decay * param)
    return (param_new, first_new, second_new)


def on_device(
    tokens,
    cotangent,
    segments,
    w_qkv,
    w_proj,
    w_fc,
    w_fc2,
    w_vectors,
    w_qvbias,
    w_fcbias,
    m_qkv,
    m_proj,
    m_fc,
    m_fc2,
    m_vectors,
    m_qvbias,
    m_fcbias,
    v_qkv,
    v_proj,
    v_fc,
    v_fc2,
    v_vectors,
    v_qvbias,
    v_fcbias,
):
    bfloat = jnp.bfloat16
    count = lax.axis_size("dp")
    depth, _, group = w_qkv.shape
    width = depth * count
    scale = 1.0 / math.sqrt(HD)
    proj_rows = w_proj.shape[0]
    qkv_bf = w_qkv.astype(bfloat)
    first_pair = jnp.concatenate([qkv_bf[:, 0], qkv_bf[:, 1]], axis=1)
    second_pair = jnp.concatenate(
        [qkv_bf[:, 2], w_proj.astype(bfloat).reshape(depth, proj_rows * width // depth)], axis=1
    )
    pair_full = gather_pair(0, first_pair, second_pair)
    first_full, second_full = (x.reshape(width, x.shape[2]) for x in pair_full)
    qkv_flat = jnp.concatenate([first_full, second_full[:, :group]], axis=1)
    proj_full = second_full[:, group:].reshape(proj_rows * count, width)

    inputs_f = tokens[0].astype(jnp.float32)
    seg_row = segments[0]
    first_in, normed_one, inverse_one = layer_norm(inputs_f, w_vectors[0], w_vectors[1])
    first_bf = first_in.astype(bfloat)
    projected = jnp.dot(first_bf, qkv_flat, preferred_element_type=jnp.float32)
    query = ((projected[:, :group] + w_qvbias[0]) * scale).astype(bfloat)
    keys = projected[:, group : 2 * group].astype(bfloat)
    values = (projected[:, 2 * group :] + w_qvbias[1]).astype(bfloat)
    sides = (seg_row[:, None], seg_row[None, :])
    context_flat, log_total = attention_forward(*sides, query, keys, values)
    attn_part = jnp.dot(context_flat, proj_full, preferred_element_type=jnp.float32)
    attn_sum, fc_full, fc2_full = sum_and_gather(
        1, attn_part.astype(bfloat), w_fc.astype(bfloat), w_fc2.astype(bfloat)
    )
    fc_full = fc_full.reshape(width, w_fc.shape[1])
    fc2_full = fc2_full.reshape(w_fc2.shape[0] * count, width)
    middle = (
        inputs_f
        + attn_sum.astype(jnp.float32)
        + w_vectors[4]
    )
    second_in, normed_two, inverse_two = layer_norm(middle, w_vectors[2], w_vectors[3])
    second_bf = second_in.astype(bfloat)
    hidden_pre = jnp.dot(second_bf, fc_full, preferred_element_type=jnp.float32) + w_fcbias
    hidden_bf = gelu_value(hidden_pre).astype(bfloat)
    mlp_part = jnp.dot(hidden_bf, fc2_full, preferred_element_type=jnp.float32)
    upstream = cotangent[0]
    grad_out = upstream.astype(jnp.float32)
    grad_fc2 = jnp.dot(hidden_bf.T, upstream, preferred_element_type=jnp.float32)
    grad_hidden = jnp.dot(upstream, fc2_full.T, preferred_element_type=jnp.float32) * gelu_slope(
        hidden_pre
    )
    grad_hidden_bf = grad_hidden.astype(bfloat)
    grad_fc = jnp.dot(second_bf.T, grad_hidden_bf, preferred_element_type=jnp.float32)
    grad_fcbias = jnp.sum(grad_hidden, axis=0)
    norm_two_part = jnp.dot(grad_hidden_bf, fc_full.T, preferred_element_type=jnp.float32)
    mlp_sum, norm_two_sum, fc2_summed, fc_summed = sum_and_reduce(
        2,
        (mlp_part.astype(bfloat), norm_two_part.astype(bfloat)),
        grad_fc2.astype(bfloat).reshape(count, w_fc2.shape[0], width),
        grad_fc.astype(bfloat).reshape(count, depth, w_fc.shape[1]),
    )
    output = (middle + mlp_sum.astype(jnp.float32) + w_vectors[5]).astype(bfloat)
    back_two, gain_two, shift_two = norm_backward(
        norm_two_sum.astype(jnp.float32),
        normed_two,
        inverse_two,
        w_vectors[2],
    )
    grad_middle = grad_out + back_two
    grad_middle_bf = grad_middle.astype(bfloat)
    grad_proj = jnp.dot(context_flat.T, grad_middle_bf, preferred_element_type=jnp.float32)
    grad_context = jnp.dot(grad_middle_bf, proj_full.T, preferred_element_type=jnp.float32).astype(
        bfloat
    )
    grad_stack, grad_qvbias = attention_backward(
        *sides, query, keys, values, context_flat, log_total, grad_context, scale
    )
    grad_qkv = jnp.dot(first_bf.T, grad_stack, preferred_element_type=jnp.float32).astype(bfloat)
    norm_one_part = jnp.dot(grad_stack, qkv_flat.T, preferred_element_type=jnp.float32)
    grad_first = grad_qkv[:, : 2 * group].reshape(count, depth, 2 * group)
    grad_second = jnp.concatenate(
        [grad_qkv[:, 2 * group :], grad_proj.astype(bfloat).reshape(width, group)], axis=1
    ).reshape(count, depth, 2 * group)
    norm_one_sum, first_summed, second_summed = sum_and_reduce(
        3, (norm_one_part.astype(bfloat),), grad_first, grad_second
    )
    qkv_summed = jnp.concatenate([first_summed, second_summed[:, :group]], axis=1).reshape(
        depth, 3, group
    )
    proj_summed = second_summed[:, group:].reshape(proj_rows, width)
    back_one, gain_one, shift_one = norm_backward(
        norm_one_sum.astype(jnp.float32),
        normed_one,
        inverse_one,
        w_vectors[0],
    )
    grad_input = (grad_middle + back_one).astype(bfloat)
    grad_vectors = jnp.stack(
        [
            gain_one,
            shift_one,
            gain_two,
            shift_two,
            jnp.sum(grad_middle, axis=0),
            jnp.sum(grad_out, axis=0),
        ]
    )
    small = jnp.concatenate(
        [grad_vectors.reshape(-1), grad_qvbias.reshape(-1), grad_fcbias.reshape(-1)]
    )
    small_size = small.shape[0]
    small_rows = -(-small_size // width)
    small_sum = sum_small(
        4, jnp.pad(small, (0, small_rows * width - small_size)).reshape(small_rows, width)
    ).reshape(-1)
    cut_one = grad_vectors.size
    cut_two = cut_one + grad_qvbias.size
    vectors_summed = small_sum[:cut_one].reshape(grad_vectors.shape)
    qvbias_summed = small_sum[cut_one:cut_two].reshape(grad_qvbias.shape)
    fcbias_summed = small_sum[cut_two:small_size]
    params = (w_qkv, w_proj, w_fc, w_fc2, w_vectors, w_qvbias, w_fcbias)
    gradients = (
        qkv_summed,
        proj_summed,
        fc_summed,
        fc2_summed,
        vectors_summed,
        qvbias_summed,
        fcbias_summed,
    )
    firsts = (m_qkv, m_proj, m_fc, m_fc2, m_vectors, m_qvbias, m_fcbias)
    seconds = (v_qkv, v_proj, v_fc, v_fc2, v_vectors, v_qvbias, v_fcbias)
    decays = (DECAY_RATE, DECAY_RATE, DECAY_RATE, DECAY_RATE, 0.0, 0.0, 0.0)
    updates = [
        adam_update(p, g, m, v, c)
        for p, g, m, v, c in zip(params, gradients, firsts, seconds, decays)
    ]
    return (
        output[None],
        grad_input[None],
        gradients[0],
        gradients[1],
        gradients[2],
        gradients[3],
        gradients[4],
        gradients[5],
        gradients[6],
        updates[0][0],
        updates[1][0],
        updates[2][0],
        updates[3][0],
        updates[4][0],
        updates[5][0],
        updates[6][0],
        updates[0][1],
        updates[1][1],
        updates[2][1],
        updates[3][1],
        updates[4][1],
        updates[5][1],
        updates[6][1],
        updates[0][2],
        updates[1][2],
        updates[2][2],
        updates[3][2],
        updates[4][2],
        updates[5][2],
        updates[6][2],
    )


BLOCK = 256


class Wires:
    def __init__(self, sends, receives):
        self.sends, self.receives, self.made = sends, receives, []

    def copy(self, source, target, peer):
        place = len(self.made)
        made = pltpu.make_async_remote_copy(
            src_ref=source,
            dst_ref=target,
            send_sem=self.sends.at[place],
            recv_sem=self.receives.at[place],
            device_id=peer,
            device_id_type=MESH_ID,
        )
        self.made.append(made)
        return made

    def drain(self):
        for made in self.made:
            made.wait_send()


class Grid:
    def __init__(self):
        self.count = lax.axis_size("dp")
        self.lines = self.count // 2
        self.index = lax.axis_index("dp")
        self.line, self.pair = lax.div(self.index, 2), lax.rem(self.index, 2)
        self.across = {"dp": self.line * 2 + 1 - self.pair}
        tensor = lax.axis_index("tensor")
        self.side = lax.rem(tensor, 2)
        self.core, self.far = {"tensor": flip_bit(tensor, 0)}, {"tensor": flip_bit(tensor, 1)}

    def owner(self, step, pair):
        return lax.rem(self.line + step + 2 * self.lines, self.lines) * 2 + pair

    def along(self, step):
        return {"dp": self.owner(step, self.pair)}

    def peers(self):
        return [self.across, self.core, self.far] + [self.along(s) for s in range(1, self.lines)]


class Gather:
    def __init__(self, grid, wires, full):
        self.full, self.count = full, grid.count
        self.depth = full.shape[0] // grid.count
        self.half = self.depth // 2
        self.place = ring_position(grid.index, grid.count)
        peers = ring_peers(grid.count)
        self.copies = {}
        for step in range(grid.count // 2):
            for way, array in self.keys(step):
                block = self.rows(self.at(-step, way), array)
                self.copies[step, way, array] = wires.copy(block, block, peers[way])

    def hops(self, way, array):
        return self.count // 2 if way == array else self.count - 1 - self.count // 2

    def keys(self, step):
        return [(w, a) for a in range(2) for w in range(2) if step < self.hops(w, a)]

    def at(self, distance, way):
        return ring_index(self.place + (1 - 2 * way) * distance + self.count, self.count)

    def span(self, owner):
        return pl.ds(pl.multiple_of(owner * self.depth, 16), self.depth)

    def rows(self, owner, array):
        begin = owner * self.depth + array * self.half
        return self.full.at[pl.ds(pl.multiple_of(begin, 16), self.half)]

    def start(self):
        for key in self.keys(0):
            self.copies[0, *key].start()

    def step(self, step):
        for key in self.keys(step):
            self.copies[step - 1, *key].wait_recv()
            self.copies[step, *key].start()

    def finish(self):
        for way in range(2):
            for array in range(2):
                self.copies[self.hops(way, array) - 1, way, array].wait_recv()


class Reduce:
    def __init__(self, grid, wires, source, near, far):
        self.grid, self.source, self.near, self.far = grid, source, near, far
        self.depth = source.shape[0] // grid.count
        self.short = [
            wires.copy(
                self.rows(grid.owner(step, 1 - grid.pair)), near.at[step - 1], grid.across
            )
            for step in range(1, grid.lines + 1)
        ]
        self.long = [
            wires.copy(self.rows(grid.owner(step, grid.pair)), far.at[step - 1], grid.along(step))
            for step in range(1, grid.lines)
        ]

    def span(self, owner):
        return pl.ds(pl.multiple_of(owner * self.depth, 16), self.depth)

    def rows(self, owner):
        return self.source.at[self.span(owner)]

    def start(self):
        for made in self.short:
            made.start()

    def forward(self):
        for step in range(1, self.grid.lines):
            self.short[step - 1].wait_recv()
            span = self.span(self.grid.owner(step, self.grid.pair))
            own, arrived = self.source[span, :], self.near[step - 1]
            self.source[span, :] = (
                own.astype(jnp.float32) + arrived.astype(jnp.float32)
            ).astype(jnp.bfloat16)
            self.long[step - 1].start()

    def finish(self):
        total = self.source[self.span(self.grid.index), :].astype(jnp.float32)
        self.short[-1].wait_recv()
        total = total + self.near[self.grid.lines - 1].astype(jnp.float32)
        for step in range(1, self.grid.lines):
            self.long[step - 1].wait_recv()
            total = total + self.far[step - 1].astype(jnp.float32)
        return total


class Share:
    def __init__(self, grid, wires, part, arrivals, out):
        self.part, self.arrivals, self.out = part, arrivals, out
        self.half, self.side = arrivals.shape[2], grid.side
        blocks = range(arrivals.shape[1])
        self.first = [
            wires.copy(part.at[self.span(b, 1 - grid.side)], arrivals.at[0, b], grid.core)
            for b in blocks
        ]
        self.second = [
            wires.copy(part.at[self.mine(b)], arrivals.at[1, b], grid.far) for b in blocks
        ]
        self.third = [
            wires.copy(out.at[self.mine(b)], out.at[self.mine(b)], grid.core) for b in blocks
        ]

    def span(self, block, side):
        begin = block * 2 * self.half + side * self.half
        return pl.ds(pl.multiple_of(begin, self.half), self.half)

    def mine(self, block):
        return self.span(block, self.side)

    def give(self, block, value):
        rows = 2 * self.half
        self.part[block * rows : (block + 1) * rows, :] = value.astype(jnp.bfloat16)
        self.first[block].start()

    def cross(self, block):
        self.first[block].wait_recv()
        span = self.mine(block)
        own, arrived = self.part[span, :], self.arrivals[0, block]
        self.part[span, :] = (own.astype(jnp.float32) + arrived.astype(jnp.float32)).astype(
            jnp.bfloat16
        )
        self.second[block].start()

    def take(self, block):
        self.second[block].wait_recv()
        own, arrived = self.part[self.mine(block), :], self.arrivals[1, block]
        return own.astype(jnp.float32) + arrived.astype(jnp.float32)

    def put(self, block, value):
        self.out[self.mine(block), :] = value.astype(jnp.bfloat16)
        self.third[block].start()

    def close(self, block):
        self.third[block].wait_recv()


def column_sum(values):
    return jnp.sum(values, axis=0, keepdims=True)


def padded_rows(rows):
    return -(-rows // 32) * 32


def fused_body(scale, shapes, *refs):
    length, width, group, hidden, depth, proj_rows = shapes
    (
        x_ref, g_ref, sr_ref, wq_ref, wo_ref, w1_ref, w2_ref, vec_ref, qv_ref, fb_ref,
        out_ref, gt_ref, gq_ref, go_ref, g1_ref, g2_ref, gv_ref, gqv_ref, gfb_ref,
        fq, fo, f1, f2, wo_f, wo, a1, q_s, k_s, v_s, c_s, pr_s, h_s, dh_s, a2, dhb, gw, u_s, dz_s,
        dk_s, dv_s, dp_s, part_a, part_n, part_m, part_i, arr_a, arr_n, arr_m, arr_i,
        sq, so, s1, s2, nq, no, n1, n2, rq, ro, r1, r2, sm_own, sm_core, sm_two, sm_pair, sm_four,
        sm_line, sc_ref, sends, receives,
    ) = refs
    f32, b16 = jnp.float32, jnp.bfloat16
    grid, wires = Grid(), Wires(sends, receives)
    heads, rows = group // HD, BLOCK
    pad = padded_rows(proj_rows)
    blocks = length // rows
    order = list(range(blocks))[::-1]

    gathers = {n: Gather(grid, wires, f) for n, f in (("q", fq), ("o", fo), ("2", f2), ("1", f1))}
    share_a = Share(grid, wires, part_a, arr_a, a2)
    share_n = Share(grid, wires, part_n, arr_n, dhb)
    share_m = Share(grid, wires, part_m, arr_m, out_ref)
    share_i = Share(grid, wires, part_i, arr_i, gt_ref)
    reduce_2, reduce_1 = Reduce(grid, wires, s2, n2, r2), Reduce(grid, wires, s1, n1, r1)
    reduce_q, reduce_o = Reduce(grid, wires, sq, nq, rq), Reduce(grid, wires, so, no, ro)
    small_core = wires.copy(sm_own, sm_core, grid.core)
    small_pair = wires.copy(sm_two, sm_pair, grid.across)
    small_line = [
        wires.copy(sm_four, sm_line.at[s - 1], grid.along(s)) for s in range(1, grid.lines)
    ]

    def block_rows(b):
        return slice(b * rows, (b + 1) * rows)

    barrier = pltpu.get_barrier_semaphore()
    peers = grid.peers()
    for peer in peers:
        pl.semaphore_signal(barrier, inc=1, device_id=peer, device_id_type=MESH_ID)
    own_rows = gathers["q"].span(grid.index)
    for j in range(3):
        fq[own_rows, j * group : (j + 1) * group] = wq_ref[j].astype(b16)
    own_proj = wo_ref[...]
    if pad > proj_rows:
        own_proj = jnp.concatenate([own_proj, jnp.zeros((pad - proj_rows, width), f32)], axis=0)
    fo[gathers["o"].span(grid.index), :] = own_proj.astype(b16)
    f2[gathers["2"].span(grid.index), :] = w2_ref[...].astype(b16)
    f1[gathers["1"].span(grid.index), :] = w1_ref[...].astype(b16)
    pl.semaphore_wait(barrier, len(peers))
    gathers["q"].start()
    gathers["o"].start()

    for b in order:
        first_in, _, _ = layer_norm(x_ref[block_rows(b), :].astype(f32), vec_ref[0:1], vec_ref[1:2])
        a1[block_rows(b), :] = first_in.astype(b16)
    dk_s[...] = jnp.zeros_like(dk_s)
    dv_s[...] = jnp.zeros_like(dv_s)
    for b in order:
        wide_row = jnp.broadcast_to(sr_ref[:, block_rows(b)], (8, rows)).astype(f32)
        sc_ref[block_rows(b), :] = jnp.transpose(wide_row)[:, :1].astype(jnp.int32)
    sum_g = jnp.zeros((1, width), f32)
    for b in order:
        sum_g = sum_g + column_sum(g_ref[share_a.mine(b), :].astype(f32))
    sm_own[5:6, :] = sum_g

    for step in range(1, grid.count // 2):
        gathers["q"].step(step)
        gathers["o"].step(step)
    gathers["2"].start()
    gathers["1"].start()
    pending = [(name, step) for step in range(1, grid.count // 2) for name in ("2", "1")]

    def poll(times=1):
        for name, step in pending[:times]:
            gathers[name].step(step)
        del pending[:times]

    gathers["q"].finish()
    for b in order:
        projected = jnp.dot(a1[block_rows(b), :], fq[...], preferred_element_type=f32)
        q_s[block_rows(b), :] = ((projected[:, :group] + qv_ref[0:1]) * scale).astype(b16)
        k_s[block_rows(b), :] = projected[:, group : 2 * group].astype(b16)
        v_s[block_rows(b), :] = (projected[:, 2 * group :] + qv_ref[1:2]).astype(b16)
    gathers["o"].finish()
    for i in range(grid.count):
        block = fo[i * pad : (i + 1) * pad, :].astype(f32)
        wo_f[i * proj_rows : (i + 1) * proj_rows, :] = block[:proj_rows]
    wo[...] = wo_f[...].astype(b16)

    def window(b):
        return max(0, b * rows - -(-SEGMENT_LIMIT // rows) * rows), (b + 1) * rows

    def attend(b):
        low, high = window(b)
        allowed = allowed_block(sc_ref, sr_ref, b * rows, rows, low, high)
        bias = jnp.where(allowed, 0.0, MASK_FILL)
        for head in range(heads):
            span = slice(head * HD, (head + 1) * HD)
            scores = contract(q_s[block_rows(b), span], k_s[low:high, span], 1, 1) + bias
            largest = jnp.max(scores, axis=1, keepdims=True)
            raised = jnp.exp(scores - largest)
            total = jnp.sum(raised, axis=1, keepdims=True)
            probs = (raised * (1.0 / total)).astype(b16)
            pr_s[b, head, :, : high - low] = probs
            c_s[block_rows(b), span] = contract(probs, v_s[low:high, span], 1, 0).astype(b16)

    for i, b in enumerate(order):
        attend(b)
        share_a.give(b, jnp.dot(c_s[block_rows(b), :], wo[...], preferred_element_type=f32))
        if i >= 1:
            share_a.cross(order[i - 1])
        poll()
    share_a.cross(order[-1])

    for i, b in enumerate(order):
        if i == blocks - 1:
            poll(len(pending))
            gathers["2"].finish()
            for c in order:
                gw[block_rows(c), :] = contract(g_ref[block_rows(c), :], f2[...], 1, 1)
        total = share_a.take(b)
        middle = x_ref[share_a.mine(b), :].astype(f32) + total + vec_ref[4:5]
        h_s[b] = middle
        second_in, _, _ = layer_norm(middle, vec_ref[2:3], vec_ref[3:4])
        share_a.put(b, second_in)
        poll()
    gathers["1"].finish()

    tile = 256 if hidden % 256 == 0 else hidden
    sum_fb = [jnp.zeros((1, tile), f32) for _ in range(hidden // tile)]
    sums = {"gain2": jnp.zeros((1, width), f32), "shift2": jnp.zeros((1, width), f32)}
    sums["mid"] = jnp.zeros((1, width), f32)

    def take_n(b):
        upstream = share_n.take(b)
        _, normed, inverse = layer_norm(h_s[b], vec_ref[2:3], vec_ref[3:4])
        back, _, _ = norm_backward(upstream, normed, inverse, vec_ref[2:3])
        sums["gain2"] = sums["gain2"] + column_sum(upstream * normed)
        sums["shift2"] = sums["shift2"] + column_sum(upstream)
        grad_middle = g_ref[share_n.mine(b), :].astype(f32) + back
        sums["mid"] = sums["mid"] + column_sum(grad_middle)
        dh_s[b] = grad_middle
        share_n.put(b, grad_middle)

    for i, b in enumerate(order):
        share_a.close(b)
        for c in range(hidden // tile):
            span = slice(c * tile, (c + 1) * tile)
            z = jnp.dot(a2[block_rows(b), :], f1[:, span], preferred_element_type=f32)
            z = z + fb_ref[span].reshape(1, tile)
            square = z * z
            tangent = jnp.tanh(GELU_COEF * z * (1.0 + CUBIC_COEF * square))
            half = 0.5 * (1.0 + tangent)
            u_s[block_rows(b), span] = (z * half).astype(b16)
            slope = half + 0.5 * z * (1.0 - tangent * tangent) * GELU_COEF * (
                1.0 + 3.0 * CUBIC_COEF * square
            )
            dz = gw[block_rows(b), span] * slope
            sum_fb[c] = sum_fb[c] + column_sum(dz)
            dz_s[block_rows(b), span] = dz.astype(b16)
        share_n.give(b, contract(dz_s[block_rows(b), :], f1[...], 1, 1))
        share_m.give(b, jnp.dot(u_s[block_rows(b), :], f2[...], preferred_element_type=f32))
        share_n.cross(b)
        if i >= 1:
            take_n(order[i - 1])
    for c in range(hidden // tile):
        sm_own[6:7, c * tile : (c + 1) * tile] = sum_fb[c]

    def outer(target, left, right):
        for begin in range(0, target.shape[0], BLOCK):
            target[begin : begin + BLOCK, :] = contract(
                left[:, begin : begin + BLOCK], right[...], 0, 0
            ).astype(b16)

    outer(s2, u_s, g_ref)
    reduce_2.start()
    take_n(order[-1])
    outer(s1, a2, dz_s)
    reduce_1.start()
    for name, row in (("gain2", 2), ("shift2", 3), ("mid", 4)):
        sm_own[row : row + 1, :] = sums[name]
    for b in order[: blocks // 2]:
        share_m.cross(b)

    bias_q = [jnp.zeros((1, HD), f32) for _ in range(heads)]
    bias_v = [jnp.zeros((1, HD), f32) for _ in range(heads)]

    def attend_back(b):
        low, high = window(b)
        grad_context = contract(dhb[block_rows(b), :], wo[...], 1, 1).astype(b16)
        for head in range(heads):
            span = slice(head * HD, (head + 1) * HD)
            upstream = grad_context[:, span]
            probs = pr_s[b, head, :, : high - low]
            keys_block = k_s[low:high, span]
            grad_probs = contract(upstream, v_s[low:high, span], 1, 1)
            delta = jnp.sum(
                upstream.astype(f32) * c_s[block_rows(b), span].astype(f32), axis=1, keepdims=True
            )
            grad_scores = (probs.astype(f32) * (grad_probs - delta)).astype(b16)
            grad_query = contract(grad_scores, keys_block, 1, 0) * scale
            dp_s[block_rows(b), span] = grad_query.astype(b16)
            bias_q[head] = bias_q[head] + column_sum(grad_query)
            dk_s[head, low:high] += contract(grad_scores, q_s[block_rows(b), span], 0, 0)
            dv_s[head, low:high] += contract(probs, upstream, 0, 0)
        for head in range(heads):
            begin = group + head * HD
            dp_s[block_rows(b), begin : begin + HD] = dk_s[head, block_rows(b)].astype(b16)
            grad_value = dv_s[head, block_rows(b)]
            bias_v[head] = bias_v[head] + column_sum(grad_value)
            dp_s[block_rows(b), begin + group : begin + group + HD] = grad_value.astype(b16)

    for i, b in enumerate(order):
        share_n.close(b)
        attend_back(b)
        share_i.give(b, contract(dp_s[block_rows(b), :], fq[...], 1, 1))
        if i >= 1:
            share_i.cross(order[i - 1])
        if i == 0:
            reduce_2.forward()
        if i == min(2, blocks - 1):
            reduce_1.forward()
    share_i.cross(order[-1])
    for b in order[blocks // 2 :]:
        share_m.cross(b)
    sm_own[7:8, :] = jnp.zeros((1, width), f32)
    for head in range(heads):
        sm_own[7:8, head * HD : (head + 1) * HD] = bias_q[head]
        sm_own[7:8, group + head * HD : group + (head + 1) * HD] = bias_v[head]

    outer(sq, a1, dp_s)
    reduce_q.start()
    grad_proj = contract(c_s[...], dhb[...], 0, 0)
    for i in range(grid.count):
        block = grad_proj[i * proj_rows : (i + 1) * proj_rows]
        if pad > proj_rows:
            block = jnp.concatenate([block, jnp.zeros((pad - proj_rows, width), f32)], axis=0)
        so[i * pad : (i + 1) * pad, :] = block.astype(b16)
    reduce_o.start()

    gain, shift = jnp.zeros((1, width), f32), jnp.zeros((1, width), f32)
    for i, b in enumerate(order):
        upstream = share_i.take(b)
        _, normed, inverse = layer_norm(
            x_ref[share_i.mine(b), :].astype(f32), vec_ref[0:1], vec_ref[1:2]
        )
        back, _, _ = norm_backward(upstream, normed, inverse, vec_ref[0:1])
        gain = gain + column_sum(upstream * normed)
        shift = shift + column_sum(upstream)
        share_i.put(b, dh_s[b] + back)
        if i == 0:
            reduce_q.forward()
            reduce_o.forward()
    sm_own[0:1, :] = gain
    sm_own[1:2, :] = shift
    small_core.start()

    def take_m(b):
        share_m.put(b, h_s[b] + share_m.take(b) + vec_ref[5:6])

    for b in order[: blocks // 2]:
        take_m(b)
    g2_ref[...] = reduce_2.finish()
    small_core.wait_recv()
    sm_two[0:6, :] = sm_own[0:6, :] + sm_core[0:6, :]
    sm_two[6:8, :] = sm_own[6:8, :]
    small_pair.start()
    g1_ref[...] = reduce_1.finish()
    small_pair.wait_recv()
    sm_four[...] = sm_two[...] + sm_pair[...]
    for made in small_line:
        made.start()
    total_q = reduce_q.finish()
    for j in range(3):
        gq_ref[j] = total_q[:, j * group : (j + 1) * group]
    go_ref[...] = reduce_o.finish()[:proj_rows]
    total = sm_four[...]
    for step, made in enumerate(small_line):
        made.wait_recv()
        total = total + sm_line[step]
    gv_ref[...] = total[0:6]
    gfb_ref[...] = total[6:7].reshape(width)
    gqv_ref[0:1, :] = total[7:8, :group]
    gqv_ref[1:2, :] = total[7:8, group : 2 * group]
    for b in order[blocks // 2 :]:
        take_m(b)
    for b in order:
        share_m.close(b)
        share_i.close(b)
    wires.drain()


def fused_call(x, g, seg, wq, wo, w1, w2, vec, qv, fb):
    f32, b16 = jnp.float32, jnp.bfloat16
    length, width = x.shape
    _, depth, group = wq.shape
    hidden, proj_rows = w1.shape[1], wo.shape[0]
    count, lines, blocks = lax.axis_size("dp"), lax.axis_size("dp") // 2, length // BLOCK
    heads, pad, half = group // HD, padded_rows(proj_rows), BLOCK // 2
    reach = min(length, -(-SEGMENT_LIMIT // BLOCK) * BLOCK + BLOCK)

    def full(*shape):
        return pltpu.VMEM(shape, b16)

    def wide(*shape):
        return pltpu.VMEM(shape, f32)

    scratch = [
        full(width, 3 * group), full(count * pad, width), full(width, hidden), full(hidden, width),
        wide(group, width), full(group, width), full(length, width),
        full(length, group), full(length, group), full(length, group), full(length, group),
        full(blocks, heads, BLOCK, reach),
        wide(blocks, half, width), wide(blocks, half, width),
        full(length, width), full(length, width), wide(length, hidden),
        full(length, hidden), full(length, hidden),
        wide(heads, length, HD), wide(heads, length, HD), full(length, 3 * group),
    ]
    scratch += [full(length, width)] * 4 + [full(2, blocks, half, width)] * 4
    shards = [(depth, 3 * group), (pad, width), (depth, hidden), (w2.shape[0], width)]
    scratch += [full(count * a, b) for a, b in shards]
    scratch += [full(lines, a, b) for a, b in shards]
    scratch += [full(lines - 1, a, b) for a, b in shards]
    scratch += [wide(8, width)] * 5 + [wide(lines - 1, 8, width)]
    copies = 4 * (2 * (count - 1) + 2 * lines - 1) + 12 * blocks + 2 + lines - 1
    scratch += [pltpu.VMEM((length, 1), jnp.int32)]
    scratch += [pltpu.SemaphoreType.DMA((copies,))] * 2
    outputs = [
        jax.ShapeDtypeStruct(s, t)
        for s, t in (
            (x.shape, b16), (x.shape, b16), (wq.shape, f32), (wo.shape, f32), (w1.shape, f32),
            (w2.shape, f32), (vec.shape, f32), (qv.shape, f32), (fb.shape, f32),
        )
    ]
    vmem = pl.BlockSpec(memory_space=pltpu.VMEM)
    inputs = (x, g, seg, wq, wo, w1, w2, vec, qv, fb)
    shapes = (length, width, group, hidden, depth, proj_rows)
    return pl.pallas_call(
        functools.partial(fused_body, 1.0 / math.sqrt(HD), shapes),
        name="fused_block",
        out_shape=outputs,
        in_specs=[vmem] * len(inputs),
        out_specs=[vmem] * len(outputs),
        scratch_shapes=scratch,
        compiler_params=pltpu.CompilerParams(
            collective_id=5, has_side_effects=True, vmem_limit_bytes=VMEM_BYTES
        ),
    )(*inputs)


VMEM_BYTES = 63 * 1024 * 1024


def adam_body(number, *refs):
    keep = number // 4
    (x_ref, g_ref), sources, refs = refs[:2], refs[2 : 2 + number], refs[2 + number :]
    (y_ref, h_ref), results = refs[:2], refs[2:]
    y_ref[...] = x_ref[...]
    h_ref[...] = g_ref[...]
    pieces = [sources[k * keep : (k + 1) * keep] for k in range(4)]
    for k in range(keep):
        param, grad, first, second = (piece[k][...] for piece in pieces)
        decay = DECAY_RATE if k < 4 else 0.0
        new, first_new, second_new = adam_update(param, grad, first, second, decay)
        results[k][...] = grad
        results[keep + k][...] = new
        results[2 * keep + k][...] = first_new
        results[3 * keep + k][...] = second_new


def adam_call(carried, params, gradients, firsts, seconds):
    inputs = (*carried, *params, *gradients, *firsts, *seconds)
    vmem = pl.BlockSpec(memory_space=pltpu.VMEM)
    outputs = [jax.ShapeDtypeStruct(p.shape, p.dtype) for p in (*carried, *params * 4)]
    return pl.pallas_call(
        functools.partial(adam_body, len(inputs) - 2),
        name="adam_step",
        out_shape=outputs,
        in_specs=[vmem] * len(inputs),
        out_specs=[vmem] * len(outputs),
        compiler_params=pltpu.CompilerParams(vmem_limit_bytes=VMEM_BYTES),
    )(*inputs)


def turn(array):
    return jnp.transpose(array, (1, 0, 2))


def on_device_fused(tokens, cotangent, segments, *state):
    params, firsts, seconds = state[:7], state[7:14], state[14:]

    def shaped(group):
        return (turn(group[0]), *group[1:])

    params, firsts, seconds = shaped(params), shaped(firsts), shaped(seconds)
    results = fused_call(tokens[0], cotangent[0], segments, *params)
    updated = adam_call(results[:2], params, results[2:], firsts, seconds)
    restored = [
        (turn(updated[k]), *updated[k + 1 : k + 7])
        for k in range(2, 30, 7)
    ]
    return (updated[0][None], updated[1][None]) + sum(restored, ())


def fused_fits(mesh, args):
    tokens, w_qkv, w_proj, w_fc, w_fc2 = args[0], args[3], args[4], args[5], args[6]
    count, wide = mesh.shape["dp"], mesh.shape["tensor"]
    width, length = tokens.shape[2], tokens.shape[1]
    depth, group, hidden = width // count, w_qkv.shape[2] // wide, w_fc.shape[1] // wide
    proj_rows = w_proj.shape[0] // (wide * count)
    return (
        wide == 4
        and count % 2 == 0
        and count >= 4
        and depth % 32 == 0
        and (w_fc2.shape[0] // (wide * count)) % 32 == 0
        and proj_rows % 8 == 0
        and length % BLOCK == 0
        and width % BLOCK == 0
        and hidden % BLOCK == 0
        and hidden == width
        and 2 * group <= width
    )


def mapped(mesh, body):
    return jax.shard_map(
        body,
        mesh=mesh,
        in_specs=(
            P("dp", None, None),
            P("dp", None, None),
            P("dp", None),
            P("dp", None, "tensor"),
            P(("tensor", "dp"), None),
            P("dp", "tensor"),
            P(("tensor", "dp"), None),
            P(),
            P(None, "tensor"),
            P("tensor"),
            P("dp", None, "tensor"),
            P(("tensor", "dp"), None),
            P("dp", "tensor"),
            P(("tensor", "dp"), None),
            P(),
            P(None, "tensor"),
            P("tensor"),
            P("dp", None, "tensor"),
            P(("tensor", "dp"), None),
            P("dp", "tensor"),
            P(("tensor", "dp"), None),
            P(),
            P(None, "tensor"),
            P("tensor"),
        ),
        out_specs=(
            P("dp", None, None),
            P("dp", None, None),
            P("dp", None, "tensor"),
            P(("tensor", "dp"), None),
            P("dp", "tensor"),
            P(("tensor", "dp"), None),
            P(),
            P(None, "tensor"),
            P("tensor"),
            P("dp", None, "tensor"),
            P(("tensor", "dp"), None),
            P("dp", "tensor"),
            P(("tensor", "dp"), None),
            P(),
            P(None, "tensor"),
            P("tensor"),
            P("dp", None, "tensor"),
            P(("tensor", "dp"), None),
            P("dp", "tensor"),
            P(("tensor", "dp"), None),
            P(),
            P(None, "tensor"),
            P("tensor"),
            P("dp", None, "tensor"),
            P(("tensor", "dp"), None),
            P("dp", "tensor"),
            P(("tensor", "dp"), None),
            P(),
            P(None, "tensor"),
            P("tensor"),
        ),
        check_vma=False,
    )


def solution(mesh):
    def run(*args):
        body = on_device_fused if fused_fits(mesh, args) else on_device
        return mapped(mesh, body)(*args)

    return run
```

```python
import functools
import math

import jax
import jax.numpy as jnp
from jax import lax
from jax.experimental import pallas as pl
from jax.experimental.pallas import tpu as pltpu
from jax.sharding import PartitionSpec as P

HD = 64
ADAM_STEP = 3


NORM_EPS = 1e-05
ADAM_EPS = 1e-08
LEARN_RATE = 0.1
BETA_ONE = 0.9
BETA_TWO = 0.95
DECAY_RATE = 0.1
MASK_FILL = -1e30
GELU_COEF = 0.7978845608028654
CUBIC_COEF = 0.044715


def layer_norm(values, gain, shift):
    center = values - jnp.mean(values, axis=1, keepdims=True)
    inverse = lax.rsqrt(jnp.mean(center * center, axis=1, keepdims=True) + NORM_EPS)
    normed = center * inverse
    return (normed * gain + shift, normed, inverse)


def norm_backward(upstream, normed, inverse, gain):
    scaled = upstream * gain
    inner = (
        scaled
        - jnp.mean(scaled, axis=1, keepdims=True)
        - normed * jnp.mean(scaled * normed, axis=1, keepdims=True)
    )
    return (inverse * inner, jnp.sum(upstream * normed, axis=0), jnp.sum(upstream, axis=0))


def gelu_value(values):
    inner = GELU_COEF * (values + CUBIC_COEF * values * values * values)
    return 0.5 * values * (1.0 + jnp.tanh(inner))


def gelu_slope(values):
    tangent = jnp.tanh(GELU_COEF * (values + CUBIC_COEF * values * values * values))
    return 0.5 * (1.0 + tangent) + 0.5 * values * (1.0 - tangent * tangent) * GELU_COEF * (
        1.0 + 3.0 * CUBIC_COEF * values * values
    )


MESH_ID = pl.DeviceIdType.MESH


def ring_position(index, count):
    odd = lax.rem(index, 2)
    return (1 - odd) * lax.div(index, 2) + odd * (count - 1 - lax.div(index, 2))


def ring_index(position, count):
    place = lax.rem(position + 2 * count, count)
    back = lax.div(place, count // 2)
    return (1 - back) * 2 * place + back * (2 * (count - 1 - place) + 1)


def greet(peers):
    barrier = pltpu.get_barrier_semaphore()
    for peer in peers:
        pl.semaphore_signal(barrier, inc=1, device_id=peer, device_id_type=MESH_ID)
    pl.semaphore_wait(barrier, len(peers))


def ring_peers(count):
    place = ring_position(lax.axis_index("dp"), count)
    return [{"dp": ring_index(place + 1, count)}, {"dp": ring_index(place - 1, count)}]


def flip_bit(index, bit):
    weight = 1 << bit
    return index + weight * (1 - 2 * lax.rem(lax.div(index, weight), 2))


def cube_peers(count):
    index = lax.axis_index("tensor")
    return [{"tensor": flip_bit(index, bit)} for bit in range(count.bit_length() - 1)]


def pieces_of(columns):
    for pieces in (3, 2):
        if columns % (pieces * 128) == 0 and columns // pieces <= 384:
            return pieces
    return 1


class Ring:
    def __init__(self, count, columns):
        self.count = count
        self.index = lax.axis_index("dp")
        self.place = ring_position(self.index, count)
        self.peers = ring_peers(count)
        self.pieces = pieces_of(columns)
        self.width = columns // self.pieces

    def span(self, piece):
        return pl.ds(piece * self.width, self.width)

    def hops(self, way, array):
        return self.count // 2 if way == array else self.count - 1 - self.count // 2

    def at(self, distance, way):
        return ring_index(self.place + (1 - 2 * way) * distance + self.count, self.count)

    def each(self, step):
        return [
            (way, array, piece)
            for piece in range(self.pieces)
            for array in range(2)
            for way in range(2)
            if step < self.hops(way, array)
        ]

    def all(self):
        return [(step, *key) for step in range(self.count // 2) for key in self.each(step)]

    def start(self):
        for key in self.each(0):
            self.copy(0, *key).start()

    def drain(self):
        for key in self.all():
            self.copy(*key).wait_send()


class RingGather(Ring):
    def __init__(self, count, sources, results, sends, receives):
        super().__init__(count, sources[0].shape[-1])
        self.sources, self.results = sources, results
        self.sends, self.receives = sends, receives

    def copy(self, step, way, array, piece):
        target = self.results[array].at[self.at(-step, way), :, self.span(piece)]
        return pltpu.make_async_remote_copy(
            src_ref=self.sources[array].at[:, self.span(piece)] if step == 0 else target,
            dst_ref=target,
            send_sem=self.sends.at[way, array, step, piece],
            recv_sem=self.receives.at[way, array, step, piece],
            device_id=self.peers[way],
            device_id_type=MESH_ID,
        )

    def own(self):
        for array in range(2):
            self.results[array][self.index] = self.sources[array][...]

    def steps(self):
        for step in range(1, self.count // 2):
            for key in self.each(step):
                self.copy(step - 1, *key).wait_recv()
                self.copy(step, *key).start()

    def finish(self):
        for way in range(2):
            for array in range(2):
                for piece in range(self.pieces):
                    self.copy(self.hops(way, array) - 1, way, array, piece).wait_recv()
        self.drain()


class RingReduce(Ring):
    def __init__(self, count, sources, slots, results, sends, receives):
        super().__init__(count, sources[0].shape[-1])
        self.sources, self.slots, self.results = sources, slots, results
        self.sends, self.receives = sends, receives

    def block(self, step, way, array):
        return self.at(self.hops(way, array) - step, way)

    def copy(self, step, way, array, piece):
        span = self.span(piece)
        if step == 0:
            source = self.sources[array].at[self.block(0, way, array), :, span]
        else:
            source = self.slots[array].at[way, step - 1, :, span]
        return pltpu.make_async_remote_copy(
            src_ref=source,
            dst_ref=self.slots[array].at[way, step, :, span],
            send_sem=self.sends.at[way, array, step, piece],
            recv_sem=self.receives.at[way, array, step, piece],
            device_id=self.peers[way],
            device_id_type=MESH_ID,
        )

    def steps(self):
        for step in range(1, self.count // 2):
            for way, array, piece in self.each(step):
                self.copy(step - 1, way, array, piece).wait_recv()
                span = self.span(piece)
                own = self.sources[array][self.block(step, way, array), :, span]
                arrived = self.slots[array][way, step - 1, :, span]
                self.slots[array][way, step - 1, :, span] = (
                    arrived.astype(jnp.float32) + own.astype(jnp.float32)
                ).astype(jnp.bfloat16)
                self.copy(step, way, array, piece).start()

    def finish(self):
        for array in range(2):
            for piece in range(self.pieces):
                span = self.span(piece)
                total = self.sources[array][self.index, :, span].astype(jnp.float32)
                for way in range(2):
                    last = self.hops(way, array) - 1
                    self.copy(last, way, array, piece).wait_recv()
                    total = total + self.slots[array][way, last, :, span].astype(jnp.float32)
                self.results[array][:, span] = total
        self.drain()


class CubeSum:
    def __init__(self, count, source, result, arrivals, sums, sends, receives):
        self.bits = count.bit_length() - 1
        self.source, self.result, self.arrivals, self.sums = source, result, arrivals, sums
        self.sends, self.receives = sends, receives
        self.peers = cube_peers(count)
        self.side = lax.rem(lax.axis_index("tensor"), 2)
        self.chunks, self.rows = arrivals.shape[1], arrivals.shape[2]
        self.half = self.chunks * self.rows

    def mine(self, chunk, side):
        return pl.ds(pl.multiple_of(side * self.half + chunk * self.rows, self.rows), self.rows)

    def copy(self, stage, chunk):
        if stage == 0:
            source = self.source.at[self.mine(chunk, 1 - self.side)]
            target = self.arrivals.at[0, chunk]
        elif stage < self.bits:
            source, target = self.sums.at[stage - 1, chunk], self.arrivals.at[stage, chunk]
        else:
            source = self.result.at[self.mine(chunk, self.side)]
            target = source
        return pltpu.make_async_remote_copy(
            src_ref=source,
            dst_ref=target,
            send_sem=self.sends.at[stage, chunk],
            recv_sem=self.receives.at[stage, chunk],
            device_id=self.peers[stage % self.bits],
            device_id_type=MESH_ID,
        )

    def start(self):
        for chunk in range(self.chunks):
            self.copy(0, chunk).start()

    def add(self, stage):
        for chunk in range(self.chunks):
            self.copy(stage, chunk).wait_recv()
            if stage == 0:
                own = self.source[self.mine(chunk, self.side)]
            else:
                own = self.sums[stage - 1, chunk]
            total = own.astype(jnp.float32) + self.arrivals[stage, chunk].astype(jnp.float32)
            if stage == self.bits - 1:
                self.result[self.mine(chunk, self.side)] = total.astype(jnp.bfloat16)
            else:
                self.sums[stage, chunk] = total.astype(jnp.bfloat16)
            self.copy(stage + 1, chunk).start()

    def last(self):
        for stage in range(1, self.bits):
            self.add(stage)

    def finish(self):
        for chunk in range(self.chunks):
            self.copy(self.bits, chunk).wait_recv()
        for stage in range(self.bits + 1):
            for chunk in range(self.chunks):
                self.copy(stage, chunk).wait_send()


CHUNKS = 4


def cube_scratch(count, rows, columns):
    bits = count.bit_length() - 1
    block = (CHUNKS, rows // 2 // CHUNKS, columns)
    return [
        pltpu.VMEM((bits,) + block, jnp.bfloat16),
        pltpu.VMEM((bits,) + block, jnp.bfloat16),
        pltpu.SemaphoreType.DMA((bits + 1, CHUNKS)),
        pltpu.SemaphoreType.DMA((bits + 1, CHUNKS)),
    ]


def ring_scratch(count, pieces):
    return [
        pltpu.SemaphoreType.DMA((2, 2, count // 2, pieces)),
        pltpu.SemaphoreType.DMA((2, 2, count // 2, pieces)),
    ]


def call_kernel(body, name, number, inputs, outputs, scratch):
    vmem = pl.BlockSpec(memory_space=pltpu.VMEM)
    return pl.pallas_call(
        body,
        name=name,
        out_shape=outputs,
        in_specs=[vmem] * len(inputs),
        out_specs=[vmem] * len(outputs),
        scratch_shapes=scratch,
        compiler_params=pltpu.CompilerParams(collective_id=number, has_side_effects=True),
    )(*inputs)


def gather_pair(number, first, second):
    count = lax.axis_size("dp")

    def body(a_ref, b_ref, c_ref, d_ref, sends, receives):
        greet(ring_peers(count))
        ring = RingGather(count, (a_ref, b_ref), (c_ref, d_ref), sends, receives)
        ring.start()
        ring.own()
        ring.steps()
        ring.finish()

    outputs = [jax.ShapeDtypeStruct((count,) + x.shape, x.dtype) for x in (first, second)]
    scratch = ring_scratch(count, pieces_of(first.shape[-1]))
    return call_kernel(body, "gather_pair", number, (first, second), outputs, scratch)


def sum_and_gather(number, part, first, second):
    count, wide = lax.axis_size("dp"), lax.axis_size("tensor")

    def body(x_ref, a_ref, b_ref, y_ref, c_ref, d_ref, sends, receives, *cube):
        greet(ring_peers(count) + cube_peers(wide))
        ring = RingGather(count, (a_ref, b_ref), (c_ref, d_ref), sends, receives)
        adder = CubeSum(wide, x_ref, y_ref, *cube)
        adder.start()
        ring.start()
        ring.own()
        adder.add(0)
        ring.steps()
        adder.last()
        adder.finish()
        ring.finish()

    outputs = [jax.ShapeDtypeStruct(part.shape, part.dtype)] + [
        jax.ShapeDtypeStruct((count,) + x.shape, x.dtype) for x in (first, second)
    ]
    scratch = ring_scratch(count, pieces_of(first.shape[-1])) + cube_scratch(wide, *part.shape)
    return call_kernel(body, "sum_and_gather", number, (part, first, second), outputs, scratch)


def sum_and_reduce(number, parts, first, second):
    count, wide, several = lax.axis_size("dp"), lax.axis_size("tensor"), len(parts)

    def body(*refs):
        x_refs, (a_ref, b_ref), refs = refs[:several], refs[several : several + 2], refs[several + 2 :]
        y_refs, (c_ref, d_ref), refs = refs[:several], refs[several : several + 2], refs[several + 2 :]
        slot_a, slot_b, sends, receives = refs[:4]
        greet(ring_peers(count) + cube_peers(wide))
        ring = RingReduce(
            count, (a_ref, b_ref), (slot_a, slot_b), (c_ref, d_ref), sends, receives
        )
        adders = [
            CubeSum(wide, x_refs[k], y_refs[k], *refs[4 + 4 * k : 8 + 4 * k])
            for k in range(several)
        ]
        for adder in adders:
            adder.start()
        ring.start()
        for adder in adders:
            adder.add(0)
        ring.steps()
        for adder in adders:
            adder.last()
        ring.finish()
        for adder in adders:
            adder.finish()

    outputs = [jax.ShapeDtypeStruct(x.shape, x.dtype) for x in parts] + [
        jax.ShapeDtypeStruct(x.shape[1:], jnp.float32) for x in (first, second)
    ]
    scratch = [
        pltpu.VMEM((2, count // 2) + x.shape[1:], jnp.bfloat16) for x in (first, second)
    ] + ring_scratch(count, pieces_of(first.shape[-1]))
    for part in parts:
        scratch += cube_scratch(wide, *part.shape)
    return call_kernel(
        body, "sum_and_reduce", number, (*parts, first, second), outputs, scratch
    )


def sum_small(number, values):
    count = lax.axis_size("dp")

    def body(x_ref, y_ref, slots, sends, receives):
        index = lax.axis_index("dp")
        peers = [lax.rem(index + step, count) for step in range(1, count)]
        greet([{"dp": peer} for peer in peers])

        def copy(step):
            return pltpu.make_async_remote_copy(
                src_ref=x_ref,
                dst_ref=slots.at[index],
                send_sem=sends.at[step],
                recv_sem=receives.at[step],
                device_id={"dp": peers[step]},
                device_id_type=MESH_ID,
            )

        for step in range(count - 1):
            copy(step).start()
        slots[index] = x_ref[...]
        for step in range(count - 1):
            copy(step).wait_recv()
        total = slots[0]
        for place in range(1, count):
            total = total + slots[place]
        y_ref[...] = total
        for step in range(count - 1):
            copy(step).wait_send()

    return call_kernel(
        body,
        "sum_small",
        number,
        (values,),
        [jax.ShapeDtypeStruct(values.shape, values.dtype)],
        [
            pltpu.VMEM((count,) + values.shape, values.dtype),
            pltpu.SemaphoreType.DMA((count - 1,)),
            pltpu.SemaphoreType.DMA((count - 1,)),
        ],
    )[0]


SEGMENT_LIMIT = 512
ROWS = 256


def row_blocks(length):
    rows = ROWS if length % ROWS == 0 else length
    for begin in range(0, length, rows):
        yield begin, rows, max(0, begin - SEGMENT_LIMIT // rows * rows), begin + rows


def allowed_block(seg_column, seg_row, begin, rows, low, high):
    query_at = begin + lax.broadcasted_iota(jnp.int32, (rows, high - low), 0)
    key_at = low + lax.broadcasted_iota(jnp.int32, (rows, high - low), 1)
    same = seg_column[begin : begin + rows, :] == seg_row[:, low:high]
    return same & (key_at <= query_at)


def contract(left, right, left_axis, right_axis):
    return lax.dot_general(
        left, right, (((left_axis,), (right_axis,)), ((), ())), preferred_element_type=jnp.float32
    )


def attention_forward(seg_column, seg_row, query, keys, values):
    length, group = query.shape
    heads = group // HD

    def body(sc_ref, sr_ref, q_ref, k_ref, v_ref, c_ref, l_ref):
        for begin, rows, low, high in row_blocks(length):
            allowed = allowed_block(sc_ref, sr_ref, begin, rows, low, high)
            for head in range(heads):
                span = slice(head * HD, (head + 1) * HD)
                own = slice(begin, begin + rows)
                scores = contract(q_ref[own, span], k_ref[low:high, span], 1, 1)
                scores = jnp.where(allowed, scores, MASK_FILL)
                largest = jnp.max(scores, axis=1, keepdims=True)
                raised = jnp.exp(scores - largest)
                total = jnp.sum(raised, axis=1, keepdims=True)
                probs = (raised * (1.0 / total)).astype(jnp.bfloat16)
                c_ref[own, span] = contract(probs, v_ref[low:high, span], 1, 0).astype(jnp.bfloat16)
                l_ref[own, head : head + 1] = largest + jnp.log(total)

    vmem = pl.BlockSpec(memory_space=pltpu.VMEM)
    return pl.pallas_call(
        body,
        name="attention_forward",
        out_shape=[
            jax.ShapeDtypeStruct((length, group), jnp.bfloat16),
            jax.ShapeDtypeStruct((length, heads), jnp.float32),
        ],
        in_specs=[vmem] * 5,
        out_specs=[vmem] * 2,
    )(seg_column, seg_row, query, keys, values)


def attention_backward(seg_column, seg_row, query, keys, values, context, logs, upstream, scale):
    length, group = query.shape
    heads = group // HD

    def body(sc_ref, sr_ref, q_ref, k_ref, v_ref, c_ref, l_ref, u_ref, g_ref, b_ref, dk_ref, dv_ref):
        dk_ref[...] = jnp.zeros_like(dk_ref)
        dv_ref[...] = jnp.zeros_like(dv_ref)
        bias = [jnp.zeros((1, HD), jnp.float32) for _ in range(heads)]
        for begin, rows, low, high in row_blocks(length):
            allowed = allowed_block(sc_ref, sr_ref, begin, rows, low, high)
            own = slice(begin, begin + rows)
            for head in range(heads):
                span = slice(head * HD, (head + 1) * HD)
                query_block, upstream_block = q_ref[own, span], u_ref[own, span]
                keys_block = k_ref[low:high, span]
                scores = jnp.where(allowed, contract(query_block, keys_block, 1, 1), MASK_FILL)
                probs = jnp.exp(scores - l_ref[own, head : head + 1])
                grad_probs = contract(upstream_block, v_ref[low:high, span], 1, 1)
                delta = jnp.sum(
                    upstream_block.astype(jnp.float32) * c_ref[own, span].astype(jnp.float32),
                    axis=1,
                    keepdims=True,
                )
                grad_scores = (probs * (grad_probs - delta)).astype(jnp.bfloat16)
                grad_query = contract(grad_scores, keys_block, 1, 0) * scale
                g_ref[own, span] = grad_query.astype(jnp.bfloat16)
                bias[head] = bias[head] + jnp.sum(grad_query, axis=0, keepdims=True)
                dk_ref[head, low:high] += contract(grad_scores, query_block, 0, 0)
                dv_ref[head, low:high] += contract(
                    probs.astype(jnp.bfloat16), upstream_block, 0, 0
                )
        for head in range(heads):
            span = slice(head * HD, (head + 1) * HD)
            b_ref[0:1, span] = bias[head]
            b_ref[1:2, span] = jnp.sum(dv_ref[head], axis=0, keepdims=True)
            g_ref[:, group + head * HD : group + (head + 1) * HD] = dk_ref[head].astype(
                jnp.bfloat16
            )
            g_ref[:, 2 * group + head * HD : 2 * group + (head + 1) * HD] = dv_ref[head].astype(
                jnp.bfloat16
            )

    vmem = pl.BlockSpec(memory_space=pltpu.VMEM)
    return pl.pallas_call(
        body,
        name="attention_backward",
        out_shape=[
            jax.ShapeDtypeStruct((length, 3 * group), jnp.bfloat16),
            jax.ShapeDtypeStruct((2, group), jnp.float32),
        ],
        in_specs=[vmem] * 8,
        out_specs=[vmem] * 2,
        scratch_shapes=[pltpu.VMEM((heads, length, HD), jnp.float32)] * 2,
    )(seg_column, seg_row, query, keys, values, context, logs, upstream)


def adam_update(param, grad, first, second, decay):
    first_new = BETA_ONE * first + (1.0 - BETA_ONE) * grad
    second_new = BETA_TWO * second + (1.0 - BETA_TWO) * grad * grad
    first_hat = first_new / (1.0 - BETA_ONE**ADAM_STEP)
    second_hat = second_new / (1.0 - BETA_TWO**ADAM_STEP)
    param_new = param - LEARN_RATE * (first_hat / (jnp.sqrt(second_hat) + ADAM_EPS) + decay * param)
    return (param_new, first_new, second_new)


def on_device(
    tokens,
    cotangent,
    segments,
    w_qkv,
    w_proj,
    w_fc,
    w_fc2,
    w_vectors,
    w_qvbias,
    w_fcbias,
    m_qkv,
    m_proj,
    m_fc,
    m_fc2,
    m_vectors,
    m_qvbias,
    m_fcbias,
    v_qkv,
    v_proj,
    v_fc,
    v_fc2,
    v_vectors,
    v_qvbias,
    v_fcbias,
):
    bfloat = jnp.bfloat16
    count = lax.axis_size("dp")
    depth, _, group = w_qkv.shape
    width = depth * count
    scale = 1.0 / math.sqrt(HD)
    proj_rows = w_proj.shape[0]
    qkv_bf = w_qkv.astype(bfloat)
    first_pair = jnp.concatenate([qkv_bf[:, 0], qkv_bf[:, 1]], axis=1)
    second_pair = jnp.concatenate(
        [qkv_bf[:, 2], w_proj.astype(bfloat).reshape(depth, proj_rows * width // depth)], axis=1
    )
    pair_full = gather_pair(0, first_pair, second_pair)
    first_full, second_full = (x.reshape(width, x.shape[2]) for x in pair_full)
    qkv_flat = jnp.concatenate([first_full, second_full[:, :group]], axis=1)
    proj_full = second_full[:, group:].reshape(proj_rows * count, width)

    inputs_f = tokens[0].astype(jnp.float32)
    seg_row = segments[0]
    first_in, normed_one, inverse_one = layer_norm(inputs_f, w_vectors[0], w_vectors[1])
    first_bf = first_in.astype(bfloat)
    projected = jnp.dot(first_bf, qkv_flat, preferred_element_type=jnp.float32)
    query = ((projected[:, :group] + w_qvbias[0]) * scale).astype(bfloat)
    keys = projected[:, group : 2 * group].astype(bfloat)
    values = (projected[:, 2 * group :] + w_qvbias[1]).astype(bfloat)
    sides = (seg_row[:, None], seg_row[None, :])
    context_flat, log_total = attention_forward(*sides, query, keys, values)
    attn_part = jnp.dot(context_flat, proj_full, preferred_element_type=jnp.float32)
    attn_sum, fc_full, fc2_full = sum_and_gather(
        1, attn_part.astype(bfloat), w_fc.astype(bfloat), w_fc2.astype(bfloat)
    )
    fc_full = fc_full.reshape(width, w_fc.shape[1])
    fc2_full = fc2_full.reshape(w_fc2.shape[0] * count, width)
    middle = (
        inputs_f
        + attn_sum.astype(jnp.float32)
        + w_vectors[4]
    )
    second_in, normed_two, inverse_two = layer_norm(middle, w_vectors[2], w_vectors[3])
    second_bf = second_in.astype(bfloat)
    hidden_pre = jnp.dot(second_bf, fc_full, preferred_element_type=jnp.float32) + w_fcbias
    hidden_bf = gelu_value(hidden_pre).astype(bfloat)
    mlp_part = jnp.dot(hidden_bf, fc2_full, preferred_element_type=jnp.float32)
    upstream = cotangent[0]
    grad_out = upstream.astype(jnp.float32)
    grad_fc2 = jnp.dot(hidden_bf.T, upstream, preferred_element_type=jnp.float32)
    grad_hidden = jnp.dot(upstream, fc2_full.T, preferred_element_type=jnp.float32) * gelu_slope(
        hidden_pre
    )
    grad_hidden_bf = grad_hidden.astype(bfloat)
    grad_fc = jnp.dot(second_bf.T, grad_hidden_bf, preferred_element_type=jnp.float32)
    grad_fcbias = jnp.sum(grad_hidden, axis=0)
    norm_two_part = jnp.dot(grad_hidden_bf, fc_full.T, preferred_element_type=jnp.float32)
    mlp_sum, norm_two_sum, fc2_summed, fc_summed = sum_and_reduce(
        2,
        (mlp_part.astype(bfloat), norm_two_part.astype(bfloat)),
        grad_fc2.astype(bfloat).reshape(count, w_fc2.shape[0], width),
        grad_fc.astype(bfloat).reshape(count, depth, w_fc.shape[1]),
    )
    output = (middle + mlp_sum.astype(jnp.float32) + w_vectors[5]).astype(bfloat)
    back_two, gain_two, shift_two = norm_backward(
        norm_two_sum.astype(jnp.float32),
        normed_two,
        inverse_two,
        w_vectors[2],
    )
    grad_middle = grad_out + back_two
    grad_middle_bf = grad_middle.astype(bfloat)
    grad_proj = jnp.dot(context_flat.T, grad_middle_bf, preferred_element_type=jnp.float32)
    grad_context = jnp.dot(grad_middle_bf, proj_full.T, preferred_element_type=jnp.float32).astype(
        bfloat
    )
    grad_stack, grad_qvbias = attention_backward(
        *sides, query, keys, values, context_flat, log_total, grad_context, scale
    )
    grad_qkv = jnp.dot(first_bf.T, grad_stack, preferred_element_type=jnp.float32).astype(bfloat)
    norm_one_part = jnp.dot(grad_stack, qkv_flat.T, preferred_element_type=jnp.float32)
    grad_first = grad_qkv[:, : 2 * group].reshape(count, depth, 2 * group)
    grad_second = jnp.concatenate(
        [grad_qkv[:, 2 * group :], grad_proj.astype(bfloat).reshape(width, group)], axis=1
    ).reshape(count, depth, 2 * group)
    norm_one_sum, first_summed, second_summed = sum_and_reduce(
        3, (norm_one_part.astype(bfloat),), grad_first, grad_second
    )
    qkv_summed = jnp.concatenate([first_summed, second_summed[:, :group]], axis=1).reshape(
        depth, 3, group
    )
    proj_summed = second_summed[:, group:].reshape(proj_rows, width)
    back_one, gain_one, shift_one = norm_backward(
        norm_one_sum.astype(jnp.float32),
        normed_one,
        inverse_one,
        w_vectors[0],
    )
    grad_input = (grad_middle + back_one).astype(bfloat)
    grad_vectors = jnp.stack(
        [
            gain_one,
            shift_one,
            gain_two,
            shift_two,
            jnp.sum(grad_middle, axis=0),
            jnp.sum(grad_out, axis=0),
        ]
    )
    small = jnp.concatenate(
        [grad_vectors.reshape(-1), grad_qvbias.reshape(-1), grad_fcbias.reshape(-1)]
    )
    small_size = small.shape[0]
    small_rows = -(-small_size // width)
    small_sum = sum_small(
        4, jnp.pad(small, (0, small_rows * width - small_size)).reshape(small_rows, width)
    ).reshape(-1)
    cut_one = grad_vectors.size
    cut_two = cut_one + grad_qvbias.size
    vectors_summed = small_sum[:cut_one].reshape(grad_vectors.shape)
    qvbias_summed = small_sum[cut_one:cut_two].reshape(grad_qvbias.shape)
    fcbias_summed = small_sum[cut_two:small_size]
    params = (w_qkv, w_proj, w_fc, w_fc2, w_vectors, w_qvbias, w_fcbias)
    gradients = (
        qkv_summed,
        proj_summed,
        fc_summed,
        fc2_summed,
        vectors_summed,
        qvbias_summed,
        fcbias_summed,
    )
    firsts = (m_qkv, m_proj, m_fc, m_fc2, m_vectors, m_qvbias, m_fcbias)
    seconds = (v_qkv, v_proj, v_fc, v_fc2, v_vectors, v_qvbias, v_fcbias)
    decays = (DECAY_RATE, DECAY_RATE, DECAY_RATE, DECAY_RATE, 0.0, 0.0, 0.0)
    updates = [
        adam_update(p, g, m, v, c)
        for p, g, m, v, c in zip(params, gradients, firsts, seconds, decays)
    ]
    return (
        output[None],
        grad_input[None],
        gradients[0],
        gradients[1],
        gradients[2],
        gradients[3],
        gradients[4],
        gradients[5],
        gradients[6],
        updates[0][0],
        updates[1][0],
        updates[2][0],
        updates[3][0],
        updates[4][0],
        updates[5][0],
        updates[6][0],
        updates[0][1],
        updates[1][1],
        updates[2][1],
        updates[3][1],
        updates[4][1],
        updates[5][1],
        updates[6][1],
        updates[0][2],
        updates[1][2],
        updates[2][2],
        updates[3][2],
        updates[4][2],
        updates[5][2],
        updates[6][2],
    )


BLOCK = 256


class Wires:
    def __init__(self, sends, receives):
        self.sends, self.receives, self.made = sends, receives, []

    def copy(self, source, target, peer):
        place = len(self.made)
        made = pltpu.make_async_remote_copy(
            src_ref=source,
            dst_ref=target,
            send_sem=self.sends.at[place],
            recv_sem=self.receives.at[place],
            device_id=peer,
            device_id_type=MESH_ID,
        )
        self.made.append(made)
        return made

    def drain(self):
        for made in self.made:
            made.wait_send()


class Grid:
    def __init__(self):
        self.count = lax.axis_size("dp")
        self.lines = self.count // 2
        self.index = lax.axis_index("dp")
        self.line, self.pair = lax.div(self.index, 2), lax.rem(self.index, 2)
        self.across = {"dp": self.line * 2 + 1 - self.pair}
        tensor = lax.axis_index("tensor")
        self.side = lax.rem(tensor, 2)
        self.core, self.far = {"tensor": flip_bit(tensor, 0)}, {"tensor": flip_bit(tensor, 1)}

    def owner(self, step, pair):
        return lax.rem(self.line + step + 2 * self.lines, self.lines) * 2 + pair

    def along(self, step):
        return {"dp": self.owner(step, self.pair)}

    def peers(self):
        return [self.across, self.core, self.far] + [self.along(s) for s in range(1, self.lines)]


class Route:
    def __init__(self, grid, rows):
        self.index, self.count = grid.index, grid.count
        self.depth = rows // grid.count
        self.half = self.depth // 2
        self.place = ring_position(grid.index, grid.count)
        self.peers = ring_peers(grid.count)

    def hops(self, way, array):
        return self.count // 2 if way == array else self.count - 1 - self.count // 2

    def keys(self, step):
        return [(w, a) for a in range(2) for w in range(2) if step < self.hops(w, a)]

    def at(self, distance, way):
        return ring_index(self.place + (1 - 2 * way) * distance + self.count, self.count)

    def span(self, owner):
        return pl.ds(pl.multiple_of(owner * self.depth, 16), self.depth)

    def half_span(self, owner, array):
        begin = owner * self.depth + array * self.half
        return pl.ds(pl.multiple_of(begin, 16), self.half)

    def start(self):
        for key in self.keys(0):
            self.copies[0, *key].start()


class Gather(Route):
    def __init__(self, grid, wires, full):
        super().__init__(grid, full.shape[0])
        self.copies = {}
        for step in range(grid.count // 2):
            for way, array in self.keys(step):
                block = full.at[self.half_span(self.at(-step, way), array)]
                self.copies[step, way, array] = wires.copy(block, block, self.peers[way])

    def step(self, step):
        for key in self.keys(step):
            self.copies[step - 1, *key].wait_recv()
            self.copies[step, *key].start()

    def finish(self):
        for way in range(2):
            for array in range(2):
                self.copies[self.hops(way, array) - 1, way, array].wait_recv()


class Reduce(Route):
    def __init__(self, grid, wires, source, slots):
        super().__init__(grid, source.shape[0])
        self.source, self.slots = source, slots
        self.copies = {}
        for step in range(grid.count // 2):
            for way, array in self.keys(step):
                if step == 0:
                    block = source.at[self.block(0, way, array)]
                else:
                    block = slots.at[array, way, step - 1]
                target = slots.at[array, way, step]
                self.copies[step, way, array] = wires.copy(block, target, self.peers[way])

    def block(self, step, way, array):
        return self.half_span(self.at(self.hops(way, array) - step, way), array)

    def step(self, step):
        for way, array in self.keys(step):
            self.copies[step - 1, way, array].wait_recv()
            own = self.source[self.block(step, way, array), :].astype(jnp.float32)
            arrived = self.slots[array, way, step - 1].astype(jnp.float32)
            self.slots[array, way, step - 1] = (own + arrived).astype(jnp.bfloat16)
            self.copies[step, way, array].start()

    def finish(self):
        halves = []
        for array in range(2):
            total = self.source[self.half_span(self.index, array), :].astype(jnp.float32)
            for way in range(2):
                last = self.hops(way, array) - 1
                self.copies[last, way, array].wait_recv()
                total = total + self.slots[array, way, last].astype(jnp.float32)
            halves.append(total)
        return jnp.concatenate(halves, axis=0)


class Share:
    def __init__(self, grid, wires, part, arrivals, out):
        self.part, self.arrivals, self.out = part, arrivals, out
        self.half, self.side = arrivals.shape[2], grid.side
        blocks = range(arrivals.shape[1])
        self.first = [
            wires.copy(part.at[self.span(b, 1 - grid.side)], arrivals.at[0, b], grid.core)
            for b in blocks
        ]
        self.second = [
            wires.copy(part.at[self.mine(b)], arrivals.at[1, b], grid.far) for b in blocks
        ]
        self.third = [
            wires.copy(out.at[self.mine(b)], out.at[self.mine(b)], grid.core) for b in blocks
        ]

    def span(self, block, side):
        begin = block * 2 * self.half + side * self.half
        return pl.ds(pl.multiple_of(begin, self.half), self.half)

    def mine(self, block):
        return self.span(block, self.side)

    def give(self, block, value):
        rows = 2 * self.half
        self.part[block * rows : (block + 1) * rows, :] = value.astype(jnp.bfloat16)
        self.first[block].start()

    def cross(self, block):
        self.first[block].wait_recv()
        span = self.mine(block)
        own, arrived = self.part[span, :], self.arrivals[0, block]
        self.part[span, :] = (own.astype(jnp.float32) + arrived.astype(jnp.float32)).astype(
            jnp.bfloat16
        )
        self.second[block].start()

    def take(self, block):
        self.second[block].wait_recv()
        own, arrived = self.part[self.mine(block), :], self.arrivals[1, block]
        return own.astype(jnp.float32) + arrived.astype(jnp.float32)

    def put(self, block, value):
        self.out[self.mine(block), :] = value.astype(jnp.bfloat16)
        self.third[block].start()

    def close(self, block):
        self.third[block].wait_recv()


def column_sum(values):
    return jnp.sum(values, axis=0, keepdims=True)


def padded_rows(rows):
    return -(-rows // 32) * 32


def fused_body(scale, shapes, *refs):
    length, width, group, hidden, depth, proj_rows = shapes
    (
        x_ref, g_ref, sr_ref, wq_ref, wo_ref, w1_ref, w2_ref, vec_ref, qv_ref, fb_ref,
        out_ref, gt_ref, gq_ref, go_ref, g1_ref, g2_ref, gv_ref, gqv_ref, gfb_ref,
        fq, fo, f1, f2, wo_f, wo, a1, q_s, k_s, v_s, c_s, pr_s, h_s, dh_s, a2, dhb, gw, u_s, dz_s,
        dk_s, dv_s, dp_s, part_a, part_n, part_m, part_i, arr_a, arr_n, arr_m, arr_i,
        sq, so, s1, s2, nq, no, n1, n2, sm_own, sm_core, sm_two, sm_pair, sm_four,
        sm_line, sc_ref, sends, receives,
    ) = refs
    f32, b16 = jnp.float32, jnp.bfloat16
    grid, wires = Grid(), Wires(sends, receives)
    heads, rows = group // HD, BLOCK
    pad = padded_rows(proj_rows)
    blocks = length // rows
    order = list(range(blocks))[::-1]

    gathers = {n: Gather(grid, wires, f) for n, f in (("q", fq), ("o", fo), ("2", f2), ("1", f1))}
    share_a = Share(grid, wires, part_a, arr_a, a2)
    share_n = Share(grid, wires, part_n, arr_n, dhb)
    share_m = Share(grid, wires, part_m, arr_m, out_ref)
    share_i = Share(grid, wires, part_i, arr_i, gt_ref)
    reduce_2, reduce_1 = Reduce(grid, wires, s2, n2), Reduce(grid, wires, s1, n1)
    reduce_q, reduce_o = Reduce(grid, wires, sq, nq), Reduce(grid, wires, so, no)
    small_core = wires.copy(sm_own, sm_core, grid.core)
    small_pair = wires.copy(sm_two, sm_pair, grid.across)
    small_line = [
        wires.copy(sm_four, sm_line.at[s - 1], grid.along(s)) for s in range(1, grid.lines)
    ]

    def block_rows(b):
        return slice(b * rows, (b + 1) * rows)

    barrier = pltpu.get_barrier_semaphore()
    peers = grid.peers()
    for peer in peers:
        pl.semaphore_signal(barrier, inc=1, device_id=peer, device_id_type=MESH_ID)
    own_rows = gathers["q"].span(grid.index)
    for j in range(3):
        fq[own_rows, j * group : (j + 1) * group] = wq_ref[j].astype(b16)
    own_proj = wo_ref[...]
    if pad > proj_rows:
        own_proj = jnp.concatenate([own_proj, jnp.zeros((pad - proj_rows, width), f32)], axis=0)
    fo[gathers["o"].span(grid.index), :] = own_proj.astype(b16)
    pl.semaphore_wait(barrier, len(peers))
    gathers["q"].start()
    gathers["o"].start()
    f2[gathers["2"].span(grid.index), :] = w2_ref[...].astype(b16)
    f1[gathers["1"].span(grid.index), :] = w1_ref[...].astype(b16)

    for b in order:
        first_in, _, _ = layer_norm(x_ref[block_rows(b), :].astype(f32), vec_ref[0:1], vec_ref[1:2])
        a1[block_rows(b), :] = first_in.astype(b16)
    dk_s[...] = jnp.zeros_like(dk_s)
    dv_s[...] = jnp.zeros_like(dv_s)
    for b in order:
        wide_row = jnp.broadcast_to(sr_ref[:, block_rows(b)], (8, rows)).astype(f32)
        sc_ref[block_rows(b), :] = jnp.transpose(wide_row)[:, :1].astype(jnp.int32)
    sum_g = jnp.zeros((1, width), f32)
    for b in order:
        sum_g = sum_g + column_sum(g_ref[share_a.mine(b), :].astype(f32))
    sm_own[5:6, :] = sum_g

    for step in range(1, grid.count // 2):
        gathers["q"].step(step)
        gathers["o"].step(step)
    gathers["2"].start()
    gathers["1"].start()
    pending = [(name, step) for step in range(1, grid.count // 2) for name in ("2", "1")]

    def poll(times=1):
        for name, step in pending[:times]:
            gathers[name].step(step)
        del pending[:times]

    gathers["q"].finish()
    for b in order:
        projected = jnp.dot(a1[block_rows(b), :], fq[...], preferred_element_type=f32)
        q_s[block_rows(b), :] = ((projected[:, :group] + qv_ref[0:1]) * scale).astype(b16)
        k_s[block_rows(b), :] = projected[:, group : 2 * group].astype(b16)
        v_s[block_rows(b), :] = (projected[:, 2 * group :] + qv_ref[1:2]).astype(b16)
    gathers["o"].finish()
    for i in range(grid.count):
        block = fo[i * pad : (i + 1) * pad, :].astype(f32)
        wo_f[i * proj_rows : (i + 1) * proj_rows, :] = block[:proj_rows]
    wo[...] = wo_f[...].astype(b16)

    def window(b):
        return max(0, b * rows - -(-SEGMENT_LIMIT // rows) * rows), (b + 1) * rows

    def attend(b):
        low, high = window(b)
        allowed = allowed_block(sc_ref, sr_ref, b * rows, rows, low, high)
        bias = jnp.where(allowed, 0.0, MASK_FILL)
        for head in range(heads):
            span = slice(head * HD, (head + 1) * HD)
            scores = contract(q_s[block_rows(b), span], k_s[low:high, span], 1, 1) + bias
            largest = jnp.max(scores, axis=1, keepdims=True)
            raised = jnp.exp(scores - largest)
            total = jnp.sum(raised, axis=1, keepdims=True)
            probs = (raised * (1.0 / total)).astype(b16)
            pr_s[b, head, :, : high - low] = probs
            c_s[block_rows(b), span] = contract(probs, v_s[low:high, span], 1, 0).astype(b16)

    for i, b in enumerate(order):
        attend(b)
        share_a.give(b, jnp.dot(c_s[block_rows(b), :], wo[...], preferred_element_type=f32))
        if i >= 1:
            share_a.cross(order[i - 1])
        poll()
    share_a.cross(order[-1])

    for i, b in enumerate(order):
        if i == blocks - 1:
            poll(len(pending))
            gathers["2"].finish()
            for c in order:
                gw[block_rows(c), :] = contract(g_ref[block_rows(c), :], f2[...], 1, 1)
        total = share_a.take(b)
        middle = x_ref[share_a.mine(b), :].astype(f32) + total + vec_ref[4:5]
        h_s[b] = middle
        second_in, _, _ = layer_norm(middle, vec_ref[2:3], vec_ref[3:4])
        share_a.put(b, second_in)
        poll()
    gathers["1"].finish()

    tile = 256 if hidden % 256 == 0 else hidden
    sum_fb = [jnp.zeros((1, tile), f32) for _ in range(hidden // tile)]
    sums = {"gain2": jnp.zeros((1, width), f32), "shift2": jnp.zeros((1, width), f32)}
    sums["mid"] = jnp.zeros((1, width), f32)

    def take_n(b):
        upstream = share_n.take(b)
        _, normed, inverse = layer_norm(h_s[b], vec_ref[2:3], vec_ref[3:4])
        back, _, _ = norm_backward(upstream, normed, inverse, vec_ref[2:3])
        sums["gain2"] = sums["gain2"] + column_sum(upstream * normed)
        sums["shift2"] = sums["shift2"] + column_sum(upstream)
        grad_middle = g_ref[share_n.mine(b), :].astype(f32) + back
        sums["mid"] = sums["mid"] + column_sum(grad_middle)
        dh_s[b] = grad_middle
        share_n.put(b, grad_middle)

    for i, b in enumerate(order):
        share_a.close(b)
        for c in range(hidden // tile):
            span = slice(c * tile, (c + 1) * tile)
            z = jnp.dot(a2[block_rows(b), :], f1[:, span], preferred_element_type=f32)
            z = z + fb_ref[span].reshape(1, tile)
            square = z * z
            tangent = jnp.tanh(GELU_COEF * z * (1.0 + CUBIC_COEF * square))
            half = 0.5 * (1.0 + tangent)
            u_s[block_rows(b), span] = (z * half).astype(b16)
            slope = half + 0.5 * z * (1.0 - tangent * tangent) * GELU_COEF * (
                1.0 + 3.0 * CUBIC_COEF * square
            )
            dz = gw[block_rows(b), span] * slope
            sum_fb[c] = sum_fb[c] + column_sum(dz)
            dz_s[block_rows(b), span] = dz.astype(b16)
        share_n.give(b, contract(dz_s[block_rows(b), :], f1[...], 1, 1))
        share_m.give(b, jnp.dot(u_s[block_rows(b), :], f2[...], preferred_element_type=f32))
        share_n.cross(b)
    for c in range(hidden // tile):
        sm_own[6:7, c * tile : (c + 1) * tile] = sum_fb[c]

    def outer(target, left, right):
        for begin in range(0, target.shape[0], BLOCK):
            target[begin : begin + BLOCK, :] = contract(
                left[:, begin : begin + BLOCK], right[...], 0, 0
            ).astype(b16)

    outer(s2, u_s, g_ref)
    reduce_2.start()
    outer(s1, a2, dz_s)
    reduce_1.start()
    later = [(r, step) for step in range(1, grid.count // 2) for r in (reduce_2, reduce_1)]

    def advance(times=1):
        for reduce, step in later[:times]:
            reduce.step(step)
        del later[:times]

    take_n(order[0])
    share_m.cross(order[0])

    bias_q = [jnp.zeros((1, HD), f32) for _ in range(heads)]
    bias_v = [jnp.zeros((1, HD), f32) for _ in range(heads)]

    def attend_back(b):
        low, high = window(b)
        grad_context = contract(dhb[block_rows(b), :], wo[...], 1, 1).astype(b16)
        for head in range(heads):
            span = slice(head * HD, (head + 1) * HD)
            upstream = grad_context[:, span]
            probs = pr_s[b, head, :, : high - low]
            keys_block = k_s[low:high, span]
            grad_probs = contract(upstream, v_s[low:high, span], 1, 1)
            delta = jnp.sum(
                upstream.astype(f32) * c_s[block_rows(b), span].astype(f32), axis=1, keepdims=True
            )
            grad_scores = (probs.astype(f32) * (grad_probs - delta)).astype(b16)
            grad_query = contract(grad_scores, keys_block, 1, 0) * scale
            dp_s[block_rows(b), span] = grad_query.astype(b16)
            bias_q[head] = bias_q[head] + column_sum(grad_query)
            dk_s[head, low:high] += contract(grad_scores, q_s[block_rows(b), span], 0, 0)
            dv_s[head, low:high] += contract(probs, upstream, 0, 0)
        for head in range(heads):
            begin = group + head * HD
            dp_s[block_rows(b), begin : begin + HD] = dk_s[head, block_rows(b)].astype(b16)
            grad_value = dv_s[head, block_rows(b)]
            bias_v[head] = bias_v[head] + column_sum(grad_value)
            dp_s[block_rows(b), begin + group : begin + group + HD] = grad_value.astype(b16)

    for i, b in enumerate(order):
        if i + 1 < blocks:
            take_n(order[i + 1])
        share_n.close(b)
        attend_back(b)
        share_i.give(b, contract(dp_s[block_rows(b), :], fq[...], 1, 1))
        if i >= 1:
            share_i.cross(order[i - 1])
        advance()
    for name, row in (("gain2", 2), ("shift2", 3), ("mid", 4)):
        sm_own[row : row + 1, :] = sums[name]
    sm_own[7:8, :] = jnp.zeros((1, width), f32)
    for head in range(heads):
        sm_own[7:8, head * HD : (head + 1) * HD] = bias_q[head]
        sm_own[7:8, group + head * HD : group + (head + 1) * HD] = bias_v[head]

    outer(sq, a1, dp_s)
    reduce_q.start()
    share_i.cross(order[-1])
    for b in order[1:]:
        share_m.cross(b)
    grad_proj = contract(c_s[...], dhb[...], 0, 0)
    for i in range(grid.count):
        block = grad_proj[i * proj_rows : (i + 1) * proj_rows]
        if pad > proj_rows:
            block = jnp.concatenate([block, jnp.zeros((pad - proj_rows, width), f32)], axis=0)
        so[i * pad : (i + 1) * pad, :] = block.astype(b16)
    reduce_o.start()
    later += [(r, step) for step in range(1, grid.count // 2) for r in (reduce_q, reduce_o)]

    gain, shift = jnp.zeros((1, width), f32), jnp.zeros((1, width), f32)
    for i, b in enumerate(order):
        upstream = share_i.take(b)
        _, normed, inverse = layer_norm(
            x_ref[share_i.mine(b), :].astype(f32), vec_ref[0:1], vec_ref[1:2]
        )
        back, _, _ = norm_backward(upstream, normed, inverse, vec_ref[0:1])
        gain = gain + column_sum(upstream * normed)
        shift = shift + column_sum(upstream)
        share_i.put(b, dh_s[b] + back)
        advance(2)
    sm_own[0:1, :] = gain
    sm_own[1:2, :] = shift
    small_core.start()

    def take_m(b):
        share_m.put(b, h_s[b] + share_m.take(b) + vec_ref[5:6])

    for b in order[: blocks // 2]:
        take_m(b)
    advance(len(later))
    g2_ref[...] = reduce_2.finish()
    small_core.wait_recv()
    sm_two[0:6, :] = sm_own[0:6, :] + sm_core[0:6, :]
    sm_two[6:8, :] = sm_own[6:8, :]
    small_pair.start()
    g1_ref[...] = reduce_1.finish()
    small_pair.wait_recv()
    sm_four[...] = sm_two[...] + sm_pair[...]
    for made in small_line:
        made.start()
    total_q = reduce_q.finish()
    for j in range(3):
        gq_ref[j] = total_q[:, j * group : (j + 1) * group]
    go_ref[...] = reduce_o.finish()[:proj_rows]
    total = sm_four[...]
    for step, made in enumerate(small_line):
        made.wait_recv()
        total = total + sm_line[step]
    gv_ref[...] = total[0:6]
    gfb_ref[...] = total[6:7].reshape(width)
    gqv_ref[0:1, :] = total[7:8, :group]
    gqv_ref[1:2, :] = total[7:8, group : 2 * group]
    for b in order[blocks // 2 :]:
        take_m(b)
    for b in order:
        share_m.close(b)
        share_i.close(b)
    wires.drain()


def fused_call(x, g, seg, wq, wo, w1, w2, vec, qv, fb):
    f32, b16 = jnp.float32, jnp.bfloat16
    length, width = x.shape
    _, depth, group = wq.shape
    hidden, proj_rows = w1.shape[1], wo.shape[0]
    count, lines, blocks = lax.axis_size("dp"), lax.axis_size("dp") // 2, length // BLOCK
    heads, pad, half = group // HD, padded_rows(proj_rows), BLOCK // 2
    reach = min(length, -(-SEGMENT_LIMIT // BLOCK) * BLOCK + BLOCK)

    def full(*shape):
        return pltpu.VMEM(shape, b16)

    def wide(*shape):
        return pltpu.VMEM(shape, f32)

    scratch = [
        full(width, 3 * group), full(count * pad, width), full(width, hidden), full(hidden, width),
        wide(group, width), full(group, width), full(length, width),
        full(length, group), full(length, group), full(length, group), full(length, group),
        full(blocks, heads, BLOCK, reach),
        wide(blocks, half, width), wide(blocks, half, width),
        full(length, width), full(length, width), wide(length, hidden),
        full(length, hidden), full(length, hidden),
        wide(heads, length, HD), wide(heads, length, HD), full(length, 3 * group),
    ]
    scratch += [full(length, width)] * 4 + [full(2, blocks, half, width)] * 4
    shards = [(depth, 3 * group), (pad, width), (depth, hidden), (w2.shape[0], width)]
    scratch += [full(count * a, b) for a, b in shards]
    scratch += [full(2, 2, count // 2, a // 2, b) for a, b in shards]
    scratch += [wide(8, width)] * 5 + [wide(lines - 1, 8, width)]
    copies = 16 * (count - 1) + 12 * blocks + 2 + lines - 1
    scratch += [pltpu.VMEM((length, 1), jnp.int32)]
    scratch += [pltpu.SemaphoreType.DMA((copies,))] * 2
    outputs = [
        jax.ShapeDtypeStruct(s, t)
        for s, t in (
            (x.shape, b16), (x.shape, b16), (wq.shape, f32), (wo.shape, f32), (w1.shape, f32),
            (w2.shape, f32), (vec.shape, f32), (qv.shape, f32), (fb.shape, f32),
        )
    ]
    vmem = pl.BlockSpec(memory_space=pltpu.VMEM)
    inputs = (x, g, seg, wq, wo, w1, w2, vec, qv, fb)
    shapes = (length, width, group, hidden, depth, proj_rows)
    return pl.pallas_call(
        functools.partial(fused_body, 1.0 / math.sqrt(HD), shapes),
        name="fused_block",
        out_shape=outputs,
        in_specs=[vmem] * len(inputs),
        out_specs=[vmem] * len(outputs),
        scratch_shapes=scratch,
        compiler_params=pltpu.CompilerParams(
            collective_id=5, has_side_effects=True, vmem_limit_bytes=VMEM_BYTES
        ),
    )(*inputs)


VMEM_BYTES = 63 * 1024 * 1024


def adam_body(number, *refs):
    keep = number // 4
    (x_ref, g_ref), sources, refs = refs[:2], refs[2 : 2 + number], refs[2 + number :]
    (y_ref, h_ref), results = refs[:2], refs[2:]
    y_ref[...] = x_ref[...]
    h_ref[...] = g_ref[...]
    pieces = [sources[k * keep : (k + 1) * keep] for k in range(4)]
    for k in range(keep):
        param, grad, first, second = (piece[k][...] for piece in pieces)
        decay = DECAY_RATE if k < 4 else 0.0
        new, first_new, second_new = adam_update(param, grad, first, second, decay)
        results[k][...] = grad
        results[keep + k][...] = new
        results[2 * keep + k][...] = first_new
        results[3 * keep + k][...] = second_new


def adam_call(carried, params, gradients, firsts, seconds):
    inputs = (*carried, *params, *gradients, *firsts, *seconds)
    vmem = pl.BlockSpec(memory_space=pltpu.VMEM)
    outputs = [jax.ShapeDtypeStruct(p.shape, p.dtype) for p in (*carried, *params * 4)]
    return pl.pallas_call(
        functools.partial(adam_body, len(inputs) - 2),
        name="adam_step",
        out_shape=outputs,
        in_specs=[vmem] * len(inputs),
        out_specs=[vmem] * len(outputs),
        compiler_params=pltpu.CompilerParams(vmem_limit_bytes=VMEM_BYTES),
    )(*inputs)


def turn(array):
    return jnp.transpose(array, (1, 0, 2))


def on_device_fused(tokens, cotangent, segments, *state):
    params, firsts, seconds = state[:7], state[7:14], state[14:]

    def shaped(group):
        return (turn(group[0]), *group[1:])

    params, firsts, seconds = shaped(params), shaped(firsts), shaped(seconds)
    results = fused_call(tokens[0], cotangent[0], segments, *params)
    updated = adam_call(results[:2], params, results[2:], firsts, seconds)
    restored = [
        (turn(updated[k]), *updated[k + 1 : k + 7])
        for k in range(2, 30, 7)
    ]
    return (updated[0][None], updated[1][None]) + sum(restored, ())


def fused_fits(mesh, args):
    tokens, w_qkv, w_proj, w_fc, w_fc2 = args[0], args[3], args[4], args[5], args[6]
    count, wide = mesh.shape["dp"], mesh.shape["tensor"]
    width, length = tokens.shape[2], tokens.shape[1]
    depth, group, hidden = width // count, w_qkv.shape[2] // wide, w_fc.shape[1] // wide
    proj_rows = w_proj.shape[0] // (wide * count)
    return (
        wide == 4
        and count % 2 == 0
        and count >= 4
        and depth % 32 == 0
        and (w_fc2.shape[0] // (wide * count)) % 32 == 0
        and proj_rows % 8 == 0
        and length % BLOCK == 0
        and width % BLOCK == 0
        and hidden % BLOCK == 0
        and hidden == width
        and 2 * group <= width
    )


def mapped(mesh, body):
    return jax.shard_map(
        body,
        mesh=mesh,
        in_specs=(
            P("dp", None, None),
            P("dp", None, None),
            P("dp", None),
            P("dp", None, "tensor"),
            P(("tensor", "dp"), None),
            P("dp", "tensor"),
            P(("tensor", "dp"), None),
            P(),
            P(None, "tensor"),
            P("tensor"),
            P("dp", None, "tensor"),
            P(("tensor", "dp"), None),
            P("dp", "tensor"),
            P(("tensor", "dp"), None),
            P(),
            P(None, "tensor"),
            P("tensor"),
            P("dp", None, "tensor"),
            P(("tensor", "dp"), None),
            P("dp", "tensor"),
            P(("tensor", "dp"), None),
            P(),
            P(None, "tensor"),
            P("tensor"),
        ),
        out_specs=(
            P("dp", None, None),
            P("dp", None, None),
            P("dp", None, "tensor"),
            P(("tensor", "dp"), None),
            P("dp", "tensor"),
            P(("tensor", "dp"), None),
            P(),
            P(None, "tensor"),
            P("tensor"),
            P("dp", None, "tensor"),
            P(("tensor", "dp"), None),
            P("dp", "tensor"),
            P(("tensor", "dp"), None),
            P(),
            P(None, "tensor"),
            P("tensor"),
            P("dp", None, "tensor"),
            P(("tensor", "dp"), None),
            P("dp", "tensor"),
            P(("tensor", "dp"), None),
            P(),
            P(None, "tensor"),
            P("tensor"),
            P("dp", None, "tensor"),
            P(("tensor", "dp"), None),
            P("dp", "tensor"),
            P(("tensor", "dp"), None),
            P(),
            P(None, "tensor"),
            P("tensor"),
        ),
        check_vma=False,
    )


def solution(mesh):
    def run(*args):
        body = on_device_fused if fused_fits(mesh, args) else on_device
        return mapped(mesh, body)(*args)

    return run
```

```python
import functools
import math

import jax
import jax.numpy as jnp
from jax import lax
from jax.experimental import pallas as pl
from jax.experimental.pallas import tpu as pltpu
from jax.sharding import PartitionSpec as P

HD = 64
ADAM_STEP = 3


NORM_EPS = 1e-05
ADAM_EPS = 1e-08
LEARN_RATE = 0.1
BETA_ONE = 0.9
BETA_TWO = 0.95
DECAY_RATE = 0.1
MASK_FILL = -1e30
GELU_COEF = 0.7978845608028654
CUBIC_COEF = 0.044715


def layer_norm(values, gain, shift):
    center = values - jnp.mean(values, axis=1, keepdims=True)
    inverse = lax.rsqrt(jnp.mean(center * center, axis=1, keepdims=True) + NORM_EPS)
    normed = center * inverse
    return (normed * gain + shift, normed, inverse)


def norm_backward(upstream, normed, inverse, gain):
    scaled = upstream * gain
    inner = (
        scaled
        - jnp.mean(scaled, axis=1, keepdims=True)
        - normed * jnp.mean(scaled * normed, axis=1, keepdims=True)
    )
    return (inverse * inner, jnp.sum(upstream * normed, axis=0), jnp.sum(upstream, axis=0))


def gelu_value(values):
    inner = GELU_COEF * (values + CUBIC_COEF * values * values * values)
    return 0.5 * values * (1.0 + jnp.tanh(inner))


def gelu_slope(values):
    tangent = jnp.tanh(GELU_COEF * (values + CUBIC_COEF * values * values * values))
    return 0.5 * (1.0 + tangent) + 0.5 * values * (1.0 - tangent * tangent) * GELU_COEF * (
        1.0 + 3.0 * CUBIC_COEF * values * values
    )


MESH_ID = pl.DeviceIdType.MESH


def ring_position(index, count):
    odd = lax.rem(index, 2)
    return (1 - odd) * lax.div(index, 2) + odd * (count - 1 - lax.div(index, 2))


def ring_index(position, count):
    place = lax.rem(position + 2 * count, count)
    back = lax.div(place, count // 2)
    return (1 - back) * 2 * place + back * (2 * (count - 1 - place) + 1)


def greet(peers):
    barrier = pltpu.get_barrier_semaphore()
    for peer in peers:
        pl.semaphore_signal(barrier, inc=1, device_id=peer, device_id_type=MESH_ID)
    pl.semaphore_wait(barrier, len(peers))


def ring_peers(count):
    place = ring_position(lax.axis_index("dp"), count)
    return [{"dp": ring_index(place + 1, count)}, {"dp": ring_index(place - 1, count)}]


def flip_bit(index, bit):
    weight = 1 << bit
    return index + weight * (1 - 2 * lax.rem(lax.div(index, weight), 2))


def cube_peers(count):
    index = lax.axis_index("tensor")
    return [{"tensor": flip_bit(index, bit)} for bit in range(count.bit_length() - 1)]


def pieces_of(columns):
    for pieces in (3, 2):
        if columns % (pieces * 128) == 0 and columns // pieces <= 384:
            return pieces
    return 1


class Ring:
    def __init__(self, count, columns):
        self.count = count
        self.index = lax.axis_index("dp")
        self.place = ring_position(self.index, count)
        self.peers = ring_peers(count)
        self.pieces = pieces_of(columns)
        self.width = columns // self.pieces

    def span(self, piece):
        return pl.ds(piece * self.width, self.width)

    def hops(self, way, array):
        return self.count // 2 if way == array else self.count - 1 - self.count // 2

    def at(self, distance, way):
        return ring_index(self.place + (1 - 2 * way) * distance + self.count, self.count)

    def each(self, step):
        return [
            (way, array, piece)
            for piece in range(self.pieces)
            for array in range(2)
            for way in range(2)
            if step < self.hops(way, array)
        ]

    def all(self):
        return [(step, *key) for step in range(self.count // 2) for key in self.each(step)]

    def start(self):
        for key in self.each(0):
            self.copy(0, *key).start()

    def drain(self):
        for key in self.all():
            self.copy(*key).wait_send()


class RingGather(Ring):
    def __init__(self, count, sources, results, sends, receives):
        super().__init__(count, sources[0].shape[-1])
        self.sources, self.results = sources, results
        self.sends, self.receives = sends, receives

    def copy(self, step, way, array, piece):
        target = self.results[array].at[self.at(-step, way), :, self.span(piece)]
        return pltpu.make_async_remote_copy(
            src_ref=self.sources[array].at[:, self.span(piece)] if step == 0 else target,
            dst_ref=target,
            send_sem=self.sends.at[way, array, step, piece],
            recv_sem=self.receives.at[way, array, step, piece],
            device_id=self.peers[way],
            device_id_type=MESH_ID,
        )

    def own(self):
        for array in range(2):
            self.results[array][self.index] = self.sources[array][...]

    def steps(self):
        for step in range(1, self.count // 2):
            for key in self.each(step):
                self.copy(step - 1, *key).wait_recv()
                self.copy(step, *key).start()

    def finish(self):
        for way in range(2):
            for array in range(2):
                for piece in range(self.pieces):
                    self.copy(self.hops(way, array) - 1, way, array, piece).wait_recv()
        self.drain()


class RingReduce(Ring):
    def __init__(self, count, sources, slots, results, sends, receives):
        super().__init__(count, sources[0].shape[-1])
        self.sources, self.slots, self.results = sources, slots, results
        self.sends, self.receives = sends, receives

    def block(self, step, way, array):
        return self.at(self.hops(way, array) - step, way)

    def copy(self, step, way, array, piece):
        span = self.span(piece)
        if step == 0:
            source = self.sources[array].at[self.block(0, way, array), :, span]
        else:
            source = self.slots[array].at[way, step - 1, :, span]
        return pltpu.make_async_remote_copy(
            src_ref=source,
            dst_ref=self.slots[array].at[way, step, :, span],
            send_sem=self.sends.at[way, array, step, piece],
            recv_sem=self.receives.at[way, array, step, piece],
            device_id=self.peers[way],
            device_id_type=MESH_ID,
        )

    def steps(self):
        for step in range(1, self.count // 2):
            for way, array, piece in self.each(step):
                self.copy(step - 1, way, array, piece).wait_recv()
                span = self.span(piece)
                own = self.sources[array][self.block(step, way, array), :, span]
                arrived = self.slots[array][way, step - 1, :, span]
                self.slots[array][way, step - 1, :, span] = (
                    arrived.astype(jnp.float32) + own.astype(jnp.float32)
                ).astype(jnp.bfloat16)
                self.copy(step, way, array, piece).start()

    def finish(self):
        for array in range(2):
            for piece in range(self.pieces):
                span = self.span(piece)
                total = self.sources[array][self.index, :, span].astype(jnp.float32)
                for way in range(2):
                    last = self.hops(way, array) - 1
                    self.copy(last, way, array, piece).wait_recv()
                    total = total + self.slots[array][way, last, :, span].astype(jnp.float32)
                self.results[array][:, span] = total
        self.drain()


class CubeSum:
    def __init__(self, count, source, result, arrivals, sums, sends, receives):
        self.bits = count.bit_length() - 1
        self.source, self.result, self.arrivals, self.sums = source, result, arrivals, sums
        self.sends, self.receives = sends, receives
        self.peers = cube_peers(count)
        self.side = lax.rem(lax.axis_index("tensor"), 2)
        self.chunks, self.rows = arrivals.shape[1], arrivals.shape[2]
        self.half = self.chunks * self.rows

    def mine(self, chunk, side):
        return pl.ds(pl.multiple_of(side * self.half + chunk * self.rows, self.rows), self.rows)

    def copy(self, stage, chunk):
        if stage == 0:
            source = self.source.at[self.mine(chunk, 1 - self.side)]
            target = self.arrivals.at[0, chunk]
        elif stage < self.bits:
            source, target = self.sums.at[stage - 1, chunk], self.arrivals.at[stage, chunk]
        else:
            source = self.result.at[self.mine(chunk, self.side)]
            target = source
        return pltpu.make_async_remote_copy(
            src_ref=source,
            dst_ref=target,
            send_sem=self.sends.at[stage, chunk],
            recv_sem=self.receives.at[stage, chunk],
            device_id=self.peers[stage % self.bits],
            device_id_type=MESH_ID,
        )

    def start(self):
        for chunk in range(self.chunks):
            self.copy(0, chunk).start()

    def add(self, stage):
        for chunk in range(self.chunks):
            self.copy(stage, chunk).wait_recv()
            if stage == 0:
                own = self.source[self.mine(chunk, self.side)]
            else:
                own = self.sums[stage - 1, chunk]
            total = own.astype(jnp.float32) + self.arrivals[stage, chunk].astype(jnp.float32)
            if stage == self.bits - 1:
                self.result[self.mine(chunk, self.side)] = total.astype(jnp.bfloat16)
            else:
                self.sums[stage, chunk] = total.astype(jnp.bfloat16)
            self.copy(stage + 1, chunk).start()

    def last(self):
        for stage in range(1, self.bits):
            self.add(stage)

    def finish(self):
        for chunk in range(self.chunks):
            self.copy(self.bits, chunk).wait_recv()
        for stage in range(self.bits + 1):
            for chunk in range(self.chunks):
                self.copy(stage, chunk).wait_send()


CHUNKS = 4


def cube_scratch(count, rows, columns):
    bits = count.bit_length() - 1
    block = (CHUNKS, rows // 2 // CHUNKS, columns)
    return [
        pltpu.VMEM((bits,) + block, jnp.bfloat16),
        pltpu.VMEM((bits,) + block, jnp.bfloat16),
        pltpu.SemaphoreType.DMA((bits + 1, CHUNKS)),
        pltpu.SemaphoreType.DMA((bits + 1, CHUNKS)),
    ]


def ring_scratch(count, pieces):
    return [
        pltpu.SemaphoreType.DMA((2, 2, count // 2, pieces)),
        pltpu.SemaphoreType.DMA((2, 2, count // 2, pieces)),
    ]


def call_kernel(body, name, number, inputs, outputs, scratch):
    vmem = pl.BlockSpec(memory_space=pltpu.VMEM)
    return pl.pallas_call(
        body,
        name=name,
        out_shape=outputs,
        in_specs=[vmem] * len(inputs),
        out_specs=[vmem] * len(outputs),
        scratch_shapes=scratch,
        compiler_params=pltpu.CompilerParams(collective_id=number, has_side_effects=True),
    )(*inputs)


def gather_pair(number, first, second):
    count = lax.axis_size("dp")

    def body(a_ref, b_ref, c_ref, d_ref, sends, receives):
        greet(ring_peers(count))
        ring = RingGather(count, (a_ref, b_ref), (c_ref, d_ref), sends, receives)
        ring.start()
        ring.own()
        ring.steps()
        ring.finish()

    outputs = [jax.ShapeDtypeStruct((count,) + x.shape, x.dtype) for x in (first, second)]
    scratch = ring_scratch(count, pieces_of(first.shape[-1]))
    return call_kernel(body, "gather_pair", number, (first, second), outputs, scratch)


def sum_and_gather(number, part, first, second):
    count, wide = lax.axis_size("dp"), lax.axis_size("tensor")

    def body(x_ref, a_ref, b_ref, y_ref, c_ref, d_ref, sends, receives, *cube):
        greet(ring_peers(count) + cube_peers(wide))
        ring = RingGather(count, (a_ref, b_ref), (c_ref, d_ref), sends, receives)
        adder = CubeSum(wide, x_ref, y_ref, *cube)
        adder.start()
        ring.start()
        ring.own()
        adder.add(0)
        ring.steps()
        adder.last()
        adder.finish()
        ring.finish()

    outputs = [jax.ShapeDtypeStruct(part.shape, part.dtype)] + [
        jax.ShapeDtypeStruct((count,) + x.shape, x.dtype) for x in (first, second)
    ]
    scratch = ring_scratch(count, pieces_of(first.shape[-1])) + cube_scratch(wide, *part.shape)
    return call_kernel(body, "sum_and_gather", number, (part, first, second), outputs, scratch)


def sum_and_reduce(number, parts, first, second):
    count, wide, several = lax.axis_size("dp"), lax.axis_size("tensor"), len(parts)

    def body(*refs):
        x_refs, (a_ref, b_ref), refs = refs[:several], refs[several : several + 2], refs[several + 2 :]
        y_refs, (c_ref, d_ref), refs = refs[:several], refs[several : several + 2], refs[several + 2 :]
        slot_a, slot_b, sends, receives = refs[:4]
        greet(ring_peers(count) + cube_peers(wide))
        ring = RingReduce(
            count, (a_ref, b_ref), (slot_a, slot_b), (c_ref, d_ref), sends, receives
        )
        adders = [
            CubeSum(wide, x_refs[k], y_refs[k], *refs[4 + 4 * k : 8 + 4 * k])
            for k in range(several)
        ]
        for adder in adders:
            adder.start()
        ring.start()
        for adder in adders:
            adder.add(0)
        ring.steps()
        for adder in adders:
            adder.last()
        ring.finish()
        for adder in adders:
            adder.finish()

    outputs = [jax.ShapeDtypeStruct(x.shape, x.dtype) for x in parts] + [
        jax.ShapeDtypeStruct(x.shape[1:], jnp.float32) for x in (first, second)
    ]
    scratch = [
        pltpu.VMEM((2, count // 2) + x.shape[1:], jnp.bfloat16) for x in (first, second)
    ] + ring_scratch(count, pieces_of(first.shape[-1]))
    for part in parts:
        scratch += cube_scratch(wide, *part.shape)
    return call_kernel(
        body, "sum_and_reduce", number, (*parts, first, second), outputs, scratch
    )


def sum_small(number, values):
    count = lax.axis_size("dp")

    def body(x_ref, y_ref, slots, sends, receives):
        index = lax.axis_index("dp")
        peers = [lax.rem(index + step, count) for step in range(1, count)]
        greet([{"dp": peer} for peer in peers])

        def copy(step):
            return pltpu.make_async_remote_copy(
                src_ref=x_ref,
                dst_ref=slots.at[index],
                send_sem=sends.at[step],
                recv_sem=receives.at[step],
                device_id={"dp": peers[step]},
                device_id_type=MESH_ID,
            )

        for step in range(count - 1):
            copy(step).start()
        slots[index] = x_ref[...]
        for step in range(count - 1):
            copy(step).wait_recv()
        total = slots[0]
        for place in range(1, count):
            total = total + slots[place]
        y_ref[...] = total
        for step in range(count - 1):
            copy(step).wait_send()

    return call_kernel(
        body,
        "sum_small",
        number,
        (values,),
        [jax.ShapeDtypeStruct(values.shape, values.dtype)],
        [
            pltpu.VMEM((count,) + values.shape, values.dtype),
            pltpu.SemaphoreType.DMA((count - 1,)),
            pltpu.SemaphoreType.DMA((count - 1,)),
        ],
    )[0]


SEGMENT_LIMIT = 512
ROWS = 256


def row_blocks(length):
    rows = ROWS if length % ROWS == 0 else length
    for begin in range(0, length, rows):
        yield begin, rows, max(0, begin - SEGMENT_LIMIT // rows * rows), begin + rows


def allowed_block(seg_column, seg_row, begin, rows, low, high):
    query_at = begin + lax.broadcasted_iota(jnp.int32, (rows, high - low), 0)
    key_at = low + lax.broadcasted_iota(jnp.int32, (rows, high - low), 1)
    same = seg_column[begin : begin + rows, :] == seg_row[:, low:high]
    return same & (key_at <= query_at)


def contract(left, right, left_axis, right_axis):
    return lax.dot_general(
        left, right, (((left_axis,), (right_axis,)), ((), ())), preferred_element_type=jnp.float32
    )


def attention_forward(seg_column, seg_row, query, keys, values):
    length, group = query.shape
    heads = group // HD

    def body(sc_ref, sr_ref, q_ref, k_ref, v_ref, c_ref, l_ref):
        for begin, rows, low, high in row_blocks(length):
            allowed = allowed_block(sc_ref, sr_ref, begin, rows, low, high)
            for head in range(heads):
                span = slice(head * HD, (head + 1) * HD)
                own = slice(begin, begin + rows)
                scores = contract(q_ref[own, span], k_ref[low:high, span], 1, 1)
                scores = jnp.where(allowed, scores, MASK_FILL)
                largest = jnp.max(scores, axis=1, keepdims=True)
                raised = jnp.exp(scores - largest)
                total = jnp.sum(raised, axis=1, keepdims=True)
                probs = (raised * (1.0 / total)).astype(jnp.bfloat16)
                c_ref[own, span] = contract(probs, v_ref[low:high, span], 1, 0).astype(jnp.bfloat16)
                l_ref[own, head : head + 1] = largest + jnp.log(total)

    vmem = pl.BlockSpec(memory_space=pltpu.VMEM)
    return pl.pallas_call(
        body,
        name="attention_forward",
        out_shape=[
            jax.ShapeDtypeStruct((length, group), jnp.bfloat16),
            jax.ShapeDtypeStruct((length, heads), jnp.float32),
        ],
        in_specs=[vmem] * 5,
        out_specs=[vmem] * 2,
    )(seg_column, seg_row, query, keys, values)


def attention_backward(seg_column, seg_row, query, keys, values, context, logs, upstream, scale):
    length, group = query.shape
    heads = group // HD

    def body(sc_ref, sr_ref, q_ref, k_ref, v_ref, c_ref, l_ref, u_ref, g_ref, b_ref, dk_ref, dv_ref):
        dk_ref[...] = jnp.zeros_like(dk_ref)
        dv_ref[...] = jnp.zeros_like(dv_ref)
        bias = [jnp.zeros((1, HD), jnp.float32) for _ in range(heads)]
        for begin, rows, low, high in row_blocks(length):
            allowed = allowed_block(sc_ref, sr_ref, begin, rows, low, high)
            own = slice(begin, begin + rows)
            for head in range(heads):
                span = slice(head * HD, (head + 1) * HD)
                query_block, upstream_block = q_ref[own, span], u_ref[own, span]
                keys_block = k_ref[low:high, span]
                scores = jnp.where(allowed, contract(query_block, keys_block, 1, 1), MASK_FILL)
                probs = jnp.exp(scores - l_ref[own, head : head + 1])
                grad_probs = contract(upstream_block, v_ref[low:high, span], 1, 1)
                delta = jnp.sum(
                    upstream_block.astype(jnp.float32) * c_ref[own, span].astype(jnp.float32),
                    axis=1,
                    keepdims=True,
                )
                grad_scores = (probs * (grad_probs - delta)).astype(jnp.bfloat16)
                grad_query = contract(grad_scores, keys_block, 1, 0) * scale
                g_ref[own, span] = grad_query.astype(jnp.bfloat16)
                bias[head] = bias[head] + jnp.sum(grad_query, axis=0, keepdims=True)
                dk_ref[head, low:high] += contract(grad_scores, query_block, 0, 0)
                dv_ref[head, low:high] += contract(
                    probs.astype(jnp.bfloat16), upstream_block, 0, 0
                )
        for head in range(heads):
            span = slice(head * HD, (head + 1) * HD)
            b_ref[0:1, span] = bias[head]
            b_ref[1:2, span] = jnp.sum(dv_ref[head], axis=0, keepdims=True)
            g_ref[:, group + head * HD : group + (head + 1) * HD] = dk_ref[head].astype(
                jnp.bfloat16
            )
            g_ref[:, 2 * group + head * HD : 2 * group + (head + 1) * HD] = dv_ref[head].astype(
                jnp.bfloat16
            )

    vmem = pl.BlockSpec(memory_space=pltpu.VMEM)
    return pl.pallas_call(
        body,
        name="attention_backward",
        out_shape=[
            jax.ShapeDtypeStruct((length, 3 * group), jnp.bfloat16),
            jax.ShapeDtypeStruct((2, group), jnp.float32),
        ],
        in_specs=[vmem] * 8,
        out_specs=[vmem] * 2,
        scratch_shapes=[pltpu.VMEM((heads, length, HD), jnp.float32)] * 2,
    )(seg_column, seg_row, query, keys, values, context, logs, upstream)


def adam_update(param, grad, first, second, decay):
    first_new = BETA_ONE * first + (1.0 - BETA_ONE) * grad
    second_new = BETA_TWO * second + (1.0 - BETA_TWO) * grad * grad
    first_hat = first_new / (1.0 - BETA_ONE**ADAM_STEP)
    second_hat = second_new / (1.0 - BETA_TWO**ADAM_STEP)
    param_new = param - LEARN_RATE * (first_hat / (jnp.sqrt(second_hat) + ADAM_EPS) + decay * param)
    return (param_new, first_new, second_new)


def on_device(
    tokens,
    cotangent,
    segments,
    w_qkv,
    w_proj,
    w_fc,
    w_fc2,
    w_vectors,
    w_qvbias,
    w_fcbias,
    m_qkv,
    m_proj,
    m_fc,
    m_fc2,
    m_vectors,
    m_qvbias,
    m_fcbias,
    v_qkv,
    v_proj,
    v_fc,
    v_fc2,
    v_vectors,
    v_qvbias,
    v_fcbias,
):
    bfloat = jnp.bfloat16
    count = lax.axis_size("dp")
    depth, _, group = w_qkv.shape
    width = depth * count
    scale = 1.0 / math.sqrt(HD)
    proj_rows = w_proj.shape[0]
    qkv_bf = w_qkv.astype(bfloat)
    first_pair = jnp.concatenate([qkv_bf[:, 0], qkv_bf[:, 1]], axis=1)
    second_pair = jnp.concatenate(
        [qkv_bf[:, 2], w_proj.astype(bfloat).reshape(depth, proj_rows * width // depth)], axis=1
    )
    pair_full = gather_pair(0, first_pair, second_pair)
    first_full, second_full = (x.reshape(width, x.shape[2]) for x in pair_full)
    qkv_flat = jnp.concatenate([first_full, second_full[:, :group]], axis=1)
    proj_full = second_full[:, group:].reshape(proj_rows * count, width)

    inputs_f = tokens[0].astype(jnp.float32)
    seg_row = segments[0]
    first_in, normed_one, inverse_one = layer_norm(inputs_f, w_vectors[0], w_vectors[1])
    first_bf = first_in.astype(bfloat)
    projected = jnp.dot(first_bf, qkv_flat, preferred_element_type=jnp.float32)
    query = ((projected[:, :group] + w_qvbias[0]) * scale).astype(bfloat)
    keys = projected[:, group : 2 * group].astype(bfloat)
    values = (projected[:, 2 * group :] + w_qvbias[1]).astype(bfloat)
    sides = (seg_row[:, None], seg_row[None, :])
    context_flat, log_total = attention_forward(*sides, query, keys, values)
    attn_part = jnp.dot(context_flat, proj_full, preferred_element_type=jnp.float32)
    attn_sum, fc_full, fc2_full = sum_and_gather(
        1, attn_part.astype(bfloat), w_fc.astype(bfloat), w_fc2.astype(bfloat)
    )
    fc_full = fc_full.reshape(width, w_fc.shape[1])
    fc2_full = fc2_full.reshape(w_fc2.shape[0] * count, width)
    middle = (
        inputs_f
        + attn_sum.astype(jnp.float32)
        + w_vectors[4]
    )
    second_in, normed_two, inverse_two = layer_norm(middle, w_vectors[2], w_vectors[3])
    second_bf = second_in.astype(bfloat)
    hidden_pre = jnp.dot(second_bf, fc_full, preferred_element_type=jnp.float32) + w_fcbias
    hidden_bf = gelu_value(hidden_pre).astype(bfloat)
    mlp_part = jnp.dot(hidden_bf, fc2_full, preferred_element_type=jnp.float32)
    upstream = cotangent[0]
    grad_out = upstream.astype(jnp.float32)
    grad_fc2 = jnp.dot(hidden_bf.T, upstream, preferred_element_type=jnp.float32)
    grad_hidden = jnp.dot(upstream, fc2_full.T, preferred_element_type=jnp.float32) * gelu_slope(
        hidden_pre
    )
    grad_hidden_bf = grad_hidden.astype(bfloat)
    grad_fc = jnp.dot(second_bf.T, grad_hidden_bf, preferred_element_type=jnp.float32)
    grad_fcbias = jnp.sum(grad_hidden, axis=0)
    norm_two_part = jnp.dot(grad_hidden_bf, fc_full.T, preferred_element_type=jnp.float32)
    mlp_sum, norm_two_sum, fc2_summed, fc_summed = sum_and_reduce(
        2,
        (mlp_part.astype(bfloat), norm_two_part.astype(bfloat)),
        grad_fc2.astype(bfloat).reshape(count, w_fc2.shape[0], width),
        grad_fc.astype(bfloat).reshape(count, depth, w_fc.shape[1]),
    )
    output = (middle + mlp_sum.astype(jnp.float32) + w_vectors[5]).astype(bfloat)
    back_two, gain_two, shift_two = norm_backward(
        norm_two_sum.astype(jnp.float32),
        normed_two,
        inverse_two,
        w_vectors[2],
    )
    grad_middle = grad_out + back_two
    grad_middle_bf = grad_middle.astype(bfloat)
    grad_proj = jnp.dot(context_flat.T, grad_middle_bf, preferred_element_type=jnp.float32)
    grad_context = jnp.dot(grad_middle_bf, proj_full.T, preferred_element_type=jnp.float32).astype(
        bfloat
    )
    grad_stack, grad_qvbias = attention_backward(
        *sides, query, keys, values, context_flat, log_total, grad_context, scale
    )
    grad_qkv = jnp.dot(first_bf.T, grad_stack, preferred_element_type=jnp.float32).astype(bfloat)
    norm_one_part = jnp.dot(grad_stack, qkv_flat.T, preferred_element_type=jnp.float32)
    grad_first = grad_qkv[:, : 2 * group].reshape(count, depth, 2 * group)
    grad_second = jnp.concatenate(
        [grad_qkv[:, 2 * group :], grad_proj.astype(bfloat).reshape(width, group)], axis=1
    ).reshape(count, depth, 2 * group)
    norm_one_sum, first_summed, second_summed = sum_and_reduce(
        3, (norm_one_part.astype(bfloat),), grad_first, grad_second
    )
    qkv_summed = jnp.concatenate([first_summed, second_summed[:, :group]], axis=1).reshape(
        depth, 3, group
    )
    proj_summed = second_summed[:, group:].reshape(proj_rows, width)
    back_one, gain_one, shift_one = norm_backward(
        norm_one_sum.astype(jnp.float32),
        normed_one,
        inverse_one,
        w_vectors[0],
    )
    grad_input = (grad_middle + back_one).astype(bfloat)
    grad_vectors = jnp.stack(
        [
            gain_one,
            shift_one,
            gain_two,
            shift_two,
            jnp.sum(grad_middle, axis=0),
            jnp.sum(grad_out, axis=0),
        ]
    )
    small = jnp.concatenate(
        [grad_vectors.reshape(-1), grad_qvbias.reshape(-1), grad_fcbias.reshape(-1)]
    )
    small_size = small.shape[0]
    small_rows = -(-small_size // width)
    small_sum = sum_small(
        4, jnp.pad(small, (0, small_rows * width - small_size)).reshape(small_rows, width)
    ).reshape(-1)
    cut_one = grad_vectors.size
    cut_two = cut_one + grad_qvbias.size
    vectors_summed = small_sum[:cut_one].reshape(grad_vectors.shape)
    qvbias_summed = small_sum[cut_one:cut_two].reshape(grad_qvbias.shape)
    fcbias_summed = small_sum[cut_two:small_size]
    params = (w_qkv, w_proj, w_fc, w_fc2, w_vectors, w_qvbias, w_fcbias)
    gradients = (
        qkv_summed,
        proj_summed,
        fc_summed,
        fc2_summed,
        vectors_summed,
        qvbias_summed,
        fcbias_summed,
    )
    firsts = (m_qkv, m_proj, m_fc, m_fc2, m_vectors, m_qvbias, m_fcbias)
    seconds = (v_qkv, v_proj, v_fc, v_fc2, v_vectors, v_qvbias, v_fcbias)
    decays = (DECAY_RATE, DECAY_RATE, DECAY_RATE, DECAY_RATE, 0.0, 0.0, 0.0)
    updates = [
        adam_update(p, g, m, v, c)
        for p, g, m, v, c in zip(params, gradients, firsts, seconds, decays)
    ]
    return (
        output[None],
        grad_input[None],
        gradients[0],
        gradients[1],
        gradients[2],
        gradients[3],
        gradients[4],
        gradients[5],
        gradients[6],
        updates[0][0],
        updates[1][0],
        updates[2][0],
        updates[3][0],
        updates[4][0],
        updates[5][0],
        updates[6][0],
        updates[0][1],
        updates[1][1],
        updates[2][1],
        updates[3][1],
        updates[4][1],
        updates[5][1],
        updates[6][1],
        updates[0][2],
        updates[1][2],
        updates[2][2],
        updates[3][2],
        updates[4][2],
        updates[5][2],
        updates[6][2],
    )


BLOCK = 256


class Wires:
    def __init__(self, sends, receives):
        self.sends, self.receives, self.made = sends, receives, []

    def copy(self, source, target, peer):
        place = len(self.made)
        made = pltpu.make_async_remote_copy(
            src_ref=source,
            dst_ref=target,
            send_sem=self.sends.at[place],
            recv_sem=self.receives.at[place],
            device_id=peer,
            device_id_type=MESH_ID,
        )
        self.made.append(made)
        return made

    def drain(self):
        for made in self.made:
            made.wait_send()


class Grid:
    def __init__(self):
        self.count = lax.axis_size("dp")
        self.lines = self.count // 2
        self.index = lax.axis_index("dp")
        self.line, self.pair = lax.div(self.index, 2), lax.rem(self.index, 2)
        self.across = {"dp": self.line * 2 + 1 - self.pair}
        tensor = lax.axis_index("tensor")
        self.side = lax.rem(tensor, 2)
        self.core, self.far = {"tensor": flip_bit(tensor, 0)}, {"tensor": flip_bit(tensor, 1)}

    def owner(self, step, pair):
        return lax.rem(self.line + step + 2 * self.lines, self.lines) * 2 + pair

    def along(self, step):
        return {"dp": self.owner(step, self.pair)}

    def peers(self):
        return [self.across, self.core, self.far] + [self.along(s) for s in range(1, self.lines)]


class Route:
    def __init__(self, grid, rows):
        self.index, self.count = grid.index, grid.count
        self.depth = rows // grid.count
        self.half = self.depth // 2
        self.place = ring_position(grid.index, grid.count)
        self.peers = ring_peers(grid.count)

    def hops(self, way, array):
        return self.count // 2 if way == array else self.count - 1 - self.count // 2

    def keys(self, step):
        return [(w, a) for a in range(2) for w in range(2) if step < self.hops(w, a)]

    def at(self, distance, way):
        return ring_index(self.place + (1 - 2 * way) * distance + self.count, self.count)

    def span(self, owner):
        return pl.ds(pl.multiple_of(owner * self.depth, 16), self.depth)

    def half_span(self, owner, array):
        begin = owner * self.depth + array * self.half
        return pl.ds(pl.multiple_of(begin, 16), self.half)

    def start(self):
        for key in self.keys(0):
            self.copies[0, *key].start()


class Gather(Route):
    def __init__(self, grid, wires, full):
        super().__init__(grid, full.shape[0])
        self.copies = {}
        for step in range(grid.count // 2):
            for way, array in self.keys(step):
                block = full.at[self.half_span(self.at(-step, way), array)]
                self.copies[step, way, array] = wires.copy(block, block, self.peers[way])

    def step(self, step):
        for key in self.keys(step):
            self.copies[step - 1, *key].wait_recv()
            self.copies[step, *key].start()

    def finish(self):
        for way in range(2):
            for array in range(2):
                self.copies[self.hops(way, array) - 1, way, array].wait_recv()


class Reduce(Route):
    def __init__(self, grid, wires, source, slots):
        super().__init__(grid, source.shape[0])
        self.source, self.slots = source, slots
        self.copies = {}
        for step in range(grid.count // 2):
            for way, array in self.keys(step):
                if step == 0:
                    block = source.at[self.block(0, way, array)]
                else:
                    block = slots.at[array, way, step - 1]
                target = slots.at[array, way, step]
                self.copies[step, way, array] = wires.copy(block, target, self.peers[way])

    def block(self, step, way, array):
        return self.half_span(self.at(self.hops(way, array) - step, way), array)

    def step(self, step):
        for way, array in self.keys(step):
            self.copies[step - 1, way, array].wait_recv()
            own = self.source[self.block(step, way, array), :].astype(jnp.float32)
            arrived = self.slots[array, way, step - 1].astype(jnp.float32)
            self.slots[array, way, step - 1] = (own + arrived).astype(jnp.bfloat16)
            self.copies[step, way, array].start()

    def finish(self):
        halves = []
        for array in range(2):
            total = self.source[self.half_span(self.index, array), :].astype(jnp.float32)
            for way in range(2):
                last = self.hops(way, array) - 1
                self.copies[last, way, array].wait_recv()
                total = total + self.slots[array, way, last].astype(jnp.float32)
            halves.append(total)
        return jnp.concatenate(halves, axis=0)


class Share:
    def __init__(self, grid, wires, part, arrivals, out):
        self.part, self.arrivals, self.out = part, arrivals, out
        self.half, self.side = arrivals.shape[2], grid.side
        blocks = range(arrivals.shape[1])
        self.first = [
            wires.copy(part.at[self.span(b, 1 - grid.side)], arrivals.at[0, b], grid.core)
            for b in blocks
        ]
        self.second = [
            wires.copy(part.at[self.mine(b)], arrivals.at[1, b], grid.far) for b in blocks
        ]
        self.third = [
            wires.copy(out.at[self.mine(b)], out.at[self.mine(b)], grid.core) for b in blocks
        ]

    def span(self, block, side):
        begin = block * 2 * self.half + side * self.half
        return pl.ds(pl.multiple_of(begin, self.half), self.half)

    def mine(self, block):
        return self.span(block, self.side)

    def give(self, block, value):
        rows = 2 * self.half
        self.part[block * rows : (block + 1) * rows, :] = value.astype(jnp.bfloat16)
        self.first[block].start()

    def cross(self, block):
        self.first[block].wait_recv()
        span = self.mine(block)
        own, arrived = self.part[span, :], self.arrivals[0, block]
        self.part[span, :] = (own.astype(jnp.float32) + arrived.astype(jnp.float32)).astype(
            jnp.bfloat16
        )
        self.second[block].start()

    def take(self, block):
        self.second[block].wait_recv()
        own, arrived = self.part[self.mine(block), :], self.arrivals[1, block]
        return own.astype(jnp.float32) + arrived.astype(jnp.float32)

    def put(self, block, value):
        self.out[self.mine(block), :] = value.astype(jnp.bfloat16)
        self.third[block].start()

    def close(self, block):
        self.third[block].wait_recv()


def column_sum(values):
    return jnp.sum(values, axis=0, keepdims=True)


def padded_rows(rows):
    return -(-rows // 32) * 32


def fused_body(scale, shapes, *refs):
    length, width, group, hidden, depth, proj_rows = shapes
    (
        x_hbm, g_hbm, sr_ref, wq_ref, wo_ref, w1_ref, w2_ref, vec_ref, qv_ref, fb_ref,
        out_ref, gt_ref, gq_ref, go_ref, g1_ref, g2_ref, gv_ref, gqv_ref, gfb_ref,
        fq, fo, f1, f2, wo_f, wo, a1, q_s, k_s, v_s, c_s, pr_s, h_s, dh_s, a2, dhb, gw, u_s, dz_s,
        dk_s, dv_s, dp_s, part_a, part_n, part_m, part_i, arr_a, arr_n, arr_m, arr_i,
        sq, so, s1, s2, nq, no, n1, n2, sm_own, sm_core, sm_two, sm_pair, sm_four,
        sm_line, sc_ref, x_ref, g_ref, sends, receives, loads,
    ) = refs
    f32, b16 = jnp.float32, jnp.bfloat16
    grid, wires = Grid(), Wires(sends, receives)
    heads, rows = group // HD, BLOCK
    pad = padded_rows(proj_rows)
    blocks = length // rows
    order = list(range(blocks))[::-1]

    gathers = {n: Gather(grid, wires, f) for n, f in (("q", fq), ("o", fo), ("2", f2), ("1", f1))}
    share_a = Share(grid, wires, part_a, arr_a, a2)
    share_n = Share(grid, wires, part_n, arr_n, dhb)
    share_m = Share(grid, wires, part_m, arr_m, out_ref)
    share_i = Share(grid, wires, part_i, arr_i, gt_ref)
    reduce_2, reduce_1 = Reduce(grid, wires, s2, n2), Reduce(grid, wires, s1, n1)
    reduce_q, reduce_o = Reduce(grid, wires, sq, nq), Reduce(grid, wires, so, no)
    small_core = wires.copy(sm_own, sm_core, grid.core)
    small_pair = wires.copy(sm_two, sm_pair, grid.across)
    small_line = [
        wires.copy(sm_four, sm_line.at[s - 1], grid.along(s)) for s in range(1, grid.lines)
    ]

    def block_rows(b):
        return slice(b * rows, (b + 1) * rows)

    load_x = pltpu.make_async_copy(x_hbm, x_ref, loads.at[0])
    load_g = pltpu.make_async_copy(g_hbm, g_ref, loads.at[1])
    barrier = pltpu.get_barrier_semaphore()
    peers = grid.peers()
    for peer in peers:
        pl.semaphore_signal(barrier, inc=1, device_id=peer, device_id_type=MESH_ID)
    load_x.start()
    load_g.start()
    own_rows = gathers["q"].span(grid.index)
    for j in range(3):
        fq[own_rows, j * group : (j + 1) * group] = wq_ref[j].astype(b16)
    own_proj = wo_ref[...]
    if pad > proj_rows:
        own_proj = jnp.concatenate([own_proj, jnp.zeros((pad - proj_rows, width), f32)], axis=0)
    fo[gathers["o"].span(grid.index), :] = own_proj.astype(b16)
    pl.semaphore_wait(barrier, len(peers))
    gathers["q"].start()
    gathers["o"].start()
    f2[gathers["2"].span(grid.index), :] = w2_ref[...].astype(b16)
    f1[gathers["1"].span(grid.index), :] = w1_ref[...].astype(b16)

    load_x.wait()
    for b in order:
        first_in, _, _ = layer_norm(x_ref[block_rows(b), :].astype(f32), vec_ref[0:1], vec_ref[1:2])
        a1[block_rows(b), :] = first_in.astype(b16)
    dk_s[...] = jnp.zeros_like(dk_s)
    dv_s[...] = jnp.zeros_like(dv_s)
    for b in order:
        wide_row = jnp.broadcast_to(sr_ref[:, block_rows(b)], (8, rows)).astype(f32)
        sc_ref[block_rows(b), :] = jnp.transpose(wide_row)[:, :1].astype(jnp.int32)
    load_g.wait()
    sum_g = jnp.zeros((1, width), f32)
    for b in order:
        sum_g = sum_g + column_sum(g_ref[share_a.mine(b), :].astype(f32))
    sm_own[5:6, :] = sum_g

    for step in range(1, grid.count // 2):
        gathers["q"].step(step)
        gathers["o"].step(step)
    gathers["2"].start()
    gathers["1"].start()
    pending = [(name, step) for step in range(1, grid.count // 2) for name in ("2", "1")]

    def poll(times=1):
        for name, step in pending[:times]:
            gathers[name].step(step)
        del pending[:times]

    gathers["q"].finish()
    for b in order:
        projected = jnp.dot(a1[block_rows(b), :], fq[...], preferred_element_type=f32)
        q_s[block_rows(b), :] = ((projected[:, :group] + qv_ref[0:1]) * scale).astype(b16)
        k_s[block_rows(b), :] = projected[:, group : 2 * group].astype(b16)
        v_s[block_rows(b), :] = (projected[:, 2 * group :] + qv_ref[1:2]).astype(b16)
    gathers["o"].finish()
    for i in range(grid.count):
        block = fo[i * pad : (i + 1) * pad, :].astype(f32)
        wo_f[i * proj_rows : (i + 1) * proj_rows, :] = block[:proj_rows]
    wo[...] = wo_f[...].astype(b16)

    def window(b):
        return max(0, b * rows - -(-SEGMENT_LIMIT // rows) * rows), (b + 1) * rows

    def attend(b):
        low, high = window(b)
        allowed = allowed_block(sc_ref, sr_ref, b * rows, rows, low, high)
        bias = jnp.where(allowed, 0.0, MASK_FILL)
        for head in range(heads):
            span = slice(head * HD, (head + 1) * HD)
            scores = contract(q_s[block_rows(b), span], k_s[low:high, span], 1, 1) + bias
            largest = jnp.max(scores, axis=1, keepdims=True)
            raised = jnp.exp(scores - largest)
            total = jnp.sum(raised, axis=1, keepdims=True)
            probs = (raised * (1.0 / total)).astype(b16)
            pr_s[b, head, :, : high - low] = probs
            c_s[block_rows(b), span] = contract(probs, v_s[low:high, span], 1, 0).astype(b16)

    order_a = order[-1:] + order[:-1]
    for i, b in enumerate(order_a):
        attend(b)
        share_a.give(b, jnp.dot(c_s[block_rows(b), :], wo[...], preferred_element_type=f32))
        if i >= 1:
            share_a.cross(order_a[i - 1])
        poll()
    share_a.cross(order_a[-1])

    def take_a(b):
        middle = x_ref[share_a.mine(b), :].astype(f32) + share_a.take(b) + vec_ref[4:5]
        h_s[b] = middle
        second_in, _, _ = layer_norm(middle, vec_ref[2:3], vec_ref[3:4])
        share_a.put(b, second_in)

    late = order_a[-1:] if blocks > 2 else []
    for b in order_a[: blocks - len(late)]:
        take_a(b)
        poll()
    poll(len(pending))
    gathers["2"].finish()
    for b in order[:blocks]:
        gw[block_rows(b), :] = contract(g_ref[block_rows(b), :], f2[...], 1, 1)
    gathers["1"].finish()

    tile = 256 if hidden % 256 == 0 else hidden
    sum_fb = [jnp.zeros((1, tile), f32) for _ in range(hidden // tile)]
    sums = {"gain2": jnp.zeros((1, width), f32), "shift2": jnp.zeros((1, width), f32)}
    sums["mid"] = jnp.zeros((1, width), f32)

    def take_n(b):
        upstream = share_n.take(b)
        _, normed, inverse = layer_norm(h_s[b], vec_ref[2:3], vec_ref[3:4])
        back, _, _ = norm_backward(upstream, normed, inverse, vec_ref[2:3])
        sums["gain2"] = sums["gain2"] + column_sum(upstream * normed)
        sums["shift2"] = sums["shift2"] + column_sum(upstream)
        grad_middle = g_ref[share_n.mine(b), :].astype(f32) + back
        sums["mid"] = sums["mid"] + column_sum(grad_middle)
        dh_s[b] = grad_middle
        share_n.put(b, grad_middle)

    for i, b in enumerate(order):
        share_a.close(b)
        for c in range(hidden // tile):
            span = slice(c * tile, (c + 1) * tile)
            z = jnp.dot(a2[block_rows(b), :], f1[:, span], preferred_element_type=f32)
            z = z + fb_ref[span].reshape(1, tile)
            square = z * z
            tangent = jnp.tanh(GELU_COEF * z * (1.0 + CUBIC_COEF * square))
            half = 0.5 * (1.0 + tangent)
            u_s[block_rows(b), span] = (z * half).astype(b16)
            slope = half + 0.5 * z * (1.0 - tangent * tangent) * GELU_COEF * (
                1.0 + 3.0 * CUBIC_COEF * square
            )
            dz = gw[block_rows(b), span] * slope
            sum_fb[c] = sum_fb[c] + column_sum(dz)
            dz_s[block_rows(b), span] = dz.astype(b16)
        share_n.give(b, contract(dz_s[block_rows(b), :], f1[...], 1, 1))
        share_m.give(b, jnp.dot(u_s[block_rows(b), :], f2[...], preferred_element_type=f32))
        share_n.cross(b)
        if i == 0:
            for other in late:
                take_a(other)
    for c in range(hidden // tile):
        sm_own[6:7, c * tile : (c + 1) * tile] = sum_fb[c]

    def outer(target, left, right):
        for begin in range(0, target.shape[0], BLOCK):
            target[begin : begin + BLOCK, :] = contract(
                left[:, begin : begin + BLOCK], right[...], 0, 0
            ).astype(b16)

    outer(s2, u_s, g_ref)
    reduce_2.start()
    outer(s1, a2, dz_s)
    reduce_1.start()
    later = [(r, step) for step in range(1, grid.count // 2) for r in (reduce_2, reduce_1)]

    def advance(times=1):
        for reduce, step in later[:times]:
            reduce.step(step)
        del later[:times]

    take_n(order[0])
    share_m.cross(order[0])

    bias_q = [jnp.zeros((1, HD), f32) for _ in range(heads)]
    bias_v = [jnp.zeros((1, HD), f32) for _ in range(heads)]

    def attend_back(b):
        low, high = window(b)
        grad_context = contract(dhb[block_rows(b), :], wo[...], 1, 1).astype(b16)
        for head in range(heads):
            span = slice(head * HD, (head + 1) * HD)
            upstream = grad_context[:, span]
            probs = pr_s[b, head, :, : high - low]
            keys_block = k_s[low:high, span]
            grad_probs = contract(upstream, v_s[low:high, span], 1, 1)
            delta = jnp.sum(
                upstream.astype(f32) * c_s[block_rows(b), span].astype(f32), axis=1, keepdims=True
            )
            grad_scores = (probs.astype(f32) * (grad_probs - delta)).astype(b16)
            grad_query = contract(grad_scores, keys_block, 1, 0) * scale
            dp_s[block_rows(b), span] = grad_query.astype(b16)
            bias_q[head] = bias_q[head] + column_sum(grad_query)
            dk_s[head, low:high] += contract(grad_scores, q_s[block_rows(b), span], 0, 0)
            dv_s[head, low:high] += contract(probs, upstream, 0, 0)
        for head in range(heads):
            begin = group + head * HD
            dp_s[block_rows(b), begin : begin + HD] = dk_s[head, block_rows(b)].astype(b16)
            grad_value = dv_s[head, block_rows(b)]
            bias_v[head] = bias_v[head] + column_sum(grad_value)
            dp_s[block_rows(b), begin + group : begin + group + HD] = grad_value.astype(b16)

    for i, b in enumerate(order):
        if i + 1 < blocks:
            take_n(order[i + 1])
        share_n.close(b)
        attend_back(b)
        share_i.give(b, contract(dp_s[block_rows(b), :], fq[...], 1, 1))
        if i >= 1:
            share_i.cross(order[i - 1])
        advance()
    for name, row in (("gain2", 2), ("shift2", 3), ("mid", 4)):
        sm_own[row : row + 1, :] = sums[name]
    sm_own[7:8, :] = jnp.zeros((1, width), f32)
    for head in range(heads):
        sm_own[7:8, head * HD : (head + 1) * HD] = bias_q[head]
        sm_own[7:8, group + head * HD : group + (head + 1) * HD] = bias_v[head]

    outer(sq, a1, dp_s)
    reduce_q.start()
    share_i.cross(order[-1])
    for b in order[1:]:
        share_m.cross(b)
    grad_proj = contract(c_s[...], dhb[...], 0, 0)
    for i in range(grid.count):
        block = grad_proj[i * proj_rows : (i + 1) * proj_rows]
        if pad > proj_rows:
            block = jnp.concatenate([block, jnp.zeros((pad - proj_rows, width), f32)], axis=0)
        so[i * pad : (i + 1) * pad, :] = block.astype(b16)
    reduce_o.start()
    later += [(r, step) for step in range(1, grid.count // 2) for r in (reduce_q, reduce_o)]

    gain, shift = jnp.zeros((1, width), f32), jnp.zeros((1, width), f32)
    for i, b in enumerate(order):
        upstream = share_i.take(b)
        _, normed, inverse = layer_norm(
            x_ref[share_i.mine(b), :].astype(f32), vec_ref[0:1], vec_ref[1:2]
        )
        back, _, _ = norm_backward(upstream, normed, inverse, vec_ref[0:1])
        gain = gain + column_sum(upstream * normed)
        shift = shift + column_sum(upstream)
        share_i.put(b, dh_s[b] + back)
        advance(2)
    sm_own[0:1, :] = gain
    sm_own[1:2, :] = shift
    small_core.start()

    def take_m(b):
        share_m.put(b, h_s[b] + share_m.take(b) + vec_ref[5:6])

    for b in order[: blocks // 2]:
        take_m(b)
    advance(len(later))
    g2_ref[...] = reduce_2.finish()
    small_core.wait_recv()
    sm_two[0:6, :] = sm_own[0:6, :] + sm_core[0:6, :]
    sm_two[6:8, :] = sm_own[6:8, :]
    small_pair.start()
    g1_ref[...] = reduce_1.finish()
    small_pair.wait_recv()
    sm_four[...] = sm_two[...] + sm_pair[...]
    for made in small_line:
        made.start()
    total_q = reduce_q.finish()
    for j in range(3):
        gq_ref[j] = total_q[:, j * group : (j + 1) * group]
    go_ref[...] = reduce_o.finish()[:proj_rows]
    total = sm_four[...]
    for step, made in enumerate(small_line):
        made.wait_recv()
        total = total + sm_line[step]
    gv_ref[...] = total[0:6]
    gfb_ref[...] = total[6:7].reshape(width)
    gqv_ref[0:1, :] = total[7:8, :group]
    gqv_ref[1:2, :] = total[7:8, group : 2 * group]
    for b in order[blocks // 2 :]:
        take_m(b)
    for b in order:
        share_m.close(b)
        share_i.close(b)
    wires.drain()


def fused_call(x, g, seg, wq, wo, w1, w2, vec, qv, fb):
    f32, b16 = jnp.float32, jnp.bfloat16
    length, width = x.shape
    _, depth, group = wq.shape
    hidden, proj_rows = w1.shape[1], wo.shape[0]
    count, lines, blocks = lax.axis_size("dp"), lax.axis_size("dp") // 2, length // BLOCK
    heads, pad, half = group // HD, padded_rows(proj_rows), BLOCK // 2
    reach = min(length, -(-SEGMENT_LIMIT // BLOCK) * BLOCK + BLOCK)

    def full(*shape):
        return pltpu.VMEM(shape, b16)

    def wide(*shape):
        return pltpu.VMEM(shape, f32)

    scratch = [
        full(width, 3 * group), full(count * pad, width), full(width, hidden), full(hidden, width),
        wide(group, width), full(group, width), full(length, width),
        full(length, group), full(length, group), full(length, group), full(length, group),
        full(blocks, heads, BLOCK, reach),
        wide(blocks, half, width), wide(blocks, half, width),
        full(length, width), full(length, width), wide(length, hidden),
        full(length, hidden), full(length, hidden),
        wide(heads, length, HD), wide(heads, length, HD), full(length, 3 * group),
    ]
    scratch += [full(length, width)] * 4 + [full(2, blocks, half, width)] * 4
    shards = [(depth, 3 * group), (pad, width), (depth, hidden), (w2.shape[0], width)]
    scratch += [full(count * a, b) for a, b in shards]
    scratch += [full(2, 2, count // 2, a // 2, b) for a, b in shards]
    scratch += [wide(8, width)] * 5 + [wide(lines - 1, 8, width)]
    copies = 16 * (count - 1) + 12 * blocks + 2 + lines - 1
    scratch += [pltpu.VMEM((length, 1), jnp.int32)]
    scratch += [full(length, width)] * 2
    scratch += [pltpu.SemaphoreType.DMA((copies,))] * 2 + [pltpu.SemaphoreType.DMA((2,))]
    outputs = [
        jax.ShapeDtypeStruct(s, t)
        for s, t in (
            (x.shape, b16), (x.shape, b16), (wq.shape, f32), (wo.shape, f32), (w1.shape, f32),
            (w2.shape, f32), (vec.shape, f32), (qv.shape, f32), (fb.shape, f32),
        )
    ]
    vmem = pl.BlockSpec(memory_space=pltpu.VMEM)
    inputs = (x, g, seg, wq, wo, w1, w2, vec, qv, fb)
    shapes = (length, width, group, hidden, depth, proj_rows)
    return pl.pallas_call(
        functools.partial(fused_body, 1.0 / math.sqrt(HD), shapes),
        name="fused_block",
        out_shape=outputs,
        in_specs=[pl.BlockSpec(memory_space=pl.ANY)] * 2 + [vmem] * (len(inputs) - 2),
        out_specs=[vmem] * len(outputs),
        scratch_shapes=scratch,
        compiler_params=pltpu.CompilerParams(
            collective_id=5, has_side_effects=True, vmem_limit_bytes=VMEM_BYTES
        ),
    )(*inputs)


VMEM_BYTES = 63 * 1024 * 1024


def adam_body(number, *refs):
    keep = number // 4
    (x_ref, g_ref), sources, refs = refs[:2], refs[2 : 2 + number], refs[2 + number :]
    (y_ref, h_ref), results = refs[:2], refs[2:]
    y_ref[...] = x_ref[...]
    h_ref[...] = g_ref[...]
    pieces = [sources[k * keep : (k + 1) * keep] for k in range(4)]
    for k in range(keep):
        param, grad, first, second = (piece[k][...] for piece in pieces)
        decay = DECAY_RATE if k < 4 else 0.0
        new, first_new, second_new = adam_update(param, grad, first, second, decay)
        results[k][...] = grad
        results[keep + k][...] = new
        results[2 * keep + k][...] = first_new
        results[3 * keep + k][...] = second_new


def adam_call(carried, params, gradients, firsts, seconds):
    inputs = (*carried, *params, *gradients, *firsts, *seconds)
    vmem = pl.BlockSpec(memory_space=pltpu.VMEM)
    outputs = [jax.ShapeDtypeStruct(p.shape, p.dtype) for p in (*carried, *params * 4)]
    return pl.pallas_call(
        functools.partial(adam_body, len(inputs) - 2),
        name="adam_step",
        out_shape=outputs,
        in_specs=[vmem] * len(inputs),
        out_specs=[vmem] * len(outputs),
        compiler_params=pltpu.CompilerParams(vmem_limit_bytes=VMEM_BYTES),
    )(*inputs)


def turn(array):
    return jnp.transpose(array, (1, 0, 2))


def on_device_fused(tokens, cotangent, segments, *state):
    params, firsts, seconds = state[:7], state[7:14], state[14:]

    def shaped(group):
        return (turn(group[0]), *group[1:])

    params, firsts, seconds = shaped(params), shaped(firsts), shaped(seconds)
    results = fused_call(tokens[0], cotangent[0], segments, *params)
    updated = adam_call(results[:2], params, results[2:], firsts, seconds)
    restored = [
        (turn(updated[k]), *updated[k + 1 : k + 7])
        for k in range(2, 30, 7)
    ]
    return (updated[0][None], updated[1][None]) + sum(restored, ())


def fused_fits(mesh, args):
    tokens, w_qkv, w_proj, w_fc, w_fc2 = args[0], args[3], args[4], args[5], args[6]
    count, wide = mesh.shape["dp"], mesh.shape["tensor"]
    width, length = tokens.shape[2], tokens.shape[1]
    depth, group, hidden = width // count, w_qkv.shape[2] // wide, w_fc.shape[1] // wide
    proj_rows = w_proj.shape[0] // (wide * count)
    return (
        wide == 4
        and count % 2 == 0
        and count >= 4
        and depth % 32 == 0
        and (w_fc2.shape[0] // (wide * count)) % 32 == 0
        and proj_rows % 8 == 0
        and length % BLOCK == 0
        and width % BLOCK == 0
        and hidden % BLOCK == 0
        and hidden == width
        and 2 * group <= width
    )


def mapped(mesh, body):
    return jax.shard_map(
        body,
        mesh=mesh,
        in_specs=(
            P("dp", None, None),
            P("dp", None, None),
            P("dp", None),
            P("dp", None, "tensor"),
            P(("tensor", "dp"), None),
            P("dp", "tensor"),
            P(("tensor", "dp"), None),
            P(),
            P(None, "tensor"),
            P("tensor"),
            P("dp", None, "tensor"),
            P(("tensor", "dp"), None),
            P("dp", "tensor"),
            P(("tensor", "dp"), None),
            P(),
            P(None, "tensor"),
            P("tensor"),
            P("dp", None, "tensor"),
            P(("tensor", "dp"), None),
            P("dp", "tensor"),
            P(("tensor", "dp"), None),
            P(),
            P(None, "tensor"),
            P("tensor"),
        ),
        out_specs=(
            P("dp", None, None),
            P("dp", None, None),
            P("dp", None, "tensor"),
            P(("tensor", "dp"), None),
            P("dp", "tensor"),
            P(("tensor", "dp"), None),
            P(),
            P(None, "tensor"),
            P("tensor"),
            P("dp", None, "tensor"),
            P(("tensor", "dp"), None),
            P("dp", "tensor"),
            P(("tensor", "dp"), None),
            P(),
            P(None, "tensor"),
            P("tensor"),
            P("dp", None, "tensor"),
            P(("tensor", "dp"), None),
            P("dp", "tensor"),
            P(("tensor", "dp"), None),
            P(),
            P(None, "tensor"),
            P("tensor"),
            P("dp", None, "tensor"),
            P(("tensor", "dp"), None),
            P("dp", "tensor"),
            P(("tensor", "dp"), None),
            P(),
            P(None, "tensor"),
            P("tensor"),
        ),
        check_vma=False,
    )


def solution(mesh):
    def run(*args):
        body = on_device_fused if fused_fits(mesh, args) else on_device
        return mapped(mesh, body)(*args)

    return run
```
